128 devices in a mesh: lon: 16 (over x, y_lo, core), lat: 8 (over z, y_hi).
Axes of the slice: x: 4, y: 4 (y_hi: 2, y_lo: 2; y = y_hi * 2 + y_lo), z: 4, core: 2. Of those that a mesh axis runs over, the one named last changes fastest.
Arguments:
- heat_content_field: float32 [12, 768, 2048], P(None, 'lat', 'lon'), may hold values from -6 to 6
- saltiness_field: float32 [12, 768, 2048], P(None, 'lat', 'lon'), may hold values from -6 to 6
- eastward_cfl_number: float32 [12, 768, 2048], P(None, 'lat', 'lon'), may hold values from -0.4 to 0.4
- northward_cfl_number: float32 [12, 768, 2048], P(None, 'lat', 'lon'), may hold values from -0.4 to 0.4
- seawater_indicator: int32 [768, 2048], P('lat', 'lon'), may hold values 0 or 1
- submerged_layer_total: int32 [768, 2048], P('lat', 'lon'), may hold values from 1 to 12
- seam_partner_index: int32 [2048], replicated, may hold values from 0 to 2047, as said below
Outputs:
- new_temperature: float32 [12, 768, 2048], P(None, 'lat', 'lon')
- new_salinity: float32 [12, 768, 2048], P(None, 'lat', 'lon')
The draws below stay inside these ranges and needn't reach their ends.
Inputs may be any that keep to these rules, and one draw needn't show every extreme that they name: Each column appears once; the map is a reflection of the columns about a pivot, seam_partner_index[i] = (s - i) mod 2048.
All inputs are finite; a program needn't handle non-finite values. No bound on the sum of `seawater_indicator` on one device may be relied on, other than what follows from the above.
Results may differ from the reference program's by a relative error of at most 0.0003.
Values sent between devices are 32-bit elements; how exact they have to be, the bound alone decides.
A program may use at most 192 MiB of HBM per device.

```python
from functools import reduce
import jax
import jax.numpy as jnp

VERTICAL_LAYERS = 12
MERIDIAN_LINES = 2048
PARALLEL_ROWS = 768


def draw_seam_partner_index(key, part):
    pivot = jax.random.randint(key, (), 0, MERIDIAN_LINES, dtype=jnp.int32)
    return ((pivot - jnp.arange(MERIDIAN_LINES, dtype=jnp.int32)) % MERIDIAN_LINES).astype(jnp.int32)


def plant(result, own_key, smallest, high):
    shape = result.shape
    place = [jax.random.randint(jax.random.fold_in(own_key, axis), (), 0, shape[axis]) for axis in range(len(shape))]
    result = result.at[tuple(place)].set(smallest)
    longest = shape.index(max(shape))
    place[longest] = (place[longest] + 1) % shape[longest]
    return result.at[tuple(place)].set(high)


def shard_levels(stream_key, extent, shards, least, high):
    loudness = 1.0
    for position, blocks in shards:
        heights = jax.random.uniform(jax.random.fold_in(jax.random.fold_in(stream_key, 6), position), (blocks,), jnp.float32, least / len(shards), high / len(shards))
        loudness = loudness * jnp.repeat(jnp.exp(heights), extent[position] // blocks).reshape((-1,) + (1,) * (len(extent) - 1 - position))
    return loudness


def bell_draw(rng, dims, deviation, most, split=(), kind=jnp.bfloat16):
    values = jax.random.normal(rng, dims, jnp.float32) * deviation
    if len(split) > 0:
        values = shard_levels(rng, dims, split, -0.22, 0.18) * values
    return jnp.clip(values, min=-most, max=most).astype(kind)


def setup_inputs(seed: int = 0) -> dict:
    splits = jax.random.split(jax.random.key(seed), 8)
    heat_content_field = bell_draw(splits[0], (VERTICAL_LAYERS, PARALLEL_ROWS, MERIDIAN_LINES), 1.0, 6.0, ((1, 8), (2, 16)), jnp.float32)
    saltiness_field = bell_draw(splits[1], (VERTICAL_LAYERS, PARALLEL_ROWS, MERIDIAN_LINES), 1.0, 6.0, ((1, 8), (2, 16)), jnp.float32)
    eastward_cfl_number = jnp.clip(jax.random.uniform(splits[2], (VERTICAL_LAYERS, PARALLEL_ROWS, MERIDIAN_LINES), jnp.float32, -0.4, 0.4) * shard_levels(splits[2], (VERTICAL_LAYERS, PARALLEL_ROWS, MERIDIAN_LINES), ((1, 8), (2, 16)), -0.4, 0.0), -0.4, 0.4)
    northward_cfl_number = jnp.clip(jax.random.uniform(splits[3], (VERTICAL_LAYERS, PARALLEL_ROWS, MERIDIAN_LINES), jnp.float32, -0.4, 0.4) * shard_levels(splits[3], (VERTICAL_LAYERS, PARALLEL_ROWS, MERIDIAN_LINES), ((1, 8), (2, 16)), -0.4, 0.0), -0.4, 0.4)
    seawater_indicator = plant((jax.random.randint(splits[4], (PARALLEL_ROWS, MERIDIAN_LINES), 0, 5) < 4).astype(jnp.int32), jax.random.fold_in(splits[4], 1), 0, 1)
    submerged_layer_total = plant(jax.random.randint(splits[5], (PARALLEL_ROWS, MERIDIAN_LINES), 1, VERTICAL_LAYERS + 1), jax.random.fold_in(splits[5], 1), 1, VERTICAL_LAYERS).astype(jnp.int32)
    seam_partner_index = draw_seam_partner_index(jax.random.fold_in(splits[7], 71), 0)
    return dict(heat_content_field=heat_content_field, saltiness_field=saltiness_field, eastward_cfl_number=eastward_cfl_number, northward_cfl_number=northward_cfl_number, seawater_indicator=seawater_indicator, submerged_layer_total=submerged_layer_total, seam_partner_index=seam_partner_index)


RATIO_FLOOR = 0.05
SLOPE_FLOOR = 0.5
SLOPE_LIMIT = 2.0
DIFFUSIVITY = 0.1
THERMAL_COEF = 0.2
HALINE_COEF = 0.8
STATE_SIGNS = (1.0, 1.0, -1.0, -1.0, 1.0)


def sign_column(values):
    return jnp.array(values, jnp.float32).reshape(len(values), 1, 1, 1)


def neighbours(field):
    at_centre = field[..., 1:-1, 1:-1]
    at_east = field[..., 1:-1, 2:]
    at_west = field[..., 1:-1, :-2]
    at_north = field[..., 2:, 1:-1]
    at_south = field[..., :-2, 1:-1]
    return at_centre, at_east, at_west, at_north, at_south


def low_order(tracer, zonal, meridional, wet_pad):
    value_centre, value_east, value_west, value_north, value_south = neighbours(tracer)
    speed_centre, _, speed_west, _, _ = neighbours(zonal)
    flow_centre, _, _, _, flow_south = neighbours(meridional)
    wet_centre, wet_east, wet_west, wet_north, wet_south = neighbours(wet_pad)
    face_east = wet_centre * wet_east
    face_west = wet_west * wet_centre
    face_north = wet_centre * wet_north
    face_south = wet_south * wet_centre
    upwind_east = face_east * (jnp.maximum(speed_centre, 0.0) * value_centre + jnp.minimum(speed_centre, 0.0) * value_east)
    upwind_west = face_west * (jnp.maximum(speed_west, 0.0) * value_west + jnp.minimum(speed_west, 0.0) * value_centre)
    upwind_north = face_north * (jnp.maximum(flow_centre, 0.0) * value_centre + jnp.minimum(flow_centre, 0.0) * value_north)
    upwind_south = face_south * (jnp.maximum(flow_south, 0.0) * value_south + jnp.minimum(flow_south, 0.0) * value_centre)
    anti_east = face_east * speed_centre * (value_centre + value_east) * 0.5 - upwind_east
    anti_west = face_west * speed_west * (value_west + value_centre) * 0.5 - upwind_west
    anti_north = face_north * flow_centre * (value_centre + value_north) * 0.5 - upwind_north
    anti_south = face_south * flow_south * (value_south + value_centre) * 0.5 - upwind_south
    upwind = value_centre - wet_centre * (upwind_east - upwind_west + upwind_north - upwind_south)
    inflow = jnp.maximum(anti_west, 0.0) - jnp.minimum(anti_east, 0.0) + jnp.maximum(anti_south, 0.0) - jnp.minimum(anti_north, 0.0)
    outflow = jnp.maximum(anti_east, 0.0) - jnp.minimum(anti_west, 0.0) + jnp.maximum(anti_north, 0.0) - jnp.minimum(anti_south, 0.0)
    anti = jnp.stack([anti_east, anti_west, anti_north, anti_south])
    return upwind, anti, inflow, outflow


def ratios(upwind_pad, wet_pad, inflow, outflow):
    value_centre, value_east, value_west, value_north, value_south = neighbours(upwind_pad)
    _, wet_east, wet_west, wet_north, wet_south = neighbours(wet_pad)
    pairs = ((value_east, wet_east), (value_west, wet_west), (value_north, wet_north), (value_south, wet_south))
    candidates = [value_centre] + [jnp.where(beside_wet > 0.5, beside, value_centre) for beside, beside_wet in pairs]
    highest = reduce(jnp.maximum, candidates)
    lowest = reduce(jnp.minimum, candidates)
    ratio_plus = jnp.minimum(1.0, (highest - value_centre) / jnp.maximum(inflow, RATIO_FLOOR))
    ratio_minus = jnp.minimum(1.0, (value_centre - lowest) / jnp.maximum(outflow, RATIO_FLOOR))
    return jnp.concatenate([ratio_plus, ratio_minus], axis=0)


def limited(ratio_pad, upwind, anti, submerged_indicator):
    plus_centre, plus_east, plus_west, plus_north, plus_south = neighbours(ratio_pad[:2])
    minus_centre, minus_east, minus_west, minus_north, minus_south = neighbours(ratio_pad[2:])
    anti_east, anti_west, anti_north, anti_south = anti[0], anti[1], anti[2], anti[3]
    coef_east = jnp.where(anti_east >= 0.0, jnp.minimum(plus_east, minus_centre), jnp.minimum(plus_centre, minus_east))
    coef_west = jnp.where(anti_west >= 0.0, jnp.minimum(plus_centre, minus_west), jnp.minimum(plus_west, minus_centre))
    coef_north = jnp.where(anti_north >= 0.0, jnp.minimum(plus_north, minus_centre), jnp.minimum(plus_centre, minus_north))
    coef_south = jnp.where(anti_south >= 0.0, jnp.minimum(plus_centre, minus_south), jnp.minimum(plus_south, minus_centre))
    return upwind - submerged_indicator * (coef_east * anti_east - coef_west * anti_west + coef_north * anti_north - coef_south * anti_south)


def isopycnal(tracer_pad, wet_pad):
    stacked_wet = wet_pad[:-1] * wet_pad[1:]
    vertical = (tracer_pad[:, 1:] - tracer_pad[:, :-1]) * stacked_wet
    vertical = jnp.concatenate([vertical, jnp.zeros_like(tracer_pad[:, :1])], axis=1)
    density = HALINE_COEF * tracer_pad[1] - THERMAL_COEF * tracer_pad[0]
    stratification = HALINE_COEF * vertical[1] - THERMAL_COEF * vertical[0]
    values = neighbours(tracer_pad)
    verticals = neighbours(vertical)
    densities = neighbours(density)
    stratas = neighbours(stratification)
    wet_sides = neighbours(wet_pad)

    def face_flux(first, second):
        face = wet_sides[first] * wet_sides[second]
        slope = jnp.clip((densities[second] - densities[first]) / jnp.maximum(0.5 * (stratas[first] + stratas[second]), SLOPE_FLOOR), -SLOPE_LIMIT, SLOPE_LIMIT)
        return DIFFUSIVITY * face * ((values[second] - values[first]) - slope * 0.5 * (verticals[first] + verticals[second]))

    east_flux = face_flux(0, 1)
    west_flux = face_flux(2, 0)
    north_flux = face_flux(0, 3)
    south_flux = face_flux(4, 0)
    return values[0] + wet_sides[0] * (east_flux - west_flux + north_flux - south_flux)


def extend(field, signs, seam_partner_index):
    ghost = jnp.take(field[:, :, -1:, :], seam_partner_index, axis=3) * signs
    bottom = jnp.zeros_like(ghost)
    tall = jnp.concatenate([bottom, field, ghost], axis=2)
    return jnp.concatenate([tall[..., -1:], tall, tall[..., :1]], axis=3)


def reference(heat_content_field, saltiness_field, eastward_cfl_number, northward_cfl_number, seawater_indicator, submerged_layer_total, seam_partner_index):
    vertical_layer = jnp.arange(VERTICAL_LAYERS, dtype=jnp.int32)[:, None, None]
    submerged_indicator = ((seawater_indicator[None] == 1) & (vertical_layer < submerged_layer_total[None])).astype(jnp.float32)
    scalar_fields_pair = jnp.stack([heat_content_field, saltiness_field, eastward_cfl_number, northward_cfl_number, submerged_indicator])
    padded = extend(scalar_fields_pair, sign_column(STATE_SIGNS), seam_partner_index)
    upwind, anti, inflow, outflow = low_order(padded[:2], padded[2], padded[3], padded[4])
    ratio = ratios(extend(upwind, sign_column((1.0, 1.0)), seam_partner_index), padded[4], inflow, outflow)
    advected = limited(extend(ratio, sign_column((1.0, 1.0, 1.0, 1.0)), seam_partner_index), upwind, anti, submerged_indicator)
    final = isopycnal(extend(advected, sign_column((1.0, 1.0)), seam_partner_index), padded[4])
    return final[0], final[1]
```

```python
from functools import reduce

import jax
import jax.numpy as jnp
from jax import lax
from jax.sharding import PartitionSpec as P

RATIO_FLOOR = 0.05
SLOPE_FLOOR = 0.5
SLOPE_LIMIT = 2.0
DIFFUSIVITY = 0.1
THERMAL_COEF = 0.2
HALINE_COEF = 0.8
STATE_SIGNS = (1.0, 1.0, -1.0, -1.0, 1.0)


def extended(cells, sides, width, closed):
    for axis, dim in sides:
        count = lax.axis_size(axis)
        ends = count if closed else count - 1
        head = lax.slice_in_dim(cells, 0, width, axis=dim)
        tail = lax.slice_in_dim(cells, cells.shape[dim] - width, cells.shape[dim], axis=dim)
        cells = jnp.concatenate(
            [
                lax.ppermute(tail, axis, [(i, (i + 1) % count) for i in range(ends)]),
                cells,
                lax.ppermute(head, axis, [((i + 1) % count, i) for i in range(ends)]),
            ],
            axis=dim,
        )
    return cells


def sign_column(values):
    return jnp.array(values, jnp.float32).reshape(len(values), 1, 1, 1)


def sided(core, west_col, east_col, south_row, north_row):
    width = core.shape[-1]
    height = core.shape[-2]
    lane = lax.broadcasted_iota(jnp.int32, core.shape, core.ndim - 1)
    level = lax.broadcasted_iota(jnp.int32, core.shape, core.ndim - 2)
    at_east = jnp.where(lane == width - 1, east_col, jnp.roll(core, -1, axis=-1))
    at_west = jnp.where(lane == 0, west_col, jnp.roll(core, 1, axis=-1))
    at_north = jnp.where(level == height - 1, north_row, jnp.roll(core, -1, axis=-2))
    at_south = jnp.where(level == 0, south_row, jnp.roll(core, 1, axis=-2))
    return (core, at_east, at_west, at_north, at_south)


def low_order(tracer, zonal, meridional, wet_sides):
    value_centre, value_east, value_west, value_north, value_south = tracer
    speed_centre, speed_west = (zonal[0], zonal[2])
    flow_centre, flow_south = (meridional[0], meridional[4])
    wet_centre, wet_east, wet_west, wet_north, wet_south = wet_sides
    face_east = wet_centre * wet_east
    face_west = wet_west * wet_centre
    face_north = wet_centre * wet_north
    face_south = wet_south * wet_centre
    upwind_east = face_east * (
        jnp.maximum(speed_centre, 0.0) * value_centre + jnp.minimum(speed_centre, 0.0) * value_east
    )
    upwind_west = face_west * (
        jnp.maximum(speed_west, 0.0) * value_west + jnp.minimum(speed_west, 0.0) * value_centre
    )
    upwind_north = face_north * (
        jnp.maximum(flow_centre, 0.0) * value_centre + jnp.minimum(flow_centre, 0.0) * value_north
    )
    upwind_south = face_south * (
        jnp.maximum(flow_south, 0.0) * value_south + jnp.minimum(flow_south, 0.0) * value_centre
    )
    anti_east = face_east * speed_centre * (value_centre + value_east) * 0.5 - upwind_east
    anti_west = face_west * speed_west * (value_west + value_centre) * 0.5 - upwind_west
    anti_north = face_north * flow_centre * (value_centre + value_north) * 0.5 - upwind_north
    anti_south = face_south * flow_south * (value_south + value_centre) * 0.5 - upwind_south
    upwind = value_centre - wet_centre * (upwind_east - upwind_west + upwind_north - upwind_south)
    inflow = (
        jnp.maximum(anti_west, 0.0)
        - jnp.minimum(anti_east, 0.0)
        + jnp.maximum(anti_south, 0.0)
        - jnp.minimum(anti_north, 0.0)
    )
    outflow = (
        jnp.maximum(anti_east, 0.0)
        - jnp.minimum(anti_west, 0.0)
        + jnp.maximum(anti_north, 0.0)
        - jnp.minimum(anti_south, 0.0)
    )
    anti = (anti_east, anti_west, anti_north, anti_south)
    return (upwind, anti, inflow, outflow)


def ratios(upwind_sides, wet_sides, inflow, outflow):
    value_centre, value_east, value_west, value_north, value_south = upwind_sides
    _, wet_east, wet_west, wet_north, wet_south = wet_sides
    pairs = (
        (value_east, wet_east),
        (value_west, wet_west),
        (value_north, wet_north),
        (value_south, wet_south),
    )
    candidates = [value_centre] + [
        jnp.where(beside_wet > 0.5, beside, value_centre) for beside, beside_wet in pairs
    ]
    highest = reduce(jnp.maximum, candidates)
    lowest = reduce(jnp.minimum, candidates)
    ratio_plus = jnp.minimum(1.0, (highest - value_centre) / jnp.maximum(inflow, RATIO_FLOOR))
    ratio_minus = jnp.minimum(1.0, (value_centre - lowest) / jnp.maximum(outflow, RATIO_FLOOR))
    return jnp.concatenate([ratio_plus, ratio_minus], axis=0)


def limited(ratio_sides, upwind, anti, wet_centre):
    plus_centre, plus_east, plus_west, plus_north, plus_south = [side[:2] for side in ratio_sides]
    minus_centre, minus_east, minus_west, minus_north, minus_south = [
        side[2:] for side in ratio_sides
    ]
    anti_east, anti_west, anti_north, anti_south = anti
    coef_east = jnp.where(
        anti_east >= 0.0, jnp.minimum(plus_east, minus_centre), jnp.minimum(plus_centre, minus_east)
    )
    coef_west = jnp.where(
        anti_west >= 0.0, jnp.minimum(plus_centre, minus_west), jnp.minimum(plus_west, minus_centre)
    )
    coef_north = jnp.where(
        anti_north >= 0.0,
        jnp.minimum(plus_north, minus_centre),
        jnp.minimum(plus_centre, minus_north),
    )
    coef_south = jnp.where(
        anti_south >= 0.0,
        jnp.minimum(plus_centre, minus_south),
        jnp.minimum(plus_south, minus_centre),
    )
    return upwind - wet_centre * (
        coef_east * anti_east
        - coef_west * anti_west
        + coef_north * anti_north
        - coef_south * anti_south
    )


def vertical_of(tracer, wet):
    stacked_wet = wet[:-1] * wet[1:]
    vertical = (tracer[:, 1:] - tracer[:, :-1]) * stacked_wet
    return jnp.concatenate([vertical, jnp.zeros_like(tracer[:, :1])], axis=1)


def isopycnal(values, wet_sides):
    verticals = tuple((vertical_of(tracer, wet) for tracer, wet in zip(values, wet_sides)))
    densities = tuple((HALINE_COEF * tracer[1] - THERMAL_COEF * tracer[0] for tracer in values))
    stratas = tuple(
        (HALINE_COEF * vertical[1] - THERMAL_COEF * vertical[0] for vertical in verticals)
    )

    def face_flux(first, second):
        face = wet_sides[first] * wet_sides[second]
        slope = jnp.clip(
            (densities[second] - densities[first])
            / jnp.maximum(0.5 * (stratas[first] + stratas[second]), SLOPE_FLOOR),
            -SLOPE_LIMIT,
            SLOPE_LIMIT,
        )
        return (
            DIFFUSIVITY
            * face
            * (
                values[second]
                - values[first]
                - slope * 0.5 * (verticals[first] + verticals[second])
            )
        )

    east_flux = face_flux(0, 1)
    west_flux = face_flux(2, 0)
    north_flux = face_flux(0, 3)
    south_flux = face_flux(4, 0)
    return values[0] + wet_sides[0] * (east_flux - west_flux + north_flux - south_flux)


def advance(state, sides):
    state_sides = sides(state, sign_column(STATE_SIGNS), 0)
    tracer = tuple((side[:2] for side in state_sides))
    zonal = tuple((side[2] for side in state_sides))
    meridional = tuple((side[3] for side in state_sides))
    wet_sides = tuple((side[4] for side in state_sides))
    upwind, anti, inflow, outflow = low_order(tracer, zonal, meridional, wet_sides)
    upwind_sides = sides(upwind, sign_column((1.0, 1.0)), 1)
    ratio = ratios(upwind_sides, wet_sides, inflow, outflow)
    ratio_sides = sides(ratio, sign_column((1.0, 1.0, 1.0, 1.0)), 2)
    advected = limited(ratio_sides, upwind, anti, wet_sides[0])
    advected_sides = sides(advected, sign_column((1.0, 1.0)), 3)
    return isopycnal(advected_sides, wet_sides)


def fold_row_of(top, pivot):
    count = lax.axis_size("lon")
    span = top.shape[-1]
    block, offset = pivot // span, pivot % span

    def branch(q):
        def exchange(row):
            lower = lax.ppermute(row, "lon", [((q - d - 1) % count, d) for d in range(count)])
            upper = lax.ppermute(row, "lon", [((q - d) % count, d) for d in range(count)])
            return lower, upper

        return exchange

    lower, upper = lax.switch(block, [branch(q) for q in range(count)], top)
    flipped = jnp.concatenate([lower, upper], axis=-1)[..., ::-1]
    return lax.dynamic_slice_in_dim(flipped, span - 1 - offset, span, axis=top.ndim - 1)


def local(
    heat_content_field,
    saltiness_field,
    eastward_cfl_number,
    northward_cfl_number,
    seawater_indicator,
    submerged_layer_total,
    seam_partner_index,
):
    span = heat_content_field.shape[2]
    anchor = lax.axis_index("lon") * span
    on_top = lax.axis_index("lat") == lax.axis_size("lat") - 1
    vertical_layer = jnp.arange(heat_content_field.shape[0], dtype=jnp.int32)[:, None, None]
    submerged_indicator = (
        (seawater_indicator[None] == 1) & (vertical_layer < submerged_layer_total[None])
    ).astype(jnp.float32)
    state = jnp.stack(
        [
            heat_content_field,
            saltiness_field,
            eastward_cfl_number,
            northward_cfl_number,
            submerged_indicator,
        ]
    )

    def rim_sides(stack, fold_row):
        columns = jnp.concatenate([stack[..., :1], stack[..., -1:]], axis=3)
        column_rim = extended(columns, (("lon", 3),), 1, True)
        rows = jnp.concatenate([stack[:, :, :1, :], stack[:, :, -1:, :]], axis=2)
        row_rim = extended(rows, (("lat", 2),), 1, False)
        north_row = jnp.where(on_top, fold_row, row_rim[:, :, 3:4, :])
        return sided(
            stack, column_rim[..., 0:1], column_rim[..., 3:4], row_rim[:, :, 0:1, :], north_row
        )

    def device_sides(stack, signs, segment):
        return rim_sides(stack, fold_row_of(stack[:, :, -1:, :], seam_partner_index[0]) * signs)

    final = advance(state, device_sides)
    return (final[0], final[1])


def solution(mesh):
    in_specs = (
        P(None, "lat", "lon"),
        P(None, "lat", "lon"),
        P(None, "lat", "lon"),
        P(None, "lat", "lon"),
        P("lat", "lon"),
        P("lat", "lon"),
        P(),
    )
    out_specs = (P(None, "lat", "lon"), P(None, "lat", "lon"))
    return jax.shard_map(local, mesh=mesh, in_specs=in_specs, out_specs=out_specs, check_vma=False)
```

```python
import functools

import jax
import jax.numpy as jnp
from jax import lax
from jax.experimental import pallas as pl
from jax.experimental.pallas import tpu as pltpu
from jax.sharding import PartitionSpec as P

RATIO_FLOOR = 0.05
SLOPE_FLOOR = 0.5
SLOPE_LIMIT = 2.0
DIFFUSIVITY = 0.1
THERMAL_COEF = 0.2
HALINE_COEF = 0.8
STATE_SIGNS = (1.0, 1.0, -1.0, -1.0, 1.0)


def sign_column(values):
    return jnp.array(values, jnp.float32).reshape(len(values), 1, 1, 1)


def around(x, west, east, south, north):
    height, width = x.shape
    lane = lax.broadcasted_iota(jnp.int32, x.shape, 1)
    level = lax.broadcasted_iota(jnp.int32, x.shape, 0)
    at_east = jnp.where(lane == width - 1, east, pltpu.roll(x, width - 1, 1))
    at_west = jnp.where(lane == 0, west, pltpu.roll(x, 1, 1))
    at_north = jnp.where(level == height - 1, north, pltpu.roll(x, height - 1, 0))
    at_south = jnp.where(level == 0, south, pltpu.roll(x, 1, 0))
    return (x, at_east, at_west, at_north, at_south)


def sides_of(refs, f, k):
    block, west, east, south, north = refs
    return around(block[f, k], west[f, k], east[f, k], south[f, k], north[f, k])


def low_order(tracer, zonal, meridional, wet_sides):
    value_centre, value_east, value_west, value_north, value_south = tracer
    speed_centre, speed_west = (zonal[0], zonal[2])
    flow_centre, flow_south = (meridional[0], meridional[4])
    wet_centre, wet_east, wet_west, wet_north, wet_south = wet_sides
    face_east = wet_centre * wet_east
    face_west = wet_west * wet_centre
    face_north = wet_centre * wet_north
    face_south = wet_south * wet_centre
    upwind_east = face_east * (
        jnp.maximum(speed_centre, 0.0) * value_centre + jnp.minimum(speed_centre, 0.0) * value_east
    )
    upwind_west = face_west * (
        jnp.maximum(speed_west, 0.0) * value_west + jnp.minimum(speed_west, 0.0) * value_centre
    )
    upwind_north = face_north * (
        jnp.maximum(flow_centre, 0.0) * value_centre + jnp.minimum(flow_centre, 0.0) * value_north
    )
    upwind_south = face_south * (
        jnp.maximum(flow_south, 0.0) * value_south + jnp.minimum(flow_south, 0.0) * value_centre
    )
    anti_east = face_east * speed_centre * (value_centre + value_east) * 0.5 - upwind_east
    anti_west = face_west * speed_west * (value_west + value_centre) * 0.5 - upwind_west
    anti_north = face_north * flow_centre * (value_centre + value_north) * 0.5 - upwind_north
    anti_south = face_south * flow_south * (value_south + value_centre) * 0.5 - upwind_south
    upwind = value_centre - wet_centre * (upwind_east - upwind_west + upwind_north - upwind_south)
    inflow = (
        jnp.maximum(anti_west, 0.0)
        - jnp.minimum(anti_east, 0.0)
        + jnp.maximum(anti_south, 0.0)
        - jnp.minimum(anti_north, 0.0)
    )
    outflow = (
        jnp.maximum(anti_east, 0.0)
        - jnp.minimum(anti_west, 0.0)
        + jnp.maximum(anti_north, 0.0)
        - jnp.minimum(anti_south, 0.0)
    )
    anti = (anti_east, anti_west, anti_north, anti_south)
    return (upwind, anti, inflow, outflow)


def level_low_order(state_refs, k, tracer):
    zonal = sides_of(state_refs, 2, k)
    meridional = sides_of(state_refs, 3, k)
    wet_sides = sides_of(state_refs, 4, k)
    return low_order(sides_of(state_refs, tracer, k), zonal, meridional, wet_sides), wet_sides


def ratio_pair(upwind_sides, wet_sides, inflow, outflow):
    value_centre = upwind_sides[0]
    candidates = [value_centre] + [
        jnp.where(beside_wet > 0.5, beside, value_centre)
        for beside, beside_wet in zip(upwind_sides[1:], wet_sides[1:])
    ]
    highest = functools.reduce(jnp.maximum, candidates)
    lowest = functools.reduce(jnp.minimum, candidates)
    ratio_plus = jnp.minimum(1.0, (highest - value_centre) / jnp.maximum(inflow, RATIO_FLOOR))
    ratio_minus = jnp.minimum(1.0, (value_centre - lowest) / jnp.maximum(outflow, RATIO_FLOOR))
    return ratio_plus, ratio_minus


def limited(plus, minus, upwind, anti, wet_centre):
    plus_centre, plus_east, plus_west, plus_north, plus_south = plus
    minus_centre, minus_east, minus_west, minus_north, minus_south = minus
    anti_east, anti_west, anti_north, anti_south = anti
    coef_east = jnp.where(
        anti_east >= 0.0, jnp.minimum(plus_east, minus_centre), jnp.minimum(plus_centre, minus_east)
    )
    coef_west = jnp.where(
        anti_west >= 0.0, jnp.minimum(plus_centre, minus_west), jnp.minimum(plus_west, minus_centre)
    )
    coef_north = jnp.where(
        anti_north >= 0.0,
        jnp.minimum(plus_north, minus_centre),
        jnp.minimum(plus_centre, minus_north),
    )
    coef_south = jnp.where(
        anti_south >= 0.0,
        jnp.minimum(plus_centre, minus_south),
        jnp.minimum(plus_south, minus_centre),
    )
    return upwind - wet_centre * (
        coef_east * anti_east
        - coef_west * anti_west
        + coef_north * anti_north
        - coef_south * anti_south
    )


def upwind_kernel(*refs):
    state_refs, out = refs[:5], refs[5]
    levels = out.shape[1]

    def body(k, carry):
        for tracer in range(2):
            (upwind, _, _, _), _ = level_low_order(state_refs, k, tracer)
            out[tracer, k] = upwind
        return carry

    lax.fori_loop(0, levels, body, 0)


def ratio_kernel(*refs):
    state_refs, upwind_refs, out = refs[:5], refs[5:10], refs[10]
    levels = out.shape[1]

    def body(k, carry):
        for tracer in range(2):
            (_, _, inflow, outflow), wet_sides = level_low_order(state_refs, k, tracer)
            plus, minus = ratio_pair(sides_of(upwind_refs, tracer, k), wet_sides, inflow, outflow)
            out[tracer, k] = plus
            out[2 + tracer, k] = minus
        return carry

    lax.fori_loop(0, levels, body, 0)


def advected_kernel(*refs):
    state_refs, upwind_ref, ratio_refs, out = refs[:5], refs[5], refs[6:11], refs[11]
    levels = out.shape[1]

    def body(k, carry):
        for tracer in range(2):
            (_, anti, _, _), wet_sides = level_low_order(state_refs, k, tracer)
            plus = sides_of(ratio_refs, tracer, k)
            minus = sides_of(ratio_refs, 2 + tracer, k)
            out[tracer, k] = limited(plus, minus, upwind_ref[tracer, k], anti, wet_sides[0])
        return carry

    lax.fori_loop(0, levels, body, 0)


def isopycnal_kernel(*refs):
    advected_refs, state_refs, out = refs[:5], refs[5:10], refs[10]
    levels = out.shape[1]

    def body(k, carry):
        above = jnp.minimum(k + 1, levels - 1)
        values = [sides_of(advected_refs, tracer, k) for tracer in range(2)]
        uppers = [sides_of(advected_refs, tracer, above) for tracer in range(2)]
        wet_sides = sides_of(state_refs, 4, k)
        wet_above = sides_of(state_refs, 4, above)
        stacked = [w * a for w, a in zip(wet_sides, wet_above)]
        verticals = [
            [(u - v) * s for u, v, s in zip(uppers[tracer], values[tracer], stacked)]
            for tracer in range(2)
        ]
        densities = [HALINE_COEF * s - THERMAL_COEF * t for t, s in zip(values[0], values[1])]
        stratas = [HALINE_COEF * s - THERMAL_COEF * t for t, s in zip(verticals[0], verticals[1])]
        for tracer in range(2):
            value, vertical = values[tracer], verticals[tracer]

            def face_flux(first, second):
                face = wet_sides[first] * wet_sides[second]
                slope = jnp.clip(
                    (densities[second] - densities[first])
                    / jnp.maximum(0.5 * (stratas[first] + stratas[second]), SLOPE_FLOOR),
                    -SLOPE_LIMIT,
                    SLOPE_LIMIT,
                )
                return (
                    DIFFUSIVITY
                    * face
                    * (
                        value[second]
                        - value[first]
                        - slope * 0.5 * (vertical[first] + vertical[second])
                    )
                )

            east_flux = face_flux(0, 1)
            west_flux = face_flux(2, 0)
            north_flux = face_flux(0, 3)
            south_flux = face_flux(4, 0)
            out[tracer, k] = value[0] + wet_sides[0] * (
                east_flux - west_flux + north_flux - south_flux
            )
        return carry

    lax.fori_loop(0, levels, body, 0)


def stage(kernel, fields, *args):
    shape = args[0].shape
    return pl.pallas_call(
        kernel,
        out_shape=jax.ShapeDtypeStruct((fields,) + shape[1:], jnp.float32),
        in_specs=[pl.BlockSpec(memory_space=pltpu.VMEM)] * len(args),
        out_specs=pl.BlockSpec(memory_space=pltpu.VMEM),
    )(*args)


def local(
    heat_content_field,
    saltiness_field,
    eastward_cfl_number,
    northward_cfl_number,
    seawater_indicator,
    submerged_layer_total,
    seam_partner_index,
):
    span = heat_content_field.shape[2]
    anchor = lax.axis_index("lon") * span
    on_top = lax.axis_index("lat") == lax.axis_size("lat") - 1
    vertical_layer = jnp.arange(heat_content_field.shape[0], dtype=jnp.int32)[:, None, None]
    submerged_indicator = (
        (seawater_indicator[None] == 1) & (vertical_layer < submerged_layer_total[None])
    ).astype(jnp.float32)
    state = jnp.stack(
        [
            heat_content_field,
            saltiness_field,
            eastward_cfl_number,
            northward_cfl_number,
            submerged_indicator,
        ]
    )
    facing = jnp.take(seam_partner_index, anchor + jnp.arange(span, dtype=jnp.int32))

    def halos(stack, signs):
        lon = lax.axis_size("lon")
        lat = lax.axis_size("lat")
        west = lax.ppermute(stack[..., -1:], "lon", [(i, (i + 1) % lon) for i in range(lon)])
        east = lax.ppermute(stack[..., :1], "lon", [((i + 1) % lon, i) for i in range(lon)])
        south = lax.ppermute(stack[:, :, -1:, :], "lat", [(i, i + 1) for i in range(lat - 1)])
        north = lax.ppermute(stack[:, :, :1, :], "lat", [(i + 1, i) for i in range(lat - 1)])
        top_row = lax.all_gather(stack[:, :, -1:, :], "lon", axis=3, tiled=True)
        fold_row = jnp.take(top_row, facing, axis=3) * signs
        return (stack, west, east, south, jnp.where(on_top, fold_row, north))

    state_refs = halos(state, sign_column(STATE_SIGNS))
    upwind = stage(upwind_kernel, 2, *state_refs)
    upwind_refs = halos(upwind, sign_column((1.0, 1.0)))
    ratio = stage(ratio_kernel, 4, *state_refs, *upwind_refs)
    ratio_refs = halos(ratio, sign_column((1.0,) * 4))
    advected = stage(advected_kernel, 2, *state_refs, upwind, *ratio_refs)
    advected_refs = halos(advected, sign_column((1.0, 1.0)))
    final = stage(isopycnal_kernel, 2, *advected_refs, *state_refs)
    return (final[0], final[1])


def solution(mesh):
    in_specs = (
        P(None, "lat", "lon"),
        P(None, "lat", "lon"),
        P(None, "lat", "lon"),
        P(None, "lat", "lon"),
        P("lat", "lon"),
        P("lat", "lon"),
        P(),
    )
    out_specs = (P(None, "lat", "lon"), P(None, "lat", "lon"))
    return jax.shard_map(local, mesh=mesh, in_specs=in_specs, out_specs=out_specs, check_vma=False)
```

```python
import functools

import jax
import jax.numpy as jnp
from jax import lax
from jax.experimental import pallas as pl
from jax.experimental.pallas import tpu as pltpu
from jax.sharding import PartitionSpec as P

RATIO_FLOOR = 0.05
SLOPE_FLOOR = 0.5
SLOPE_LIMIT = 2.0
DIFFUSIVITY = 0.1
THERMAL_COEF = 0.2
HALINE_COEF = 0.8
STATE_SIGNS = (1.0, 1.0, -1.0, -1.0, 1.0)


def sign_column(values):
    return jnp.array(values, jnp.float32).reshape(len(values), 1, 1, 1)


def around(x, west, east, south, north):
    height, width = x.shape
    lane = lax.broadcasted_iota(jnp.int32, x.shape, 1)
    level = lax.broadcasted_iota(jnp.int32, x.shape, 0)
    at_east = jnp.where(lane == width - 1, east, pltpu.roll(x, width - 1, 1))
    at_west = jnp.where(lane == 0, west, pltpu.roll(x, 1, 1))
    at_north = jnp.where(level == height - 1, north, pltpu.roll(x, height - 1, 0))
    at_south = jnp.where(level == 0, south, pltpu.roll(x, 1, 0))
    return (x, at_east, at_west, at_north, at_south)


def sides_of(refs, f, k):
    block, west, east, south, north = refs
    return around(block[f, k], west[f, k], east[f, k], south[f, k], north[f, k])


def low_order(tracer, zonal, meridional, wet_sides):
    value_centre, value_east, value_west, value_north, value_south = tracer
    speed_centre, speed_west = (zonal[0], zonal[2])
    flow_centre, flow_south = (meridional[0], meridional[4])
    wet_centre, wet_east, wet_west, wet_north, wet_south = wet_sides
    face_east = wet_centre * wet_east
    face_west = wet_west * wet_centre
    face_north = wet_centre * wet_north
    face_south = wet_south * wet_centre
    upwind_east = face_east * (
        jnp.maximum(speed_centre, 0.0) * value_centre + jnp.minimum(speed_centre, 0.0) * value_east
    )
    upwind_west = face_west * (
        jnp.maximum(speed_west, 0.0) * value_west + jnp.minimum(speed_west, 0.0) * value_centre
    )
    upwind_north = face_north * (
        jnp.maximum(flow_centre, 0.0) * value_centre + jnp.minimum(flow_centre, 0.0) * value_north
    )
    upwind_south = face_south * (
        jnp.maximum(flow_south, 0.0) * value_south + jnp.minimum(flow_south, 0.0) * value_centre
    )
    anti_east = face_east * speed_centre * (value_centre + value_east) * 0.5 - upwind_east
    anti_west = face_west * speed_west * (value_west + value_centre) * 0.5 - upwind_west
    anti_north = face_north * flow_centre * (value_centre + value_north) * 0.5 - upwind_north
    anti_south = face_south * flow_south * (value_south + value_centre) * 0.5 - upwind_south
    upwind = value_centre - wet_centre * (upwind_east - upwind_west + upwind_north - upwind_south)
    inflow = (
        jnp.maximum(anti_west, 0.0)
        - jnp.minimum(anti_east, 0.0)
        + jnp.maximum(anti_south, 0.0)
        - jnp.minimum(anti_north, 0.0)
    )
    outflow = (
        jnp.maximum(anti_east, 0.0)
        - jnp.minimum(anti_west, 0.0)
        + jnp.maximum(anti_north, 0.0)
        - jnp.minimum(anti_south, 0.0)
    )
    anti = (anti_east, anti_west, anti_north, anti_south)
    return (upwind, anti, inflow, outflow)


def level_low_order(state_refs, k, tracer):
    zonal = sides_of(state_refs, 2, k)
    meridional = sides_of(state_refs, 3, k)
    wet_sides = sides_of(state_refs, 4, k)
    return low_order(sides_of(state_refs, tracer, k), zonal, meridional, wet_sides), wet_sides


def ratio_pair(upwind_sides, wet_sides, inflow, outflow):
    value_centre = upwind_sides[0]
    candidates = [value_centre] + [
        jnp.where(beside_wet > 0.5, beside, value_centre)
        for beside, beside_wet in zip(upwind_sides[1:], wet_sides[1:])
    ]
    highest = functools.reduce(jnp.maximum, candidates)
    lowest = functools.reduce(jnp.minimum, candidates)
    ratio_plus = jnp.minimum(1.0, (highest - value_centre) / jnp.maximum(inflow, RATIO_FLOOR))
    ratio_minus = jnp.minimum(1.0, (value_centre - lowest) / jnp.maximum(outflow, RATIO_FLOOR))
    return ratio_plus, ratio_minus


def limited(plus, minus, upwind, anti, wet_centre):
    plus_centre, plus_east, plus_west, plus_north, plus_south = plus
    minus_centre, minus_east, minus_west, minus_north, minus_south = minus
    anti_east, anti_west, anti_north, anti_south = anti
    coef_east = jnp.where(
        anti_east >= 0.0, jnp.minimum(plus_east, minus_centre), jnp.minimum(plus_centre, minus_east)
    )
    coef_west = jnp.where(
        anti_west >= 0.0, jnp.minimum(plus_centre, minus_west), jnp.minimum(plus_west, minus_centre)
    )
    coef_north = jnp.where(
        anti_north >= 0.0,
        jnp.minimum(plus_north, minus_centre),
        jnp.minimum(plus_centre, minus_north),
    )
    coef_south = jnp.where(
        anti_south >= 0.0,
        jnp.minimum(plus_centre, minus_south),
        jnp.minimum(plus_south, minus_centre),
    )
    return upwind - wet_centre * (
        coef_east * anti_east
        - coef_west * anti_west
        + coef_north * anti_north
        - coef_south * anti_south
    )


def upwind_kernel(*refs):
    state_refs, out = refs[:5], refs[5]
    levels = out.shape[1]

    def body(k, carry):
        for tracer in range(2):
            (upwind, _, _, _), _ = level_low_order(state_refs, k, tracer)
            out[tracer, k] = upwind
        return carry

    lax.fori_loop(0, levels, body, 0)


def ratio_kernel(*refs):
    state_refs, upwind_refs, out = refs[:5], refs[5:10], refs[10]
    levels = out.shape[1]

    def body(k, carry):
        for tracer in range(2):
            (_, _, inflow, outflow), wet_sides = level_low_order(state_refs, k, tracer)
            plus, minus = ratio_pair(sides_of(upwind_refs, tracer, k), wet_sides, inflow, outflow)
            out[tracer, k] = plus
            out[2 + tracer, k] = minus
        return carry

    lax.fori_loop(0, levels, body, 0)


def advected_kernel(*refs):
    state_refs, upwind_ref, ratio_refs, out = refs[:5], refs[5], refs[6:11], refs[11]
    levels = out.shape[1]

    def body(k, carry):
        for tracer in range(2):
            (_, anti, _, _), wet_sides = level_low_order(state_refs, k, tracer)
            plus = sides_of(ratio_refs, tracer, k)
            minus = sides_of(ratio_refs, 2 + tracer, k)
            out[tracer, k] = limited(plus, minus, upwind_ref[tracer, k], anti, wet_sides[0])
        return carry

    lax.fori_loop(0, levels, body, 0)


def isopycnal_kernel(*refs):
    advected_refs, state_refs, out = refs[:5], refs[5:10], refs[10]
    levels = out.shape[1]

    def body(k, carry):
        above = jnp.minimum(k + 1, levels - 1)
        values = [sides_of(advected_refs, tracer, k) for tracer in range(2)]
        uppers = [sides_of(advected_refs, tracer, above) for tracer in range(2)]
        wet_sides = sides_of(state_refs, 4, k)
        wet_above = sides_of(state_refs, 4, above)
        stacked = [w * a for w, a in zip(wet_sides, wet_above)]
        verticals = [
            [(u - v) * s for u, v, s in zip(uppers[tracer], values[tracer], stacked)]
            for tracer in range(2)
        ]
        densities = [HALINE_COEF * s - THERMAL_COEF * t for t, s in zip(values[0], values[1])]
        stratas = [HALINE_COEF * s - THERMAL_COEF * t for t, s in zip(verticals[0], verticals[1])]
        for tracer in range(2):
            value, vertical = values[tracer], verticals[tracer]

            def face_flux(first, second):
                face = wet_sides[first] * wet_sides[second]
                slope = jnp.clip(
                    (densities[second] - densities[first])
                    / jnp.maximum(0.5 * (stratas[first] + stratas[second]), SLOPE_FLOOR),
                    -SLOPE_LIMIT,
                    SLOPE_LIMIT,
                )
                return (
                    DIFFUSIVITY
                    * face
                    * (
                        value[second]
                        - value[first]
                        - slope * 0.5 * (vertical[first] + vertical[second])
                    )
                )

            east_flux = face_flux(0, 1)
            west_flux = face_flux(2, 0)
            north_flux = face_flux(0, 3)
            south_flux = face_flux(4, 0)
            out[tracer, k] = value[0] + wet_sides[0] * (
                east_flux - west_flux + north_flux - south_flux
            )
        return carry

    lax.fori_loop(0, levels, body, 0)


def exchange_kernel(
    lon,
    lat,
    west_col,
    east_col,
    south_row,
    north_row,
    gathered,
    west_halo,
    east_halo,
    south_halo,
    north_halo,
    fold_send,
    fold_recv,
    side_send,
    side_recv,
):
    mesh = pl.DeviceIdType.MESH
    me = lax.axis_index("lon")
    row = lax.axis_index("lat")
    west = lax.rem(me + lon - 1, lon)
    east = lax.rem(me + 1, lon)
    has_south = row > 0
    has_north = row < lat - 1

    barrier = pltpu.get_barrier_semaphore()
    for peer in range(lon):

        @pl.when(me != peer)
        def _():
            pl.semaphore_signal(barrier, 1, device_id={"lon": peer}, device_id_type=mesh)

    @pl.when(has_south)
    def _():
        pl.semaphore_signal(barrier, 1, device_id={"lat": row - 1}, device_id_type=mesh)

    @pl.when(has_north)
    def _():
        pl.semaphore_signal(barrier, 1, device_id={"lat": row + 1}, device_id_type=mesh)

    pl.semaphore_wait(
        barrier, lon - 1 + has_south.astype(jnp.int32) + has_north.astype(jnp.int32)
    )

    def fold_copy(peer, slot):
        return pltpu.make_async_remote_copy(
            src_ref=north_row,
            dst_ref=gathered.at[slot],
            send_sem=fold_send.at[peer],
            recv_sem=fold_recv.at[slot],
            device_id={"lon": peer},
            device_id_type=mesh,
        )

    for peer in range(lon):

        @pl.when(me != peer)
        def _():
            fold_copy(peer, me).start()

    to_west = pltpu.make_async_remote_copy(
        src_ref=west_col,
        dst_ref=east_halo,
        send_sem=side_send.at[0],
        recv_sem=side_recv.at[0],
        device_id={"lon": west},
        device_id_type=mesh,
    )
    to_east = pltpu.make_async_remote_copy(
        src_ref=east_col,
        dst_ref=west_halo,
        send_sem=side_send.at[1],
        recv_sem=side_recv.at[1],
        device_id={"lon": east},
        device_id_type=mesh,
    )
    to_west.start()
    to_east.start()
    to_south = pltpu.make_async_remote_copy(
        src_ref=south_row,
        dst_ref=north_halo,
        send_sem=side_send.at[2],
        recv_sem=side_recv.at[2],
        device_id={"lat": row - 1},
        device_id_type=mesh,
    )
    to_north = pltpu.make_async_remote_copy(
        src_ref=north_row,
        dst_ref=south_halo,
        send_sem=side_send.at[3],
        recv_sem=side_recv.at[3],
        device_id={"lat": row + 1},
        device_id_type=mesh,
    )

    @pl.when(has_south)
    def _():
        to_south.start()

    @pl.when(has_north)
    def _():
        to_north.start()

    gathered[me] = north_row[...]

    for peer in range(lon):

        @pl.when(me != peer)
        def _():
            fold_copy(peer, me).wait_send()
            fold_copy(peer, peer).wait_recv()

    to_west.wait()
    to_east.wait()

    @pl.when(has_south)
    def _():
        to_south.wait_send()
        to_north.wait_recv()

    @pl.when(has_north)
    def _():
        to_north.wait_send()
        to_south.wait_recv()

    @pl.when(jnp.logical_not(has_south))
    def _():
        south_halo[...] = jnp.zeros_like(south_halo)

    @pl.when(jnp.logical_not(has_north))
    def _():
        north_halo[...] = jnp.zeros_like(north_halo)


def stage(kernel, fields, *args):
    shape = args[0].shape
    return pl.pallas_call(
        kernel,
        out_shape=jax.ShapeDtypeStruct((fields,) + shape[1:], jnp.float32),
        in_specs=[pl.BlockSpec(memory_space=pltpu.VMEM)] * len(args),
        out_specs=pl.BlockSpec(memory_space=pltpu.VMEM),
    )(*args)


def local(
    heat_content_field,
    saltiness_field,
    eastward_cfl_number,
    northward_cfl_number,
    seawater_indicator,
    submerged_layer_total,
    seam_partner_index,
):
    span = heat_content_field.shape[2]
    anchor = lax.axis_index("lon") * span
    on_top = lax.axis_index("lat") == lax.axis_size("lat") - 1
    vertical_layer = jnp.arange(heat_content_field.shape[0], dtype=jnp.int32)[:, None, None]
    submerged_indicator = (
        (seawater_indicator[None] == 1) & (vertical_layer < submerged_layer_total[None])
    ).astype(jnp.float32)
    state = jnp.stack(
        [
            heat_content_field,
            saltiness_field,
            eastward_cfl_number,
            northward_cfl_number,
            submerged_indicator,
        ]
    )
    facing = jnp.take(seam_partner_index, anchor + jnp.arange(span, dtype=jnp.int32))

    def halos(stack, signs, cid):
        fields = stack.shape[0]
        lon = lax.axis_size("lon")
        lat = lax.axis_size("lat")
        row_shape = jax.ShapeDtypeStruct((fields,) + stack.shape[1:2] + stack.shape[3:], jnp.float32)
        col_shape = jax.ShapeDtypeStruct(stack.shape[:3], jnp.float32)
        gathered, west, east, south, north = pl.pallas_call(
            functools.partial(exchange_kernel, lon, lat),
            out_shape=(
                jax.ShapeDtypeStruct((lon,) + row_shape.shape, jnp.float32),
                col_shape,
                col_shape,
                row_shape,
                row_shape,
            ),
            in_specs=[pl.BlockSpec(memory_space=pltpu.VMEM)] * 4,
            out_specs=[pl.BlockSpec(memory_space=pltpu.VMEM)] * 5,
            scratch_shapes=[
                pltpu.SemaphoreType.DMA((lon,)),
                pltpu.SemaphoreType.DMA((lon,)),
                pltpu.SemaphoreType.DMA((4,)),
                pltpu.SemaphoreType.DMA((4,)),
            ],
            compiler_params=pltpu.CompilerParams(collective_id=cid, has_side_effects=True),
        )(stack[..., 0], stack[..., -1], stack[:, :, 0, :], stack[:, :, -1, :])
        top_row = jnp.moveaxis(gathered, 0, 2).reshape(row_shape.shape[:2] + (-1,))
        fold_row = jnp.take(top_row, facing, axis=2)[:, :, None, :] * signs
        return (
            stack,
            west[..., None],
            east[..., None],
            south[:, :, None, :],
            jnp.where(on_top, fold_row, north[:, :, None, :]),
        )

    state_refs = halos(state, sign_column(STATE_SIGNS), 0)
    upwind = stage(upwind_kernel, 2, *state_refs)
    upwind_refs = halos(upwind, sign_column((1.0, 1.0)), 1)
    ratio = stage(ratio_kernel, 4, *state_refs, *upwind_refs)
    ratio_refs = halos(ratio, sign_column((1.0,) * 4), 2)
    advected = stage(advected_kernel, 2, *state_refs, upwind, *ratio_refs)
    advected_refs = halos(advected, sign_column((1.0, 1.0)), 3)
    final = stage(isopycnal_kernel, 2, *advected_refs, *state_refs)
    return (final[0], final[1])


def solution(mesh):
    in_specs = (
        P(None, "lat", "lon"),
        P(None, "lat", "lon"),
        P(None, "lat", "lon"),
        P(None, "lat", "lon"),
        P("lat", "lon"),
        P("lat", "lon"),
        P(),
    )
    out_specs = (P(None, "lat", "lon"), P(None, "lat", "lon"))
    return jax.shard_map(local, mesh=mesh, in_specs=in_specs, out_specs=out_specs, check_vma=False)
```

```python
import functools

import jax
import jax.numpy as jnp
from jax import lax
from jax.experimental import pallas as pl
from jax.experimental.pallas import tpu as pltpu
from jax.sharding import PartitionSpec as P

RATIO_FLOOR = 0.05
SLOPE_FLOOR = 0.5
SLOPE_LIMIT = 2.0
DIFFUSIVITY = 0.1
THERMAL_COEF = 0.2
HALINE_COEF = 0.8
STATE_SIGNS = (1.0, 1.0, -1.0, -1.0, 1.0)


def sign_column(values):
    return jnp.array(values, jnp.float32).reshape(len(values), 1, 1, 1)


def around(x, west, east, south, north):
    height, width = x.shape
    lane = lax.broadcasted_iota(jnp.int32, x.shape, 1)
    level = lax.broadcasted_iota(jnp.int32, x.shape, 0)
    at_east = jnp.where(lane == width - 1, east, pltpu.roll(x, width - 1, 1))
    at_west = jnp.where(lane == 0, west, pltpu.roll(x, 1, 1))
    at_north = jnp.where(level == height - 1, north, pltpu.roll(x, height - 1, 0))
    at_south = jnp.where(level == 0, south, pltpu.roll(x, 1, 0))
    return (x, at_east, at_west, at_north, at_south)


def sides_of(refs, f, k):
    block, west, east, south, north = refs
    return around(
        block[f, k], west[f, k], east[f, k], south[f, pl.ds(k, 1), :], north[f, pl.ds(k, 1), :]
    )


def low_order(tracer, zonal, meridional, wet_sides):
    value_centre, value_east, value_west, value_north, value_south = tracer
    speed_centre, speed_west = (zonal[0], zonal[2])
    flow_centre, flow_south = (meridional[0], meridional[4])
    wet_centre, wet_east, wet_west, wet_north, wet_south = wet_sides
    face_east = wet_centre * wet_east
    face_west = wet_west * wet_centre
    face_north = wet_centre * wet_north
    face_south = wet_south * wet_centre
    upwind_east = face_east * (
        jnp.maximum(speed_centre, 0.0) * value_centre + jnp.minimum(speed_centre, 0.0) * value_east
    )
    upwind_west = face_west * (
        jnp.maximum(speed_west, 0.0) * value_west + jnp.minimum(speed_west, 0.0) * value_centre
    )
    upwind_north = face_north * (
        jnp.maximum(flow_centre, 0.0) * value_centre + jnp.minimum(flow_centre, 0.0) * value_north
    )
    upwind_south = face_south * (
        jnp.maximum(flow_south, 0.0) * value_south + jnp.minimum(flow_south, 0.0) * value_centre
    )
    anti_east = face_east * speed_centre * (value_centre + value_east) * 0.5 - upwind_east
    anti_west = face_west * speed_west * (value_west + value_centre) * 0.5 - upwind_west
    anti_north = face_north * flow_centre * (value_centre + value_north) * 0.5 - upwind_north
    anti_south = face_south * flow_south * (value_south + value_centre) * 0.5 - upwind_south
    upwind = value_centre - wet_centre * (upwind_east - upwind_west + upwind_north - upwind_south)
    inflow = (
        jnp.maximum(anti_west, 0.0)
        - jnp.minimum(anti_east, 0.0)
        + jnp.maximum(anti_south, 0.0)
        - jnp.minimum(anti_north, 0.0)
    )
    outflow = (
        jnp.maximum(anti_east, 0.0)
        - jnp.minimum(anti_west, 0.0)
        + jnp.maximum(anti_north, 0.0)
        - jnp.minimum(anti_south, 0.0)
    )
    anti = (anti_east, anti_west, anti_north, anti_south)
    return (upwind, anti, inflow, outflow)


def level_low_order(state_refs, k, tracer):
    zonal = sides_of(state_refs, 2, k)
    meridional = sides_of(state_refs, 3, k)
    wet_sides = sides_of(state_refs, 4, k)
    return low_order(sides_of(state_refs, tracer, k), zonal, meridional, wet_sides), wet_sides


def ratio_pair(upwind_sides, wet_sides, inflow, outflow):
    value_centre = upwind_sides[0]
    candidates = [value_centre] + [
        jnp.where(beside_wet > 0.5, beside, value_centre)
        for beside, beside_wet in zip(upwind_sides[1:], wet_sides[1:])
    ]
    highest = functools.reduce(jnp.maximum, candidates)
    lowest = functools.reduce(jnp.minimum, candidates)
    ratio_plus = jnp.minimum(1.0, (highest - value_centre) / jnp.maximum(inflow, RATIO_FLOOR))
    ratio_minus = jnp.minimum(1.0, (value_centre - lowest) / jnp.maximum(outflow, RATIO_FLOOR))
    return ratio_plus, ratio_minus


def limited(plus, minus, upwind, anti, wet_centre):
    plus_centre, plus_east, plus_west, plus_north, plus_south = plus
    minus_centre, minus_east, minus_west, minus_north, minus_south = minus
    anti_east, anti_west, anti_north, anti_south = anti
    coef_east = jnp.where(
        anti_east >= 0.0, jnp.minimum(plus_east, minus_centre), jnp.minimum(plus_centre, minus_east)
    )
    coef_west = jnp.where(
        anti_west >= 0.0, jnp.minimum(plus_centre, minus_west), jnp.minimum(plus_west, minus_centre)
    )
    coef_north = jnp.where(
        anti_north >= 0.0,
        jnp.minimum(plus_north, minus_centre),
        jnp.minimum(plus_centre, minus_north),
    )
    coef_south = jnp.where(
        anti_south >= 0.0,
        jnp.minimum(plus_centre, minus_south),
        jnp.minimum(plus_south, minus_centre),
    )
    return upwind - wet_centre * (
        coef_east * anti_east
        - coef_west * anti_west
        + coef_north * anti_north
        - coef_south * anti_south
    )


def upwind_kernel(*refs):
    state_refs, out = refs[:5], refs[5]
    levels = out.shape[1]

    def body(k, carry):
        for tracer in range(2):
            (upwind, _, _, _), _ = level_low_order(state_refs, k, tracer)
            out[tracer, k] = upwind
        return carry

    lax.fori_loop(0, levels, body, 0)


def ratio_kernel(*refs):
    state_refs, upwind_refs, out = refs[:5], refs[5:10], refs[10]
    levels = out.shape[1]

    def body(k, carry):
        for tracer in range(2):
            (_, _, inflow, outflow), wet_sides = level_low_order(state_refs, k, tracer)
            plus, minus = ratio_pair(sides_of(upwind_refs, tracer, k), wet_sides, inflow, outflow)
            out[tracer, k] = plus
            out[2 + tracer, k] = minus
        return carry

    lax.fori_loop(0, levels, body, 0)


def advected_kernel(*refs):
    state_refs, upwind_ref, ratio_refs, out = refs[:5], refs[5], refs[6:11], refs[11]
    levels = out.shape[1]

    def body(k, carry):
        for tracer in range(2):
            (_, anti, _, _), wet_sides = level_low_order(state_refs, k, tracer)
            plus = sides_of(ratio_refs, tracer, k)
            minus = sides_of(ratio_refs, 2 + tracer, k)
            out[tracer, k] = limited(plus, minus, upwind_ref[tracer, k], anti, wet_sides[0])
        return carry

    lax.fori_loop(0, levels, body, 0)


def isopycnal_kernel(*refs):
    advected_refs, state_refs, out = refs[:5], refs[5:10], refs[10]
    levels = out.shape[1]

    def body(k, carry):
        above = jnp.minimum(k + 1, levels - 1)
        values = [sides_of(advected_refs, tracer, k) for tracer in range(2)]
        uppers = [sides_of(advected_refs, tracer, above) for tracer in range(2)]
        wet_sides = sides_of(state_refs, 4, k)
        wet_above = sides_of(state_refs, 4, above)
        stacked = [w * a for w, a in zip(wet_sides, wet_above)]
        verticals = [
            [(u - v) * s for u, v, s in zip(uppers[tracer], values[tracer], stacked)]
            for tracer in range(2)
        ]
        densities = [HALINE_COEF * s - THERMAL_COEF * t for t, s in zip(values[0], values[1])]
        stratas = [HALINE_COEF * s - THERMAL_COEF * t for t, s in zip(verticals[0], verticals[1])]
        for tracer in range(2):
            value, vertical = values[tracer], verticals[tracer]

            def face_flux(first, second):
                face = wet_sides[first] * wet_sides[second]
                slope = jnp.clip(
                    (densities[second] - densities[first])
                    / jnp.maximum(0.5 * (stratas[first] + stratas[second]), SLOPE_FLOOR),
                    -SLOPE_LIMIT,
                    SLOPE_LIMIT,
                )
                return (
                    DIFFUSIVITY
                    * face
                    * (
                        value[second]
                        - value[first]
                        - slope * 0.5 * (vertical[first] + vertical[second])
                    )
                )

            east_flux = face_flux(0, 1)
            west_flux = face_flux(2, 0)
            north_flux = face_flux(0, 3)
            south_flux = face_flux(4, 0)
            out[tracer, k] = value[0] + wet_sides[0] * (
                east_flux - west_flux + north_flux - south_flux
            )
        return carry

    lax.fori_loop(0, levels, body, 0)


class Pair:
    def __init__(self, first, second):
        self.refs = (first, second)
        self.shape = (2,) + first.shape

    def __setitem__(self, index, value):
        self.refs[index[0]][index[1]] = value


def buffers_for(fields, levels, height, width, lon):
    columns = pltpu.VMEM((fields, 16, height), jnp.float32)
    rows = pltpu.VMEM((fields, levels, width), jnp.float32)
    halo = pltpu.VMEM((fields, levels, height, 1), jnp.float32)
    return [
        columns,
        columns,
        rows,
        rows,
        columns,
        columns,
        rows,
        rows,
        pltpu.VMEM((lon, fields, levels, width), jnp.float32),
        halo,
        halo,
        rows,
    ]


STAGE_FIELDS = (5, 2, 4, 2)


def fused_kernel(lon, lat, signs, blocks, reverse, state, first_out, second_out, *scratch):
    mesh = pl.DeviceIdType.MESH
    upwind, ratio, advected = scratch[:3]
    count = len(STAGE_FIELDS)
    per_stage = [scratch[3 + 12 * s : 15 + 12 * s] for s in range(count)]
    fold_send, fold_recv, side_send, side_recv = scratch[3 + 12 * count :]
    me = lax.axis_index("lon")
    row = lax.axis_index("lat")
    west = lax.rem(me + lon - 1, lon)
    east = lax.rem(me + 1, lon)
    has_south = row > 0
    has_north = row < lat - 1
    on_top = row == lat - 1
    levels, height, width = state.shape[1:]

    barrier = pltpu.get_barrier_semaphore()
    for peer in range(lon):

        @pl.when(me != peer)
        def _():
            pl.semaphore_signal(barrier, 1, device_id={"lon": peer}, device_id_type=mesh)

    @pl.when(has_south)
    def _():
        pl.semaphore_signal(barrier, 1, device_id={"lat": row - 1}, device_id_type=mesh)

    @pl.when(has_north)
    def _():
        pl.semaphore_signal(barrier, 1, device_id={"lat": row + 1}, device_id_type=mesh)

    pl.semaphore_wait(
        barrier, lon - 1 + has_south.astype(jnp.int32) + has_north.astype(jnp.int32)
    )

    def exchange(s, source):
        wsend, esend, ssend, nsend, whalo, ehalo, shalo, nhalo, gathered, wcol, ecol, north = (
            per_stage[s]
        )
        fields = source.shape[0]
        lane = lax.broadcasted_iota(jnp.int32, (height, width), 1)
        for f in range(fields):
            packed = jnp.zeros((height, width), jnp.float32)
            for k in range(levels):
                tile = source[f, k]
                packed = jnp.where(lane == k, tile[:, 0:1], packed)
                packed = jnp.where(lane == 16 + k, tile[:, width - 1 : width], packed)
                ssend[f, pl.ds(k, 1), :] = tile[0:1, :]
                nsend[f, pl.ds(k, 1), :] = tile[height - 1 : height, :]
            flipped = packed.T
            wsend[f] = flipped[0:16, :]
            esend[f] = flipped[16:32, :]

        def fold_copy(peer, slot):
            return pltpu.make_async_remote_copy(
                src_ref=nsend,
                dst_ref=gathered.at[slot],
                send_sem=fold_send.at[s, peer],
                recv_sem=fold_recv.at[s, slot],
                device_id={"lon": peer},
                device_id_type=mesh,
            )

        for peer in range(lon):

            @pl.when(me != peer)
            def _():
                fold_copy(peer, me).start()

        def side(i, src, dst, device):
            return pltpu.make_async_remote_copy(
                src_ref=src,
                dst_ref=dst,
                send_sem=side_send.at[s, i],
                recv_sem=side_recv.at[s, i],
                device_id=device,
                device_id_type=mesh,
            )

        to_west = side(0, wsend, ehalo, {"lon": west})
        to_east = side(1, esend, whalo, {"lon": east})
        to_south = side(2, ssend, nhalo, {"lat": row - 1})
        to_north = side(3, nsend, shalo, {"lat": row + 1})
        to_west.start()
        to_east.start()

        @pl.when(has_south)
        def _():
            to_south.start()

        @pl.when(has_north)
        def _():
            to_north.start()

        gathered[me] = nsend[...]

        for peer in range(lon):

            @pl.when(me != peer)
            def _():
                fold_copy(peer, me).wait_send()
                fold_copy(peer, peer).wait_recv()

        to_west.wait()
        to_east.wait()

        @pl.when(has_south)
        def _():
            to_south.wait_send()
            to_north.wait_recv()

        @pl.when(has_north)
        def _():
            to_north.wait_send()
            to_south.wait_recv()

        @pl.when(jnp.logical_not(has_south))
        def _():
            shalo[...] = jnp.zeros_like(shalo)

        @pl.when(jnp.logical_not(has_north))
        def _():
            nhalo[...] = jnp.zeros_like(nhalo)

        lower, upper = blocks[0], blocks[1]
        for f in range(fields):
            both = jnp.concatenate([whalo[f], ehalo[f]], axis=0).T
            for k in range(levels):
                wcol[f, k] = both[:, k : k + 1]
                ecol[f, k] = both[:, 16 + k : 17 + k]
            ghost = jnp.dot(
                gathered[lower, f],
                reverse[0],
                precision=lax.Precision.HIGHEST,
                preferred_element_type=jnp.float32,
            ) + jnp.dot(
                gathered[upper, f],
                reverse[1],
                precision=lax.Precision.HIGHEST,
                preferred_element_type=jnp.float32,
            )
            sign = signs[f] if s == 0 else 1.0
            north[f] = jnp.where(on_top, ghost * sign, nhalo[f])
        return (source, wcol, ecol, shalo, north)

    state_refs = exchange(0, state)
    upwind_kernel(*state_refs, upwind)
    upwind_refs = exchange(1, upwind)
    ratio_kernel(*state_refs, *upwind_refs, ratio)
    ratio_refs = exchange(2, ratio)
    advected_kernel(*state_refs, upwind, *ratio_refs, advected)
    advected_refs = exchange(3, advected)
    isopycnal_kernel(*advected_refs, *state_refs, Pair(first_out, second_out))


def fused(state, blocks, reverse):
    lon = lax.axis_size("lon")
    lat = lax.axis_size("lat")
    levels, height, width = state.shape[1:]
    block = jax.ShapeDtypeStruct((levels, height, width), jnp.float32)
    scratch = [
        pltpu.VMEM((2, levels, height, width), jnp.float32),
        pltpu.VMEM((4, levels, height, width), jnp.float32),
        pltpu.VMEM((2, levels, height, width), jnp.float32),
    ]
    for fields in STAGE_FIELDS:
        scratch += buffers_for(fields, levels, height, width, lon)
    count = len(STAGE_FIELDS)
    scratch += [
        pltpu.SemaphoreType.DMA((count, lon)),
        pltpu.SemaphoreType.DMA((count, lon)),
        pltpu.SemaphoreType.DMA((count, 4)),
        pltpu.SemaphoreType.DMA((count, 4)),
    ]
    return pl.pallas_call(
        functools.partial(fused_kernel, lon, lat, STATE_SIGNS),
        out_shape=(block, block),
        in_specs=[
            pl.BlockSpec(memory_space=pltpu.SMEM),
            pl.BlockSpec(memory_space=pltpu.VMEM),
            pl.BlockSpec(memory_space=pltpu.VMEM),
        ],
        out_specs=[pl.BlockSpec(memory_space=pltpu.VMEM)] * 2,
        scratch_shapes=scratch,
        compiler_params=pltpu.CompilerParams(
            collective_id=0, has_side_effects=True, vmem_limit_bytes=60 * 1024 * 1024
        ),
    )(blocks, reverse, state)


def local(
    heat_content_field,
    saltiness_field,
    eastward_cfl_number,
    northward_cfl_number,
    seawater_indicator,
    submerged_layer_total,
    seam_partner_index,
):
    span = heat_content_field.shape[2]
    lon = lax.axis_size("lon")
    vertical_layer = jnp.arange(heat_content_field.shape[0], dtype=jnp.int32)[:, None, None]
    submerged_indicator = (
        (seawater_indicator[None] == 1) & (vertical_layer < submerged_layer_total[None])
    ).astype(jnp.float32)
    state = jnp.stack(
        [
            heat_content_field,
            saltiness_field,
            eastward_cfl_number,
            northward_cfl_number,
            submerged_indicator,
        ]
    )
    pivot = seam_partner_index[0]
    pivot_block, pivot_offset = pivot // span, pivot % span
    me = lax.axis_index("lon")
    blocks = jnp.stack([(pivot_block - me - 1) % lon, (pivot_block - me) % lon]).astype(jnp.int32)
    source = lax.broadcasted_iota(jnp.int32, (span, span), 0)
    target = lax.broadcasted_iota(jnp.int32, (span, span), 1)
    reverse = jnp.stack(
        [source == span + pivot_offset - target, source == pivot_offset - target]
    ).astype(jnp.float32)
    return fused(state, blocks, reverse)


def solution(mesh):
    in_specs = (
        P(None, "lat", "lon"),
        P(None, "lat", "lon"),
        P(None, "lat", "lon"),
        P(None, "lat", "lon"),
        P("lat", "lon"),
        P("lat", "lon"),
        P(),
    )
    out_specs = (P(None, "lat", "lon"), P(None, "lat", "lon"))
    return jax.shard_map(local, mesh=mesh, in_specs=in_specs, out_specs=out_specs, check_vma=False)
```

```python
import functools

import jax
import jax.numpy as jnp
from jax import lax
from jax.experimental import pallas as pl
from jax.experimental.pallas import tpu as pltpu
from jax.sharding import PartitionSpec as P

RATIO_FLOOR = 0.05
SLOPE_FLOOR = 0.5
SLOPE_LIMIT = 2.0
DIFFUSIVITY = 0.1
THERMAL_COEF = 0.2
HALINE_COEF = 0.8
STATE_SIGNS = (1.0, 1.0, -1.0, -1.0, 1.0)


def sign_column(values):
    return jnp.array(values, jnp.float32).reshape(len(values), 1, 1, 1)


def around(x, west, east, south, north):
    height, width = x.shape
    lane = lax.broadcasted_iota(jnp.int32, x.shape, 1)
    level = lax.broadcasted_iota(jnp.int32, x.shape, 0)
    at_east = jnp.where(lane == width - 1, east, pltpu.roll(x, width - 1, 1))
    at_west = jnp.where(lane == 0, west, pltpu.roll(x, 1, 1))
    at_north = jnp.where(level == height - 1, north, pltpu.roll(x, height - 1, 0))
    at_south = jnp.where(level == 0, south, pltpu.roll(x, 1, 0))
    return (x, at_east, at_west, at_north, at_south)


def sides_of(refs, f, k):
    block, west, east, south, north = refs
    return around(
        block[f, k], west[f, k], east[f, k], south[f, pl.ds(k, 1), :], north[f, pl.ds(k, 1), :]
    )


def low_order(tracer, zonal, meridional, wet_sides):
    value_centre, value_east, value_west, value_north, value_south = tracer
    speed_centre, speed_west = (zonal[0], zonal[2])
    flow_centre, flow_south = (meridional[0], meridional[4])
    wet_centre, wet_east, wet_west, wet_north, wet_south = wet_sides
    face_east = wet_centre * wet_east
    face_west = wet_west * wet_centre
    face_north = wet_centre * wet_north
    face_south = wet_south * wet_centre
    upwind_east = face_east * (
        jnp.maximum(speed_centre, 0.0) * value_centre + jnp.minimum(speed_centre, 0.0) * value_east
    )
    upwind_west = face_west * (
        jnp.maximum(speed_west, 0.0) * value_west + jnp.minimum(speed_west, 0.0) * value_centre
    )
    upwind_north = face_north * (
        jnp.maximum(flow_centre, 0.0) * value_centre + jnp.minimum(flow_centre, 0.0) * value_north
    )
    upwind_south = face_south * (
        jnp.maximum(flow_south, 0.0) * value_south + jnp.minimum(flow_south, 0.0) * value_centre
    )
    anti_east = face_east * speed_centre * (value_centre + value_east) * 0.5 - upwind_east
    anti_west = face_west * speed_west * (value_west + value_centre) * 0.5 - upwind_west
    anti_north = face_north * flow_centre * (value_centre + value_north) * 0.5 - upwind_north
    anti_south = face_south * flow_south * (value_south + value_centre) * 0.5 - upwind_south
    upwind = value_centre - wet_centre * (upwind_east - upwind_west + upwind_north - upwind_south)
    inflow = (
        jnp.maximum(anti_west, 0.0)
        - jnp.minimum(anti_east, 0.0)
        + jnp.maximum(anti_south, 0.0)
        - jnp.minimum(anti_north, 0.0)
    )
    outflow = (
        jnp.maximum(anti_east, 0.0)
        - jnp.minimum(anti_west, 0.0)
        + jnp.maximum(anti_north, 0.0)
        - jnp.minimum(anti_south, 0.0)
    )
    anti = (anti_east, anti_west, anti_north, anti_south)
    return (upwind, anti, inflow, outflow)


def level_low_order(state_refs, k, tracer):
    zonal = sides_of(state_refs, 2, k)
    meridional = sides_of(state_refs, 3, k)
    wet_sides = sides_of(state_refs, 4, k)
    return low_order(sides_of(state_refs, tracer, k), zonal, meridional, wet_sides), wet_sides


def ratio_pair(upwind_sides, wet_sides, inflow, outflow):
    value_centre = upwind_sides[0]
    candidates = [value_centre] + [
        jnp.where(beside_wet > 0.5, beside, value_centre)
        for beside, beside_wet in zip(upwind_sides[1:], wet_sides[1:])
    ]
    highest = functools.reduce(jnp.maximum, candidates)
    lowest = functools.reduce(jnp.minimum, candidates)
    ratio_plus = jnp.minimum(1.0, (highest - value_centre) / jnp.maximum(inflow, RATIO_FLOOR))
    ratio_minus = jnp.minimum(1.0, (value_centre - lowest) / jnp.maximum(outflow, RATIO_FLOOR))
    return ratio_plus, ratio_minus


def limited(plus, minus, upwind, anti, wet_centre):
    plus_centre, plus_east, plus_west, plus_north, plus_south = plus
    minus_centre, minus_east, minus_west, minus_north, minus_south = minus
    anti_east, anti_west, anti_north, anti_south = anti
    coef_east = jnp.where(
        anti_east >= 0.0, jnp.minimum(plus_east, minus_centre), jnp.minimum(plus_centre, minus_east)
    )
    coef_west = jnp.where(
        anti_west >= 0.0, jnp.minimum(plus_centre, minus_west), jnp.minimum(plus_west, minus_centre)
    )
    coef_north = jnp.where(
        anti_north >= 0.0,
        jnp.minimum(plus_north, minus_centre),
        jnp.minimum(plus_centre, minus_north),
    )
    coef_south = jnp.where(
        anti_south >= 0.0,
        jnp.minimum(plus_centre, minus_south),
        jnp.minimum(plus_south, minus_centre),
    )
    return upwind - wet_centre * (
        coef_east * anti_east
        - coef_west * anti_west
        + coef_north * anti_north
        - coef_south * anti_south
    )


def upwind_kernel(state_refs, out, anti_out, flow_out):
    levels = out.shape[1]

    def body(k, carry):
        for tracer in range(2):
            (upwind, anti, inflow, outflow), _ = level_low_order(state_refs, k, tracer)
            out[tracer, k] = upwind
            for face in range(4):
                anti_out[4 * tracer + face, k] = anti[face]
            flow_out[tracer, k] = inflow
            flow_out[2 + tracer, k] = outflow
        return carry

    lax.fori_loop(0, levels, body, 0)


def ratio_kernel(state_refs, upwind_refs, flow, out):
    levels = out.shape[1]

    def body(k, carry):
        wet_sides = sides_of(state_refs, 4, k)
        for tracer in range(2):
            plus, minus = ratio_pair(
                sides_of(upwind_refs, tracer, k), wet_sides, flow[tracer, k], flow[2 + tracer, k]
            )
            out[tracer, k] = plus
            out[2 + tracer, k] = minus
        return carry

    lax.fori_loop(0, levels, body, 0)


def advected_kernel(wet, upwind_ref, anti_ref, ratio_refs, out):
    levels = out.shape[1]

    def body(k, carry):
        wet_centre = wet[k]
        for tracer in range(2):
            anti = tuple(anti_ref[4 * tracer + face, k] for face in range(4))
            plus = sides_of(ratio_refs, tracer, k)
            minus = sides_of(ratio_refs, 2 + tracer, k)
            out[tracer, k] = limited(plus, minus, upwind_ref[tracer, k], anti, wet_centre)
        return carry

    lax.fori_loop(0, levels, body, 0)


def isopycnal_kernel(*refs):
    advected_refs, state_refs, out = refs[:5], refs[5:10], refs[10]
    levels = out.shape[1]

    def body(k, carry):
        above = jnp.minimum(k + 1, levels - 1)
        values = [sides_of(advected_refs, tracer, k) for tracer in range(2)]
        uppers = [sides_of(advected_refs, tracer, above) for tracer in range(2)]
        wet_sides = sides_of(state_refs, 4, k)
        wet_above = sides_of(state_refs, 4, above)
        stacked = [w * a for w, a in zip(wet_sides, wet_above)]
        verticals = [
            [(u - v) * s for u, v, s in zip(uppers[tracer], values[tracer], stacked)]
            for tracer in range(2)
        ]
        densities = [HALINE_COEF * s - THERMAL_COEF * t for t, s in zip(values[0], values[1])]
        stratas = [HALINE_COEF * s - THERMAL_COEF * t for t, s in zip(verticals[0], verticals[1])]
        for tracer in range(2):
            value, vertical = values[tracer], verticals[tracer]

            def face_flux(first, second):
                face = wet_sides[first] * wet_sides[second]
                slope = jnp.clip(
                    (densities[second] - densities[first])
                    / jnp.maximum(0.5 * (stratas[first] + stratas[second]), SLOPE_FLOOR),
                    -SLOPE_LIMIT,
                    SLOPE_LIMIT,
                )
                return (
                    DIFFUSIVITY
                    * face
                    * (
                        value[second]
                        - value[first]
                        - slope * 0.5 * (vertical[first] + vertical[second])
                    )
                )

            east_flux = face_flux(0, 1)
            west_flux = face_flux(2, 0)
            north_flux = face_flux(0, 3)
            south_flux = face_flux(4, 0)
            out[tracer, k] = value[0] + wet_sides[0] * (
                east_flux - west_flux + north_flux - south_flux
            )
        return carry

    lax.fori_loop(0, levels, body, 0)


class Stack:
    def __init__(self, *refs):
        self.refs = refs
        self.shape = (len(refs),) + refs[0].shape

    def __getitem__(self, index):
        return self.refs[index[0]][index[1:]]


class Pair:
    def __init__(self, first, second):
        self.refs = (first, second)
        self.shape = (2,) + first.shape

    def __setitem__(self, index, value):
        self.refs[index[0]][index[1]] = value


def buffers_for(fields, levels, height, width, lon):
    columns = pltpu.VMEM((fields, 16, height), jnp.float32)
    rows = pltpu.VMEM((fields, levels, width), jnp.float32)
    halo = pltpu.VMEM((fields, levels, height, 1), jnp.float32)
    return [
        columns,
        columns,
        rows,
        rows,
        columns,
        columns,
        rows,
        rows,
        pltpu.VMEM((lon, fields, levels, width), jnp.float32),
        halo,
        halo,
        rows,
    ]


STAGE_FIELDS = (5, 2, 4, 2)


def fused_kernel(
    lon, lat, signs, seam, heat, salt, zonal, meridional, sea, depth, first_out, second_out, *scratch
):
    mesh = pl.DeviceIdType.MESH
    upwind, ratio, advected, anti, flow, wet = scratch[:6]
    count = len(STAGE_FIELDS)
    per_stage = [scratch[6 + 12 * s : 18 + 12 * s] for s in range(count)]
    fold_send, fold_recv, side_send, side_recv = scratch[6 + 12 * count :]
    me = lax.axis_index("lon")
    row = lax.axis_index("lat")
    west = lax.rem(me + lon - 1, lon)
    east = lax.rem(me + 1, lon)
    has_south = row > 0
    has_north = row < lat - 1
    on_top = row == lat - 1
    levels, height, width = heat.shape
    wet_column = sea[...] == 1
    for k in range(levels):
        wet[k] = jnp.where(wet_column & (k < depth[...]), 1.0, 0.0).astype(jnp.float32)
    state = Stack(heat, salt, zonal, meridional, wet)
    pivot = seam[0]
    pivot_block, pivot_offset = pivot // width, pivot % width
    lower = lax.rem(pivot_block - me - 1 + 2 * lon, lon)
    upper = lax.rem(pivot_block - me + 2 * lon, lon)
    source_lane = lax.broadcasted_iota(jnp.int32, (width, width), 0)
    target_lane = lax.broadcasted_iota(jnp.int32, (width, width), 1)
    reverse = (
        jnp.where(source_lane == width + pivot_offset - target_lane, 1.0, 0.0).astype(jnp.float32),
        jnp.where(source_lane == pivot_offset - target_lane, 1.0, 0.0).astype(jnp.float32),
    )

    barrier = pltpu.get_barrier_semaphore()
    for peer in range(lon):

        @pl.when(me != peer)
        def _():
            pl.semaphore_signal(barrier, 1, device_id={"lon": peer}, device_id_type=mesh)

    @pl.when(has_south)
    def _():
        pl.semaphore_signal(barrier, 1, device_id={"lat": row - 1}, device_id_type=mesh)

    @pl.when(has_north)
    def _():
        pl.semaphore_signal(barrier, 1, device_id={"lat": row + 1}, device_id_type=mesh)

    pl.semaphore_wait(
        barrier, lon - 1 + has_south.astype(jnp.int32) + has_north.astype(jnp.int32)
    )

    def exchange(s, source):
        wsend, esend, ssend, nsend, whalo, ehalo, shalo, nhalo, gathered, wcol, ecol, north = (
            per_stage[s]
        )
        fields = source.shape[0]
        lane = lax.broadcasted_iota(jnp.int32, (height, width), 1)
        for f in range(fields):
            packed = jnp.zeros((height, width), jnp.float32)
            for k in range(levels):
                tile = source[f, k]
                packed = jnp.where(lane == k, tile[:, 0:1], packed)
                packed = jnp.where(lane == 16 + k, tile[:, width - 1 : width], packed)
                ssend[f, pl.ds(k, 1), :] = tile[0:1, :]
                nsend[f, pl.ds(k, 1), :] = tile[height - 1 : height, :]
            flipped = packed.T
            wsend[f] = flipped[0:16, :]
            esend[f] = flipped[16:32, :]

        def fold_copy(peer, slot):
            return pltpu.make_async_remote_copy(
                src_ref=nsend,
                dst_ref=gathered.at[slot],
                send_sem=fold_send.at[s, peer],
                recv_sem=fold_recv.at[s, slot],
                device_id={"lon": peer},
                device_id_type=mesh,
            )

        for peer in range(lon):

            @pl.when(me != peer)
            def _():
                fold_copy(peer, me).start()

        def side(i, src, dst, device):
            return pltpu.make_async_remote_copy(
                src_ref=src,
                dst_ref=dst,
                send_sem=side_send.at[s, i],
                recv_sem=side_recv.at[s, i],
                device_id=device,
                device_id_type=mesh,
            )

        to_west = side(0, wsend, ehalo, {"lon": west})
        to_east = side(1, esend, whalo, {"lon": east})
        to_south = side(2, ssend, nhalo, {"lat": row - 1})
        to_north = side(3, nsend, shalo, {"lat": row + 1})
        to_west.start()
        to_east.start()

        @pl.when(has_south)
        def _():
            to_south.start()

        @pl.when(has_north)
        def _():
            to_north.start()

        gathered[me] = nsend[...]

        for peer in range(lon):

            @pl.when(me != peer)
            def _():
                fold_copy(peer, me).wait_send()
                fold_copy(peer, peer).wait_recv()

        to_west.wait()
        to_east.wait()

        @pl.when(has_south)
        def _():
            to_south.wait_send()
            to_north.wait_recv()

        @pl.when(has_north)
        def _():
            to_north.wait_send()
            to_south.wait_recv()

        @pl.when(jnp.logical_not(has_south))
        def _():
            shalo[...] = jnp.zeros_like(shalo)

        @pl.when(jnp.logical_not(has_north))
        def _():
            nhalo[...] = jnp.zeros_like(nhalo)

        for f in range(fields):
            both = jnp.concatenate([whalo[f], ehalo[f]], axis=0).T
            for k in range(levels):
                wcol[f, k] = both[:, k : k + 1]
                ecol[f, k] = both[:, 16 + k : 17 + k]
            ghost = jnp.dot(
                gathered[lower, f],
                reverse[0],
                precision=lax.Precision.HIGHEST,
                preferred_element_type=jnp.float32,
            ) + jnp.dot(
                gathered[upper, f],
                reverse[1],
                precision=lax.Precision.HIGHEST,
                preferred_element_type=jnp.float32,
            )
            sign = signs[f] if s == 0 else 1.0
            north[f] = jnp.where(on_top, ghost * sign, nhalo[f])
        return (source, wcol, ecol, shalo, north)

    state_refs = exchange(0, state)
    upwind_kernel(state_refs, upwind, anti, flow)
    upwind_refs = exchange(1, upwind)
    ratio_kernel(state_refs, upwind_refs, flow, ratio)
    ratio_refs = exchange(2, ratio)
    advected_kernel(wet, upwind, anti, ratio_refs, advected)
    advected_refs = exchange(3, advected)
    isopycnal_kernel(*advected_refs, *state_refs, Pair(first_out, second_out))


def fused(fields, seam):
    lon = lax.axis_size("lon")
    lat = lax.axis_size("lat")
    levels, height, width = fields[0].shape
    block = jax.ShapeDtypeStruct((levels, height, width), jnp.float32)
    scratch = [
        pltpu.VMEM((2, levels, height, width), jnp.float32),
        pltpu.VMEM((4, levels, height, width), jnp.float32),
        pltpu.VMEM((2, levels, height, width), jnp.float32),
        pltpu.VMEM((8, levels, height, width), jnp.float32),
        pltpu.VMEM((4, levels, height, width), jnp.float32),
        pltpu.VMEM((levels, height, width), jnp.float32),
    ]
    for count in STAGE_FIELDS:
        scratch += buffers_for(count, levels, height, width, lon)
    stages = len(STAGE_FIELDS)
    scratch += [
        pltpu.SemaphoreType.DMA((stages, lon)),
        pltpu.SemaphoreType.DMA((stages, lon)),
        pltpu.SemaphoreType.DMA((stages, 4)),
        pltpu.SemaphoreType.DMA((stages, 4)),
    ]
    return pl.pallas_call(
        functools.partial(fused_kernel, lon, lat, STATE_SIGNS),
        out_shape=(block, block),
        in_specs=[pl.BlockSpec(memory_space=pltpu.SMEM)]
        + [pl.BlockSpec(memory_space=pltpu.VMEM)] * len(fields),
        out_specs=[pl.BlockSpec(memory_space=pltpu.VMEM)] * 2,
        scratch_shapes=scratch,
        compiler_params=pltpu.CompilerParams(
            collective_id=0, has_side_effects=True, vmem_limit_bytes=60 * 1024 * 1024
        ),
    )(seam, *fields)


def local(
    heat_content_field,
    saltiness_field,
    eastward_cfl_number,
    northward_cfl_number,
    seawater_indicator,
    submerged_layer_total,
    seam_partner_index,
):
    return fused(
        (
            heat_content_field,
            saltiness_field,
            eastward_cfl_number,
            northward_cfl_number,
            seawater_indicator,
            submerged_layer_total,
        ),
        seam_partner_index,
    )


def solution(mesh):
    in_specs = (
        P(None, "lat", "lon"),
        P(None, "lat", "lon"),
        P(None, "lat", "lon"),
        P(None, "lat", "lon"),
        P("lat", "lon"),
        P("lat", "lon"),
        P(),
    )
    out_specs = (P(None, "lat", "lon"), P(None, "lat", "lon"))
    return jax.shard_map(local, mesh=mesh, in_specs=in_specs, out_specs=out_specs, check_vma=False)
```

```python
import functools

import jax
import jax.numpy as jnp
from jax import lax
from jax.experimental import pallas as pl
from jax.experimental.pallas import tpu as pltpu
from jax.sharding import PartitionSpec as P

RATIO_FLOOR = 0.05
SLOPE_FLOOR = 0.5
SLOPE_LIMIT = 2.0
DIFFUSIVITY = 0.1
THERMAL_COEF = 0.2
HALINE_COEF = 0.8
STATE_SIGNS = (1.0, 1.0, -1.0, -1.0, 1.0)


def sign_column(values):
    return jnp.array(values, jnp.float32).reshape(len(values), 1, 1, 1)


def around(x, west, east, south, north):
    height, width = x.shape
    lane = lax.broadcasted_iota(jnp.int32, x.shape, 1)
    level = lax.broadcasted_iota(jnp.int32, x.shape, 0)
    at_east = jnp.where(lane == width - 1, east, pltpu.roll(x, width - 1, 1))
    at_west = jnp.where(lane == 0, west, pltpu.roll(x, 1, 1))
    at_north = jnp.where(level == height - 1, north, pltpu.roll(x, height - 1, 0))
    at_south = jnp.where(level == 0, south, pltpu.roll(x, 1, 0))
    return (x, at_east, at_west, at_north, at_south)


def sides_of(refs, f, k):
    block, west, east, south, north = refs
    return around(
        block[f, k], west[f, k], east[f, k], south[f, pl.ds(k, 1), :], north[f, pl.ds(k, 1), :]
    )


def low_order(tracer, zonal, meridional, wet_sides):
    value_centre, value_east, value_west, value_north, value_south = tracer
    speed_centre, speed_west = (zonal[0], zonal[2])
    flow_centre, flow_south = (meridional[0], meridional[4])
    wet_centre, wet_east, wet_west, wet_north, wet_south = wet_sides
    face_east = wet_centre * wet_east
    face_west = wet_west * wet_centre
    face_north = wet_centre * wet_north
    face_south = wet_south * wet_centre
    upwind_east = face_east * (
        jnp.maximum(speed_centre, 0.0) * value_centre + jnp.minimum(speed_centre, 0.0) * value_east
    )
    upwind_west = face_west * (
        jnp.maximum(speed_west, 0.0) * value_west + jnp.minimum(speed_west, 0.0) * value_centre
    )
    upwind_north = face_north * (
        jnp.maximum(flow_centre, 0.0) * value_centre + jnp.minimum(flow_centre, 0.0) * value_north
    )
    upwind_south = face_south * (
        jnp.maximum(flow_south, 0.0) * value_south + jnp.minimum(flow_south, 0.0) * value_centre
    )
    anti_east = face_east * speed_centre * (value_centre + value_east) * 0.5 - upwind_east
    anti_west = face_west * speed_west * (value_west + value_centre) * 0.5 - upwind_west
    anti_north = face_north * flow_centre * (value_centre + value_north) * 0.5 - upwind_north
    anti_south = face_south * flow_south * (value_south + value_centre) * 0.5 - upwind_south
    upwind = value_centre - wet_centre * (upwind_east - upwind_west + upwind_north - upwind_south)
    inflow = (
        jnp.maximum(anti_west, 0.0)
        - jnp.minimum(anti_east, 0.0)
        + jnp.maximum(anti_south, 0.0)
        - jnp.minimum(anti_north, 0.0)
    )
    outflow = (
        jnp.maximum(anti_east, 0.0)
        - jnp.minimum(anti_west, 0.0)
        + jnp.maximum(anti_north, 0.0)
        - jnp.minimum(anti_south, 0.0)
    )
    anti = (anti_east, anti_west, anti_north, anti_south)
    return (upwind, anti, inflow, outflow)


def level_low_order(state_refs, k, tracer):
    zonal = sides_of(state_refs, 2, k)
    meridional = sides_of(state_refs, 3, k)
    wet_sides = sides_of(state_refs, 4, k)
    return low_order(sides_of(state_refs, tracer, k), zonal, meridional, wet_sides), wet_sides


def ratio_pair(upwind_sides, wet_sides, inflow, outflow):
    value_centre = upwind_sides[0]
    candidates = [value_centre] + [
        jnp.where(beside_wet > 0.5, beside, value_centre)
        for beside, beside_wet in zip(upwind_sides[1:], wet_sides[1:])
    ]
    highest = functools.reduce(jnp.maximum, candidates)
    lowest = functools.reduce(jnp.minimum, candidates)
    ratio_plus = jnp.minimum(1.0, (highest - value_centre) / jnp.maximum(inflow, RATIO_FLOOR))
    ratio_minus = jnp.minimum(1.0, (value_centre - lowest) / jnp.maximum(outflow, RATIO_FLOOR))
    return ratio_plus, ratio_minus


def limited(plus, minus, upwind, anti, wet_centre):
    plus_centre, plus_east, plus_west, plus_north, plus_south = plus
    minus_centre, minus_east, minus_west, minus_north, minus_south = minus
    anti_east, anti_west, anti_north, anti_south = anti
    coef_east = jnp.where(
        anti_east >= 0.0, jnp.minimum(plus_east, minus_centre), jnp.minimum(plus_centre, minus_east)
    )
    coef_west = jnp.where(
        anti_west >= 0.0, jnp.minimum(plus_centre, minus_west), jnp.minimum(plus_west, minus_centre)
    )
    coef_north = jnp.where(
        anti_north >= 0.0,
        jnp.minimum(plus_north, minus_centre),
        jnp.minimum(plus_centre, minus_north),
    )
    coef_south = jnp.where(
        anti_south >= 0.0,
        jnp.minimum(plus_centre, minus_south),
        jnp.minimum(plus_south, minus_centre),
    )
    return upwind - wet_centre * (
        coef_east * anti_east
        - coef_west * anti_west
        + coef_north * anti_north
        - coef_south * anti_south
    )


def upwind_kernel(state_refs, out, anti_out, flow_out):
    levels = out.shape[1]

    def body(k, carry):
        zonal = sides_of(state_refs, 2, k)
        meridional = sides_of(state_refs, 3, k)
        wet_sides = sides_of(state_refs, 4, k)
        for tracer in range(2):
            tracer_sides = sides_of(state_refs, tracer, k)
            upwind, anti, inflow, outflow = low_order(tracer_sides, zonal, meridional, wet_sides)
            out[tracer, k] = upwind
            for face in range(4):
                anti_out[4 * tracer + face, k] = anti[face]
            flow_out[tracer, k] = inflow
            flow_out[2 + tracer, k] = outflow
        return carry

    lax.fori_loop(0, levels, body, 0)


def ratio_kernel(state_refs, upwind_refs, flow, out):
    levels = out.shape[1]

    def body(k, carry):
        wet_sides = sides_of(state_refs, 4, k)
        for tracer in range(2):
            plus, minus = ratio_pair(
                sides_of(upwind_refs, tracer, k), wet_sides, flow[tracer, k], flow[2 + tracer, k]
            )
            out[tracer, k] = plus
            out[2 + tracer, k] = minus
        return carry

    lax.fori_loop(0, levels, body, 0)


def advected_kernel(wet, upwind_ref, anti_ref, ratio_refs, out):
    levels = out.shape[1]

    def body(k, carry):
        wet_centre = wet[k]
        for tracer in range(2):
            anti = tuple(anti_ref[4 * tracer + face, k] for face in range(4))
            plus = sides_of(ratio_refs, tracer, k)
            minus = sides_of(ratio_refs, 2 + tracer, k)
            out[tracer, k] = limited(plus, minus, upwind_ref[tracer, k], anti, wet_centre)
        return carry

    lax.fori_loop(0, levels, body, 0)


def isopycnal_kernel(*refs):
    advected_refs, state_refs, out = refs[:5], refs[5:10], refs[10]
    levels = out.shape[1]

    def body(k, carry):
        above = jnp.minimum(k + 1, levels - 1)
        values = [sides_of(advected_refs, tracer, k) for tracer in range(2)]
        uppers = [sides_of(advected_refs, tracer, above) for tracer in range(2)]
        wet_sides = sides_of(state_refs, 4, k)
        wet_above = sides_of(state_refs, 4, above)
        stacked = [w * a for w, a in zip(wet_sides, wet_above)]
        verticals = [
            [(u - v) * s for u, v, s in zip(uppers[tracer], values[tracer], stacked)]
            for tracer in range(2)
        ]
        densities = [HALINE_COEF * s - THERMAL_COEF * t for t, s in zip(values[0], values[1])]
        stratas = [HALINE_COEF * s - THERMAL_COEF * t for t, s in zip(verticals[0], verticals[1])]
        for tracer in range(2):
            value, vertical = values[tracer], verticals[tracer]

            def face_flux(first, second):
                face = wet_sides[first] * wet_sides[second]
                slope = jnp.clip(
                    (densities[second] - densities[first])
                    / jnp.maximum(0.5 * (stratas[first] + stratas[second]), SLOPE_FLOOR),
                    -SLOPE_LIMIT,
                    SLOPE_LIMIT,
                )
                return (
                    DIFFUSIVITY
                    * face
                    * (
                        value[second]
                        - value[first]
                        - slope * 0.5 * (vertical[first] + vertical[second])
                    )
                )

            east_flux = face_flux(0, 1)
            west_flux = face_flux(2, 0)
            north_flux = face_flux(0, 3)
            south_flux = face_flux(4, 0)
            out[tracer, k] = value[0] + wet_sides[0] * (
                east_flux - west_flux + north_flux - south_flux
            )
        return carry

    lax.fori_loop(0, levels, body, 0)


class Stack:
    def __init__(self, *refs):
        self.refs = refs
        self.shape = (len(refs),) + refs[0].shape

    def __getitem__(self, index):
        return self.refs[index[0]][index[1:]]


class Pair:
    def __init__(self, first, second):
        self.refs = (first, second)
        self.shape = (2,) + first.shape

    def __setitem__(self, index, value):
        self.refs[index[0]][index[1]] = value


def buffers_for(fields, levels, height, width, lon):
    columns = pltpu.VMEM((fields, 16, height), jnp.float32)
    rows = pltpu.VMEM((fields, levels, width), jnp.float32)
    halo = pltpu.VMEM((fields, levels, height, 1), jnp.float32)
    return [
        columns,
        columns,
        rows,
        rows,
        columns,
        columns,
        rows,
        rows,
        pltpu.VMEM((lon, fields, levels, width), jnp.float32),
        halo,
        halo,
        rows,
    ]


STAGE_FIELDS = (5, 2, 4, 2)


def fused_kernel(
    lon, lat, signs, seam, heat, salt, zonal, meridional, sea, depth, first_out, second_out, *scratch
):
    mesh = pl.DeviceIdType.MESH
    upwind, ratio, advected, anti, flow, wet = scratch[:6]
    count = len(STAGE_FIELDS)
    per_stage = [scratch[6 + 12 * s : 18 + 12 * s] for s in range(count)]
    fold_send, fold_recv, side_send, side_recv = scratch[6 + 12 * count :]
    me = lax.axis_index("lon")
    row = lax.axis_index("lat")
    west = lax.rem(me + lon - 1, lon)
    east = lax.rem(me + 1, lon)
    has_south = row > 0
    has_north = row < lat - 1
    on_top = row == lat - 1
    levels, height, width = heat.shape
    wet_column = sea[...] == 1
    for k in range(levels):
        wet[k] = jnp.where(wet_column & (k < depth[...]), 1.0, 0.0).astype(jnp.float32)
    state = Stack(heat, salt, zonal, meridional, wet)
    pivot = seam[0]
    pivot_block, pivot_offset = pivot // width, pivot % width
    lower = lax.rem(pivot_block - me - 1 + 2 * lon, lon)
    upper = lax.rem(pivot_block - me + 2 * lon, lon)
    source_lane = lax.broadcasted_iota(jnp.int32, (width, width), 0)
    target_lane = lax.broadcasted_iota(jnp.int32, (width, width), 1)
    reverse = (
        jnp.where(source_lane == width + pivot_offset - target_lane, 1.0, 0.0).astype(jnp.float32),
        jnp.where(source_lane == pivot_offset - target_lane, 1.0, 0.0).astype(jnp.float32),
    )

    barrier = pltpu.get_barrier_semaphore()
    for peer in range(lon):

        @pl.when((me != peer) & (on_top | (peer == west) | (peer == east)))
        def _():
            pl.semaphore_signal(barrier, 1, device_id={"lon": peer}, device_id_type=mesh)

    @pl.when(has_south)
    def _():
        pl.semaphore_signal(barrier, 1, device_id={"lat": row - 1}, device_id_type=mesh)

    @pl.when(has_north)
    def _():
        pl.semaphore_signal(barrier, 1, device_id={"lat": row + 1}, device_id_type=mesh)

    beside = 1 if lon == 2 else 2
    pl.semaphore_wait(
        barrier,
        jnp.where(on_top, lon - 1, beside)
        + has_south.astype(jnp.int32)
        + has_north.astype(jnp.int32),
    )

    def exchange(s, source):
        wsend, esend, ssend, nsend, whalo, ehalo, shalo, nhalo, gathered, wcol, ecol, north = (
            per_stage[s]
        )
        fields = source.shape[0]
        lane = lax.broadcasted_iota(jnp.int32, (height, width), 1)
        for f in range(fields):
            packed = jnp.zeros((height, width), jnp.float32)
            for k in range(levels):
                tile = source[f, k]
                packed = jnp.where(lane == k, tile[:, 0:1], packed)
                packed = jnp.where(lane == 16 + k, tile[:, width - 1 : width], packed)
                ssend[f, pl.ds(k, 1), :] = tile[0:1, :]
                nsend[f, pl.ds(k, 1), :] = tile[height - 1 : height, :]
            flipped = packed.T
            wsend[f] = flipped[0:16, :]
            esend[f] = flipped[16:32, :]

        def fold_copy(peer, slot):
            return pltpu.make_async_remote_copy(
                src_ref=nsend,
                dst_ref=gathered.at[slot],
                send_sem=fold_send.at[s, peer],
                recv_sem=fold_recv.at[s, slot],
                device_id={"lon": peer},
                device_id_type=mesh,
            )

        def side(i, src, dst, device):
            return pltpu.make_async_remote_copy(
                src_ref=src,
                dst_ref=dst,
                send_sem=side_send.at[s, i],
                recv_sem=side_recv.at[s, i],
                device_id=device,
                device_id_type=mesh,
            )

        to_west = side(0, wsend, ehalo, {"lon": west})
        to_east = side(1, esend, whalo, {"lon": east})
        to_south = side(2, ssend, nhalo, {"lat": row - 1})
        to_north = side(3, nsend, shalo, {"lat": row + 1})
        to_west.start()
        to_east.start()

        @pl.when(has_south)
        def _():
            to_south.start()

        @pl.when(has_north)
        def _():
            to_north.start()

        for peer in range(lon):

            @pl.when((me != peer) & on_top)
            def _():
                fold_copy(peer, me).start()

        @pl.when(on_top)
        def _():
            gathered[me] = nsend[...]

        for peer in range(lon):

            @pl.when((me != peer) & on_top)
            def _():
                fold_copy(peer, me).wait_send()
                fold_copy(peer, peer).wait_recv()

        to_west.wait()
        to_east.wait()

        @pl.when(has_south)
        def _():
            to_south.wait_send()
            to_north.wait_recv()

        @pl.when(has_north)
        def _():
            to_north.wait_send()
            to_south.wait_recv()

        @pl.when(jnp.logical_not(has_south))
        def _():
            shalo[...] = jnp.zeros_like(shalo)

        @pl.when(jnp.logical_not(has_north))
        def _():
            nhalo[...] = jnp.zeros_like(nhalo)

        for f in range(fields):
            both = jnp.concatenate([whalo[f], ehalo[f]], axis=0).T
            for k in range(levels):
                wcol[f, k] = both[:, k : k + 1]
                ecol[f, k] = both[:, 16 + k : 17 + k]
            sign = signs[f] if s == 0 else 1.0

            @pl.when(on_top)
            def _():
                ghost = jnp.dot(
                    gathered[lower, f],
                    reverse[0],
                    precision=lax.Precision.HIGHEST,
                    preferred_element_type=jnp.float32,
                ) + jnp.dot(
                    gathered[upper, f],
                    reverse[1],
                    precision=lax.Precision.HIGHEST,
                    preferred_element_type=jnp.float32,
                )
                north[f] = ghost * sign

            @pl.when(jnp.logical_not(on_top))
            def _():
                north[f] = nhalo[f]
        return (source, wcol, ecol, shalo, north)

    state_refs = exchange(0, state)
    upwind_kernel(state_refs, upwind, anti, flow)
    upwind_refs = exchange(1, upwind)
    ratio_kernel(state_refs, upwind_refs, flow, ratio)
    ratio_refs = exchange(2, ratio)
    advected_kernel(wet, upwind, anti, ratio_refs, advected)
    advected_refs = exchange(3, advected)
    isopycnal_kernel(*advected_refs, *state_refs, Pair(first_out, second_out))


def fused(fields, seam):
    lon = lax.axis_size("lon")
    lat = lax.axis_size("lat")
    levels, height, width = fields[0].shape
    block = jax.ShapeDtypeStruct((levels, height, width), jnp.float32)
    scratch = [
        pltpu.VMEM((2, levels, height, width), jnp.float32),
        pltpu.VMEM((4, levels, height, width), jnp.float32),
        pltpu.VMEM((2, levels, height, width), jnp.float32),
        pltpu.VMEM((8, levels, height, width), jnp.float32),
        pltpu.VMEM((4, levels, height, width), jnp.float32),
        pltpu.VMEM((levels, height, width), jnp.float32),
    ]
    for count in STAGE_FIELDS:
        scratch += buffers_for(count, levels, height, width, lon)
    stages = len(STAGE_FIELDS)
    scratch += [
        pltpu.SemaphoreType.DMA((stages, lon)),
        pltpu.SemaphoreType.DMA((stages, lon)),
        pltpu.SemaphoreType.DMA((stages, 4)),
        pltpu.SemaphoreType.DMA((stages, 4)),
    ]
    return pl.pallas_call(
        functools.partial(fused_kernel, lon, lat, STATE_SIGNS),
        out_shape=(block, block),
        in_specs=[pl.BlockSpec(memory_space=pltpu.SMEM)]
        + [pl.BlockSpec(memory_space=pltpu.VMEM)] * len(fields),
        out_specs=[pl.BlockSpec(memory_space=pltpu.VMEM)] * 2,
        scratch_shapes=scratch,
        compiler_params=pltpu.CompilerParams(
            collective_id=0, has_side_effects=True, vmem_limit_bytes=60 * 1024 * 1024
        ),
    )(seam, *fields)


def local(
    heat_content_field,
    saltiness_field,
    eastward_cfl_number,
    northward_cfl_number,
    seawater_indicator,
    submerged_layer_total,
    seam_partner_index,
):
    return fused(
        (
            heat_content_field,
            saltiness_field,
            eastward_cfl_number,
            northward_cfl_number,
            seawater_indicator,
            submerged_layer_total,
        ),
        seam_partner_index,
    )


def solution(mesh):
    in_specs = (
        P(None, "lat", "lon"),
        P(None, "lat", "lon"),
        P(None, "lat", "lon"),
        P(None, "lat", "lon"),
        P("lat", "lon"),
        P("lat", "lon"),
        P(),
    )
    out_specs = (P(None, "lat", "lon"), P(None, "lat", "lon"))
    return jax.shard_map(local, mesh=mesh, in_specs=in_specs, out_specs=out_specs, check_vma=False)
```

```python
import functools

import jax
import jax.numpy as jnp
from jax import lax
from jax.experimental import pallas as pl
from jax.experimental.pallas import tpu as pltpu
from jax.sharding import PartitionSpec as P

RATIO_FLOOR = 0.05
SLOPE_FLOOR = 0.5
SLOPE_LIMIT = 2.0
DIFFUSIVITY = 0.1
THERMAL_COEF = 0.2
HALINE_COEF = 0.8
STATE_SIGNS = (1.0, 1.0, -1.0, -1.0, 1.0)


def sign_column(values):
    return jnp.array(values, jnp.float32).reshape(len(values), 1, 1, 1)


def around(x, west, east, south, north):
    height, width = x.shape
    lane = lax.broadcasted_iota(jnp.int32, x.shape, 1)
    level = lax.broadcasted_iota(jnp.int32, x.shape, 0)
    at_east = jnp.where(lane == width - 1, east, pltpu.roll(x, width - 1, 1))
    at_west = jnp.where(lane == 0, west, pltpu.roll(x, 1, 1))
    at_north = jnp.where(level == height - 1, north, pltpu.roll(x, height - 1, 0))
    at_south = jnp.where(level == 0, south, pltpu.roll(x, 1, 0))
    return (x, at_east, at_west, at_north, at_south)


def around_top(pair, west, east, north):
    x = pair[1:2]
    width = x.shape[1]
    lane = lax.broadcasted_iota(jnp.int32, x.shape, 1)
    at_east = jnp.where(lane == width - 1, east, pltpu.roll(x, width - 1, 1))
    at_west = jnp.where(lane == 0, west, pltpu.roll(x, 1, 1))
    return (x, at_east, at_west, north, pair[0:1])


def sides_of(refs, f, k, top=False):
    block, west, east, south, north = refs
    if top:
        height = west.shape[2]
        return around_top(
            block[f, k, pl.ds(height - 2, 2), :],
            west[f, k, pl.ds(height - 1, 1), :],
            east[f, k, pl.ds(height - 1, 1), :],
            north[f, pl.ds(k, 1), :],
        )
    return around(
        block[f, k], west[f, k], east[f, k], south[f, pl.ds(k, 1), :], north[f, pl.ds(k, 1), :]
    )


def tail_of(shape, top):
    return (pl.ds(shape[-2] - 1, 1), slice(None)) if top else ()


def low_order(tracer, zonal, meridional, wet_sides):
    value_centre, value_east, value_west, value_north, value_south = tracer
    speed_centre, speed_west = (zonal[0], zonal[2])
    flow_centre, flow_south = (meridional[0], meridional[4])
    wet_centre, wet_east, wet_west, wet_north, wet_south = wet_sides
    face_east = wet_centre * wet_east
    face_west = wet_west * wet_centre
    face_north = wet_centre * wet_north
    face_south = wet_south * wet_centre
    upwind_east = face_east * (
        jnp.maximum(speed_centre, 0.0) * value_centre + jnp.minimum(speed_centre, 0.0) * value_east
    )
    upwind_west = face_west * (
        jnp.maximum(speed_west, 0.0) * value_west + jnp.minimum(speed_west, 0.0) * value_centre
    )
    upwind_north = face_north * (
        jnp.maximum(flow_centre, 0.0) * value_centre + jnp.minimum(flow_centre, 0.0) * value_north
    )
    upwind_south = face_south * (
        jnp.maximum(flow_south, 0.0) * value_south + jnp.minimum(flow_south, 0.0) * value_centre
    )
    anti_east = face_east * speed_centre * (value_centre + value_east) * 0.5 - upwind_east
    anti_west = face_west * speed_west * (value_west + value_centre) * 0.5 - upwind_west
    anti_north = face_north * flow_centre * (value_centre + value_north) * 0.5 - upwind_north
    anti_south = face_south * flow_south * (value_south + value_centre) * 0.5 - upwind_south
    upwind = value_centre - wet_centre * (upwind_east - upwind_west + upwind_north - upwind_south)
    inflow = (
        jnp.maximum(anti_west, 0.0)
        - jnp.minimum(anti_east, 0.0)
        + jnp.maximum(anti_south, 0.0)
        - jnp.minimum(anti_north, 0.0)
    )
    outflow = (
        jnp.maximum(anti_east, 0.0)
        - jnp.minimum(anti_west, 0.0)
        + jnp.maximum(anti_north, 0.0)
        - jnp.minimum(anti_south, 0.0)
    )
    anti = (anti_east, anti_west, anti_north, anti_south)
    return (upwind, anti, inflow, outflow)


def level_low_order(state_refs, k, tracer):
    zonal = sides_of(state_refs, 2, k)
    meridional = sides_of(state_refs, 3, k)
    wet_sides = sides_of(state_refs, 4, k)
    return low_order(sides_of(state_refs, tracer, k), zonal, meridional, wet_sides), wet_sides


def ratio_pair(upwind_sides, wet_sides, inflow, outflow):
    value_centre = upwind_sides[0]
    candidates = [value_centre] + [
        jnp.where(beside_wet > 0.5, beside, value_centre)
        for beside, beside_wet in zip(upwind_sides[1:], wet_sides[1:])
    ]
    highest = functools.reduce(jnp.maximum, candidates)
    lowest = functools.reduce(jnp.minimum, candidates)
    ratio_plus = jnp.minimum(1.0, (highest - value_centre) / jnp.maximum(inflow, RATIO_FLOOR))
    ratio_minus = jnp.minimum(1.0, (value_centre - lowest) / jnp.maximum(outflow, RATIO_FLOOR))
    return ratio_plus, ratio_minus


def limited(plus, minus, upwind, anti, wet_centre):
    plus_centre, plus_east, plus_west, plus_north, plus_south = plus
    minus_centre, minus_east, minus_west, minus_north, minus_south = minus
    anti_east, anti_west, anti_north, anti_south = anti
    coef_east = jnp.where(
        anti_east >= 0.0, jnp.minimum(plus_east, minus_centre), jnp.minimum(plus_centre, minus_east)
    )
    coef_west = jnp.where(
        anti_west >= 0.0, jnp.minimum(plus_centre, minus_west), jnp.minimum(plus_west, minus_centre)
    )
    coef_north = jnp.where(
        anti_north >= 0.0,
        jnp.minimum(plus_north, minus_centre),
        jnp.minimum(plus_centre, minus_north),
    )
    coef_south = jnp.where(
        anti_south >= 0.0,
        jnp.minimum(plus_centre, minus_south),
        jnp.minimum(plus_south, minus_centre),
    )
    return upwind - wet_centre * (
        coef_east * anti_east
        - coef_west * anti_west
        + coef_north * anti_north
        - coef_south * anti_south
    )


def upwind_kernel(state_refs, out, anti_out, flow_out, top=False):
    levels = out.shape[1]
    tail = tail_of(out.shape, top)

    def body(k, carry):
        zonal = sides_of(state_refs, 2, k, top)
        meridional = sides_of(state_refs, 3, k, top)
        wet_sides = sides_of(state_refs, 4, k, top)
        for tracer in range(2):
            tracer_sides = sides_of(state_refs, tracer, k, top)
            upwind, anti, inflow, outflow = low_order(tracer_sides, zonal, meridional, wet_sides)
            out[(tracer, k) + tail] = upwind
            for face in range(4):
                anti_out[(4 * tracer + face, k) + tail] = anti[face]
            flow_out[(tracer, k) + tail] = inflow
            flow_out[(2 + tracer, k) + tail] = outflow
        return carry

    lax.fori_loop(0, levels, body, 0)


def ratio_kernel(state_refs, upwind_refs, flow, out, top=False):
    levels = out.shape[1]
    tail = tail_of(out.shape, top)

    def body(k, carry):
        wet_sides = sides_of(state_refs, 4, k, top)
        for tracer in range(2):
            plus, minus = ratio_pair(
                sides_of(upwind_refs, tracer, k, top),
                wet_sides,
                flow[(tracer, k) + tail],
                flow[(2 + tracer, k) + tail],
            )
            out[(tracer, k) + tail] = plus
            out[(2 + tracer, k) + tail] = minus
        return carry

    lax.fori_loop(0, levels, body, 0)


def advected_kernel(wet, upwind_ref, anti_ref, ratio_refs, out, top=False):
    levels = out.shape[1]
    tail = tail_of(out.shape, top)

    def body(k, carry):
        wet_centre = wet[(k,) + tail]
        for tracer in range(2):
            anti = tuple(anti_ref[(4 * tracer + face, k) + tail] for face in range(4))
            plus = sides_of(ratio_refs, tracer, k, top)
            minus = sides_of(ratio_refs, 2 + tracer, k, top)
            out[(tracer, k) + tail] = limited(
                plus, minus, upwind_ref[(tracer, k) + tail], anti, wet_centre
            )
        return carry

    lax.fori_loop(0, levels, body, 0)


def isopycnal_kernel(advected_refs, state_refs, out, top=False):
    levels = out.shape[1]
    tail = tail_of(out.shape, top)

    def body(k, carry):
        above = jnp.minimum(k + 1, levels - 1)
        values = [sides_of(advected_refs, tracer, k, top) for tracer in range(2)]
        uppers = [sides_of(advected_refs, tracer, above, top) for tracer in range(2)]
        wet_sides = sides_of(state_refs, 4, k, top)
        wet_above = sides_of(state_refs, 4, above, top)
        stacked = [w * a for w, a in zip(wet_sides, wet_above)]
        verticals = [
            [(u - v) * s for u, v, s in zip(uppers[tracer], values[tracer], stacked)]
            for tracer in range(2)
        ]
        densities = [HALINE_COEF * s - THERMAL_COEF * t for t, s in zip(values[0], values[1])]
        stratas = [HALINE_COEF * s - THERMAL_COEF * t for t, s in zip(verticals[0], verticals[1])]
        for tracer in range(2):
            value, vertical = values[tracer], verticals[tracer]

            def face_flux(first, second):
                face = wet_sides[first] * wet_sides[second]
                slope = jnp.clip(
                    (densities[second] - densities[first])
                    / jnp.maximum(0.5 * (stratas[first] + stratas[second]), SLOPE_FLOOR),
                    -SLOPE_LIMIT,
                    SLOPE_LIMIT,
                )
                return (
                    DIFFUSIVITY
                    * face
                    * (
                        value[second]
                        - value[first]
                        - slope * 0.5 * (vertical[first] + vertical[second])
                    )
                )

            east_flux = face_flux(0, 1)
            west_flux = face_flux(2, 0)
            north_flux = face_flux(0, 3)
            south_flux = face_flux(4, 0)
            out[(tracer, k) + tail] = value[0] + wet_sides[0] * (
                east_flux - west_flux + north_flux - south_flux
            )
        return carry

    lax.fori_loop(0, levels, body, 0)


class Stack:
    def __init__(self, *refs):
        self.refs = refs
        self.shape = (len(refs),) + refs[0].shape

    def __getitem__(self, index):
        return self.refs[index[0]][index[1:]]


class Pair:
    def __init__(self, first, second):
        self.refs = (first, second)
        self.shape = (2,) + first.shape

    def __setitem__(self, index, value):
        self.refs[index[0]][index[1:]] = value


def buffers_for(fields, levels, height, width, lon):
    columns = pltpu.VMEM((fields, 16, height), jnp.float32)
    rows = pltpu.VMEM((fields, levels, width), jnp.float32)
    halo = pltpu.VMEM((fields, levels, height, 1), jnp.float32)
    return [
        columns,
        columns,
        rows,
        rows,
        columns,
        columns,
        rows,
        rows,
        pltpu.VMEM((lon, fields, levels, width), jnp.float32),
        halo,
        halo,
        rows,
    ]


STAGE_FIELDS = (5, 2, 4, 2)


def fused_kernel(
    lon, lat, signs, seam, heat, salt, zonal, meridional, sea, depth, first_out, second_out, *scratch
):
    mesh = pl.DeviceIdType.MESH
    upwind, ratio, advected, anti, flow, wet = scratch[:6]
    count = len(STAGE_FIELDS)
    per_stage = [scratch[6 + 12 * s : 18 + 12 * s] for s in range(count)]
    fold_send, fold_recv, side_send, side_recv = scratch[6 + 12 * count :]
    me = lax.axis_index("lon")
    row = lax.axis_index("lat")
    west = lax.rem(me + lon - 1, lon)
    east = lax.rem(me + 1, lon)
    has_south = row > 0
    has_north = row < lat - 1
    on_top = row == lat - 1
    levels, height, width = heat.shape
    wet_column = sea[...] == 1
    for k in range(levels):
        wet[k] = jnp.where(wet_column & (k < depth[...]), 1.0, 0.0).astype(jnp.float32)
    state = Stack(heat, salt, zonal, meridional, wet)
    pivot = seam[0]
    pivot_block, pivot_offset = pivot // width, pivot % width
    lower = lax.rem(pivot_block - me - 1 + 2 * lon, lon)
    upper = lax.rem(pivot_block - me + 2 * lon, lon)
    source_lane = lax.broadcasted_iota(jnp.int32, (width, width), 0)
    target_lane = lax.broadcasted_iota(jnp.int32, (width, width), 1)
    reverse = (
        jnp.where(source_lane == width + pivot_offset - target_lane, 1.0, 0.0).astype(jnp.float32),
        jnp.where(source_lane == pivot_offset - target_lane, 1.0, 0.0).astype(jnp.float32),
    )

    barrier = pltpu.get_barrier_semaphore()
    for peer in range(lon):

        @pl.when((me != peer) & (on_top | (peer == west) | (peer == east)))
        def _():
            pl.semaphore_signal(barrier, 1, device_id={"lon": peer}, device_id_type=mesh)

    @pl.when(has_south)
    def _():
        pl.semaphore_signal(barrier, 1, device_id={"lat": row - 1}, device_id_type=mesh)

    @pl.when(has_north)
    def _():
        pl.semaphore_signal(barrier, 1, device_id={"lat": row + 1}, device_id_type=mesh)

    beside = 1 if lon == 2 else 2
    pl.semaphore_wait(
        barrier,
        jnp.where(on_top, lon - 1, beside)
        + has_south.astype(jnp.int32)
        + has_north.astype(jnp.int32),
    )

    def exchange(s, source):
        wsend, esend, ssend, nsend, whalo, ehalo, shalo, nhalo, gathered, wcol, ecol, north = (
            per_stage[s]
        )
        fields = source.shape[0]
        lane = lax.broadcasted_iota(jnp.int32, (height, width), 1)
        for f in range(fields):
            packed = jnp.zeros((height, width), jnp.float32)
            for k in range(levels):
                tile = source[f, k]
                packed = jnp.where(lane == k, tile[:, 0:1], packed)
                packed = jnp.where(lane == 16 + k, tile[:, width - 1 : width], packed)
                ssend[f, pl.ds(k, 1), :] = tile[0:1, :]
                nsend[f, pl.ds(k, 1), :] = tile[height - 1 : height, :]
            flipped = packed.T
            wsend[f] = flipped[0:16, :]
            esend[f] = flipped[16:32, :]

        def fold_copy(peer, slot):
            return pltpu.make_async_remote_copy(
                src_ref=nsend,
                dst_ref=gathered.at[slot],
                send_sem=fold_send.at[s, peer],
                recv_sem=fold_recv.at[s, slot],
                device_id={"lon": peer},
                device_id_type=mesh,
            )

        def side(i, src, dst, device):
            return pltpu.make_async_remote_copy(
                src_ref=src,
                dst_ref=dst,
                send_sem=side_send.at[s, i],
                recv_sem=side_recv.at[s, i],
                device_id=device,
                device_id_type=mesh,
            )

        to_west = side(0, wsend, ehalo, {"lon": west})
        to_east = side(1, esend, whalo, {"lon": east})
        to_south = side(2, ssend, nhalo, {"lat": row - 1})
        to_north = side(3, nsend, shalo, {"lat": row + 1})
        to_west.start()
        to_east.start()

        @pl.when(has_south)
        def _():
            to_south.start()

        @pl.when(has_north)
        def _():
            to_north.start()

        for peer in range(lon):

            @pl.when((me != peer) & on_top)
            def _():
                fold_copy(peer, me).start()

        @pl.when(on_top)
        def _():
            gathered[me] = nsend[...]

        to_west.wait()
        to_east.wait()

        @pl.when(has_south)
        def _():
            to_south.wait_send()
            to_north.wait_recv()

        @pl.when(has_north)
        def _():
            to_north.wait_send()
            to_south.wait_recv()

        @pl.when(jnp.logical_not(has_south))
        def _():
            shalo[...] = jnp.zeros_like(shalo)

        @pl.when(jnp.logical_not(has_north))
        def _():
            nhalo[...] = jnp.zeros_like(nhalo)

        for f in range(fields):
            both = jnp.concatenate([whalo[f], ehalo[f]], axis=0).T
            for k in range(levels):
                wcol[f, k] = both[:, k : k + 1]
                ecol[f, k] = both[:, 16 + k : 17 + k]
            north[f] = nhalo[f]

        def finish():
            for peer in range(lon):

                @pl.when((me != peer) & on_top)
                def _():
                    fold_copy(peer, me).wait_send()
                    fold_copy(peer, peer).wait_recv()

            @pl.when(on_top)
            def _():
                for f in range(fields):
                    ghost = jnp.dot(
                        gathered[lower, f],
                        reverse[0],
                        precision=lax.Precision.HIGHEST,
                        preferred_element_type=jnp.float32,
                    ) + jnp.dot(
                        gathered[upper, f],
                        reverse[1],
                        precision=lax.Precision.HIGHEST,
                        preferred_element_type=jnp.float32,
                    )
                    north[f] = ghost * (signs[f] if s == 0 else 1.0)

        return (source, wcol, ecol, shalo, north), finish

    def run(stage, finish):
        stage(False)
        finish()
        pl.when(on_top)(lambda: stage(True))

    state_refs, finish = exchange(0, state)
    run(lambda top: upwind_kernel(state_refs, upwind, anti, flow, top), finish)
    upwind_refs, finish = exchange(1, upwind)
    run(lambda top: ratio_kernel(state_refs, upwind_refs, flow, ratio, top), finish)
    ratio_refs, finish = exchange(2, ratio)
    run(lambda top: advected_kernel(wet, upwind, anti, ratio_refs, advected, top), finish)
    advected_refs, finish = exchange(3, advected)
    final = Pair(first_out, second_out)
    run(lambda top: isopycnal_kernel(advected_refs, state_refs, final, top), finish)


def fused(fields, seam):
    lon = lax.axis_size("lon")
    lat = lax.axis_size("lat")
    levels, height, width = fields[0].shape
    block = jax.ShapeDtypeStruct((levels, height, width), jnp.float32)
    scratch = [
        pltpu.VMEM((2, levels, height, width), jnp.float32),
        pltpu.VMEM((4, levels, height, width), jnp.float32),
        pltpu.VMEM((2, levels, height, width), jnp.float32),
        pltpu.VMEM((8, levels, height, width), jnp.float32),
        pltpu.VMEM((4, levels, height, width), jnp.float32),
        pltpu.VMEM((levels, height, width), jnp.float32),
    ]
    for count in STAGE_FIELDS:
        scratch += buffers_for(count, levels, height, width, lon)
    stages = len(STAGE_FIELDS)
    scratch += [
        pltpu.SemaphoreType.DMA((stages, lon)),
        pltpu.SemaphoreType.DMA((stages, lon)),
        pltpu.SemaphoreType.DMA((stages, 4)),
        pltpu.SemaphoreType.DMA((stages, 4)),
    ]
    return pl.pallas_call(
        functools.partial(fused_kernel, lon, lat, STATE_SIGNS),
        out_shape=(block, block),
        in_specs=[pl.BlockSpec(memory_space=pltpu.SMEM)]
        + [pl.BlockSpec(memory_space=pltpu.VMEM)] * len(fields),
        out_specs=[pl.BlockSpec(memory_space=pltpu.VMEM)] * 2,
        scratch_shapes=scratch,
        compiler_params=pltpu.CompilerParams(
            collective_id=0, has_side_effects=True, vmem_limit_bytes=60 * 1024 * 1024
        ),
    )(seam, *fields)


def local(
    heat_content_field,
    saltiness_field,
    eastward_cfl_number,
    northward_cfl_number,
    seawater_indicator,
    submerged_layer_total,
    seam_partner_index,
):
    return fused(
        (
            heat_content_field,
            saltiness_field,
            eastward_cfl_number,
            northward_cfl_number,
            seawater_indicator,
            submerged_layer_total,
        ),
        seam_partner_index,
    )


def solution(mesh):
    in_specs = (
        P(None, "lat", "lon"),
        P(None, "lat", "lon"),
        P(None, "lat", "lon"),
        P(None, "lat", "lon"),
        P("lat", "lon"),
        P("lat", "lon"),
        P(),
    )
    out_specs = (P(None, "lat", "lon"), P(None, "lat", "lon"))
    return jax.shard_map(local, mesh=mesh, in_specs=in_specs, out_specs=out_specs, check_vma=False)
```

```python
import functools

import jax
import jax.numpy as jnp
from jax import lax
from jax.experimental import pallas as pl
from jax.experimental.pallas import tpu as pltpu
from jax.sharding import PartitionSpec as P

RATIO_FLOOR = 0.05
SLOPE_FLOOR = 0.5
SLOPE_LIMIT = 2.0
DIFFUSIVITY = 0.1
THERMAL_COEF = 0.2
HALINE_COEF = 0.8
STATE_SIGNS = (1.0, 1.0, -1.0, -1.0, 1.0)


def sign_column(values):
    return jnp.array(values, jnp.float32).reshape(len(values), 1, 1, 1)


def around(x, west, east, south, north):
    height, width = x.shape
    lane = lax.broadcasted_iota(jnp.int32, x.shape, 1)
    level = lax.broadcasted_iota(jnp.int32, x.shape, 0)
    at_east = jnp.where(lane == width - 1, east, pltpu.roll(x, width - 1, 1))
    at_west = jnp.where(lane == 0, west, pltpu.roll(x, 1, 1))
    at_north = jnp.where(level == height - 1, north, pltpu.roll(x, height - 1, 0))
    at_south = jnp.where(level == 0, south, pltpu.roll(x, 1, 0))
    return (x, at_east, at_west, at_north, at_south)


def pick_rows(low, high):
    level = lax.broadcasted_iota(jnp.int32, (2, high.shape[-1]), 0)
    return jnp.where(level == 0, low, high)


def load_view(ref, index, rows):
    if not rows:
        return ref[index]
    height = ref.shape[-2]
    return pick_rows(
        ref[index + (pl.ds(0, 1), slice(None))], ref[index + (pl.ds(height - 1, 1), slice(None))]
    )


def store_view(ref, index, value, rows):
    if not rows:
        ref[index] = value
        return
    height = ref.shape[-2]
    ref[index + (pl.ds(0, 1), slice(None))] = value[0:1]
    ref[index + (pl.ds(height - 1, 1), slice(None))] = value[1:2]


def sides_of(refs, f, k, rows=False):
    block, west, east, south, north = refs
    if not rows:
        return around(
            block[f, k], west[f, k], east[f, k], south[f, pl.ds(k, 1), :], north[f, pl.ds(k, 1), :]
        )
    height = west.shape[2]
    low = block[f, k, pl.ds(0, 2), :]
    high = block[f, k, pl.ds(height - 2, 2), :]
    centre = pick_rows(low[0:1], high[1:2])
    at_north = pick_rows(low[1:2], north[f, pl.ds(k, 1), :])
    at_south = pick_rows(south[f, pl.ds(k, 1), :], high[0:1])
    west_end = pick_rows(west[f, k, pl.ds(0, 1), :], west[f, k, pl.ds(height - 1, 1), :])
    east_end = pick_rows(east[f, k, pl.ds(0, 1), :], east[f, k, pl.ds(height - 1, 1), :])
    width = centre.shape[1]
    lane = lax.broadcasted_iota(jnp.int32, centre.shape, 1)
    at_east = jnp.where(lane == width - 1, east_end, pltpu.roll(centre, width - 1, 1))
    at_west = jnp.where(lane == 0, west_end, pltpu.roll(centre, 1, 1))
    return (centre, at_east, at_west, at_north, at_south)


def low_order(tracer, zonal, meridional, wet_sides):
    value_centre, value_east, value_west, value_north, value_south = tracer
    speed_centre, speed_west = (zonal[0], zonal[2])
    flow_centre, flow_south = (meridional[0], meridional[4])
    wet_centre, wet_east, wet_west, wet_north, wet_south = wet_sides
    face_east = wet_centre * wet_east
    face_west = wet_west * wet_centre
    face_north = wet_centre * wet_north
    face_south = wet_south * wet_centre
    upwind_east = face_east * (
        jnp.maximum(speed_centre, 0.0) * value_centre + jnp.minimum(speed_centre, 0.0) * value_east
    )
    upwind_west = face_west * (
        jnp.maximum(speed_west, 0.0) * value_west + jnp.minimum(speed_west, 0.0) * value_centre
    )
    upwind_north = face_north * (
        jnp.maximum(flow_centre, 0.0) * value_centre + jnp.minimum(flow_centre, 0.0) * value_north
    )
    upwind_south = face_south * (
        jnp.maximum(flow_south, 0.0) * value_south + jnp.minimum(flow_south, 0.0) * value_centre
    )
    anti_east = face_east * speed_centre * (value_centre + value_east) * 0.5 - upwind_east
    anti_west = face_west * speed_west * (value_west + value_centre) * 0.5 - upwind_west
    anti_north = face_north * flow_centre * (value_centre + value_north) * 0.5 - upwind_north
    anti_south = face_south * flow_south * (value_south + value_centre) * 0.5 - upwind_south
    upwind = value_centre - wet_centre * (upwind_east - upwind_west + upwind_north - upwind_south)
    inflow = (
        jnp.maximum(anti_west, 0.0)
        - jnp.minimum(anti_east, 0.0)
        + jnp.maximum(anti_south, 0.0)
        - jnp.minimum(anti_north, 0.0)
    )
    outflow = (
        jnp.maximum(anti_east, 0.0)
        - jnp.minimum(anti_west, 0.0)
        + jnp.maximum(anti_north, 0.0)
        - jnp.minimum(anti_south, 0.0)
    )
    anti = (anti_east, anti_west, anti_north, anti_south)
    return (upwind, anti, inflow, outflow)


def level_low_order(state_refs, k, tracer):
    zonal = sides_of(state_refs, 2, k)
    meridional = sides_of(state_refs, 3, k)
    wet_sides = sides_of(state_refs, 4, k)
    return low_order(sides_of(state_refs, tracer, k), zonal, meridional, wet_sides), wet_sides


def ratio_pair(upwind_sides, wet_sides, inflow, outflow):
    value_centre = upwind_sides[0]
    candidates = [value_centre] + [
        jnp.where(beside_wet > 0.5, beside, value_centre)
        for beside, beside_wet in zip(upwind_sides[1:], wet_sides[1:])
    ]
    highest = functools.reduce(jnp.maximum, candidates)
    lowest = functools.reduce(jnp.minimum, candidates)
    ratio_plus = jnp.minimum(1.0, (highest - value_centre) / jnp.maximum(inflow, RATIO_FLOOR))
    ratio_minus = jnp.minimum(1.0, (value_centre - lowest) / jnp.maximum(outflow, RATIO_FLOOR))
    return ratio_plus, ratio_minus


def limited(plus, minus, upwind, anti, wet_centre):
    plus_centre, plus_east, plus_west, plus_north, plus_south = plus
    minus_centre, minus_east, minus_west, minus_north, minus_south = minus
    anti_east, anti_west, anti_north, anti_south = anti
    coef_east = jnp.where(
        anti_east >= 0.0, jnp.minimum(plus_east, minus_centre), jnp.minimum(plus_centre, minus_east)
    )
    coef_west = jnp.where(
        anti_west >= 0.0, jnp.minimum(plus_centre, minus_west), jnp.minimum(plus_west, minus_centre)
    )
    coef_north = jnp.where(
        anti_north >= 0.0,
        jnp.minimum(plus_north, minus_centre),
        jnp.minimum(plus_centre, minus_north),
    )
    coef_south = jnp.where(
        anti_south >= 0.0,
        jnp.minimum(plus_centre, minus_south),
        jnp.minimum(plus_south, minus_centre),
    )
    return upwind - wet_centre * (
        coef_east * anti_east
        - coef_west * anti_west
        + coef_north * anti_north
        - coef_south * anti_south
    )


def upwind_kernel(state_refs, out, anti_out, flow_out, rows=False):
    levels = out.shape[1]

    def body(k, carry):
        zonal = sides_of(state_refs, 2, k, rows)
        meridional = sides_of(state_refs, 3, k, rows)
        wet_sides = sides_of(state_refs, 4, k, rows)
        for tracer in range(2):
            tracer_sides = sides_of(state_refs, tracer, k, rows)
            upwind, anti, inflow, outflow = low_order(tracer_sides, zonal, meridional, wet_sides)
            store_view(out, (tracer, k), upwind, rows)
            for face in range(4):
                store_view(anti_out, (4 * tracer + face, k), anti[face], rows)
            store_view(flow_out, (tracer, k), inflow, rows)
            store_view(flow_out, (2 + tracer, k), outflow, rows)
        return carry

    lax.fori_loop(0, levels, body, 0)


def ratio_kernel(state_refs, upwind_refs, flow, out, rows=False):
    levels = out.shape[1]

    def body(k, carry):
        wet_sides = sides_of(state_refs, 4, k, rows)
        for tracer in range(2):
            plus, minus = ratio_pair(
                sides_of(upwind_refs, tracer, k, rows),
                wet_sides,
                load_view(flow, (tracer, k), rows),
                load_view(flow, (2 + tracer, k), rows),
            )
            store_view(out, (tracer, k), plus, rows)
            store_view(out, (2 + tracer, k), minus, rows)
        return carry

    lax.fori_loop(0, levels, body, 0)


def advected_kernel(wet, upwind_ref, anti_ref, ratio_refs, out, rows=False):
    levels = out.shape[1]

    def body(k, carry):
        wet_centre = load_view(wet, (k,), rows)
        for tracer in range(2):
            anti = tuple(load_view(anti_ref, (4 * tracer + face, k), rows) for face in range(4))
            plus = sides_of(ratio_refs, tracer, k, rows)
            minus = sides_of(ratio_refs, 2 + tracer, k, rows)
            upwind = load_view(upwind_ref, (tracer, k), rows)
            store_view(out, (tracer, k), limited(plus, minus, upwind, anti, wet_centre), rows)
        return carry

    lax.fori_loop(0, levels, body, 0)


def isopycnal_kernel(advected_refs, state_refs, out, rows=False):
    levels = out.shape[1]

    def body(k, carry):
        above = jnp.minimum(k + 1, levels - 1)
        values = [sides_of(advected_refs, tracer, k, rows) for tracer in range(2)]
        uppers = [sides_of(advected_refs, tracer, above, rows) for tracer in range(2)]
        wet_sides = sides_of(state_refs, 4, k, rows)
        wet_above = sides_of(state_refs, 4, above, rows)
        stacked = [w * a for w, a in zip(wet_sides, wet_above)]
        verticals = [
            [(u - v) * s for u, v, s in zip(uppers[tracer], values[tracer], stacked)]
            for tracer in range(2)
        ]
        densities = [HALINE_COEF * s - THERMAL_COEF * t for t, s in zip(values[0], values[1])]
        stratas = [HALINE_COEF * s - THERMAL_COEF * t for t, s in zip(verticals[0], verticals[1])]
        for tracer in range(2):
            value, vertical = values[tracer], verticals[tracer]

            def face_flux(first, second):
                face = wet_sides[first] * wet_sides[second]
                slope = jnp.clip(
                    (densities[second] - densities[first])
                    / jnp.maximum(0.5 * (stratas[first] + stratas[second]), SLOPE_FLOOR),
                    -SLOPE_LIMIT,
                    SLOPE_LIMIT,
                )
                return (
                    DIFFUSIVITY
                    * face
                    * (
                        value[second]
                        - value[first]
                        - slope * 0.5 * (vertical[first] + vertical[second])
                    )
                )

            east_flux = face_flux(0, 1)
            west_flux = face_flux(2, 0)
            north_flux = face_flux(0, 3)
            south_flux = face_flux(4, 0)
            result = value[0] + wet_sides[0] * (east_flux - west_flux + north_flux - south_flux)
            store_view(out, (tracer, k), result, rows)
        return carry

    lax.fori_loop(0, levels, body, 0)


class Stack:
    def __init__(self, *refs):
        self.refs = refs
        self.shape = (len(refs),) + refs[0].shape

    def __getitem__(self, index):
        return self.refs[index[0]][index[1:]]


class Pair:
    def __init__(self, first, second):
        self.refs = (first, second)
        self.shape = (2,) + first.shape

    def __setitem__(self, index, value):
        self.refs[index[0]][index[1:]] = value


def buffers_for(fields, levels, height, width, lon):
    columns = pltpu.VMEM((fields, 16, height), jnp.float32)
    rows = pltpu.VMEM((fields, levels, width), jnp.float32)
    halo = pltpu.VMEM((fields, levels, height, 1), jnp.float32)
    return [
        columns,
        columns,
        rows,
        rows,
        columns,
        columns,
        rows,
        rows,
        pltpu.VMEM((lon, fields, levels, width), jnp.float32),
        halo,
        halo,
        rows,
    ]


STAGE_FIELDS = (5, 2, 4, 2)


def fused_kernel(
    lon, lat, signs, seam, heat, salt, zonal, meridional, sea, depth, first_out, second_out, *scratch
):
    mesh = pl.DeviceIdType.MESH
    upwind, ratio, advected, anti, flow, wet = scratch[:6]
    count = len(STAGE_FIELDS)
    per_stage = [scratch[6 + 12 * s : 18 + 12 * s] for s in range(count)]
    fold_send, fold_recv, side_send, side_recv = scratch[6 + 12 * count :]
    me = lax.axis_index("lon")
    row = lax.axis_index("lat")
    west = lax.rem(me + lon - 1, lon)
    east = lax.rem(me + 1, lon)
    has_south = row > 0
    has_north = row < lat - 1
    on_top = row == lat - 1
    levels, height, width = heat.shape
    wet_column = sea[...] == 1
    for k in range(levels):
        wet[k] = jnp.where(wet_column & (k < depth[...]), 1.0, 0.0).astype(jnp.float32)
    state = Stack(heat, salt, zonal, meridional, wet)
    pivot = seam[0]
    pivot_block, pivot_offset = pivot // width, pivot % width
    lower = lax.rem(pivot_block - me - 1 + 2 * lon, lon)
    upper = lax.rem(pivot_block - me + 2 * lon, lon)
    source_lane = lax.broadcasted_iota(jnp.int32, (width, width), 0)
    target_lane = lax.broadcasted_iota(jnp.int32, (width, width), 1)
    reverse = (
        jnp.where(source_lane == width + pivot_offset - target_lane, 1.0, 0.0).astype(jnp.float32),
        jnp.where(source_lane == pivot_offset - target_lane, 1.0, 0.0).astype(jnp.float32),
    )

    barrier = pltpu.get_barrier_semaphore()
    for peer in range(lon):

        @pl.when((me != peer) & (on_top | (peer == west) | (peer == east)))
        def _():
            pl.semaphore_signal(barrier, 1, device_id={"lon": peer}, device_id_type=mesh)

    @pl.when(has_south)
    def _():
        pl.semaphore_signal(barrier, 1, device_id={"lat": row - 1}, device_id_type=mesh)

    @pl.when(has_north)
    def _():
        pl.semaphore_signal(barrier, 1, device_id={"lat": row + 1}, device_id_type=mesh)

    beside = 1 if lon == 2 else 2
    pl.semaphore_wait(
        barrier,
        jnp.where(on_top, lon - 1, beside)
        + has_south.astype(jnp.int32)
        + has_north.astype(jnp.int32),
    )

    def exchange(s, source):
        wsend, esend, ssend, nsend, whalo, ehalo, shalo, nhalo, gathered, wcol, ecol, north = (
            per_stage[s]
        )
        fields = source.shape[0]
        lane = lax.broadcasted_iota(jnp.int32, (height, width), 1)
        for f in range(fields):
            packed = jnp.zeros((height, width), jnp.float32)
            for k in range(levels):
                tile = source[f, k]
                packed = jnp.where(lane == k, tile[:, 0:1], packed)
                packed = jnp.where(lane == 16 + k, tile[:, width - 1 : width], packed)
                ssend[f, pl.ds(k, 1), :] = tile[0:1, :]
                nsend[f, pl.ds(k, 1), :] = tile[height - 1 : height, :]
            flipped = packed.T
            wsend[f] = flipped[0:16, :]
            esend[f] = flipped[16:32, :]

        def fold_copy(peer, slot):
            return pltpu.make_async_remote_copy(
                src_ref=nsend,
                dst_ref=gathered.at[slot],
                send_sem=fold_send.at[s, peer],
                recv_sem=fold_recv.at[s, slot],
                device_id={"lon": peer},
                device_id_type=mesh,
            )

        def side(i, src, dst, device):
            return pltpu.make_async_remote_copy(
                src_ref=src,
                dst_ref=dst,
                send_sem=side_send.at[s, i],
                recv_sem=side_recv.at[s, i],
                device_id=device,
                device_id_type=mesh,
            )

        to_west = side(0, wsend, ehalo, {"lon": west})
        to_east = side(1, esend, whalo, {"lon": east})
        to_south = side(2, ssend, nhalo, {"lat": row - 1})
        to_north = side(3, nsend, shalo, {"lat": row + 1})
        to_west.start()
        to_east.start()

        @pl.when(has_south)
        def _():
            to_south.start()

        @pl.when(has_north)
        def _():
            to_north.start()

        for peer in range(lon):

            @pl.when((me != peer) & on_top)
            def _():
                fold_copy(peer, me).start()

        @pl.when(on_top)
        def _():
            gathered[me] = nsend[...]

        to_west.wait()
        to_east.wait()

        for f in range(fields):
            both = jnp.concatenate([whalo[f], ehalo[f]], axis=0).T
            for k in range(levels):
                wcol[f, k] = both[:, k : k + 1]
                ecol[f, k] = both[:, 16 + k : 17 + k]

        def finish():
            @pl.when(has_south)
            def _():
                to_south.wait_send()
                to_north.wait_recv()

            @pl.when(has_north)
            def _():
                to_north.wait_send()
                to_south.wait_recv()

            @pl.when(jnp.logical_not(has_south))
            def _():
                shalo[...] = jnp.zeros_like(shalo)

            @pl.when(jnp.logical_not(has_north))
            def _():
                nhalo[...] = jnp.zeros_like(nhalo)

            @pl.when(jnp.logical_not(on_top))
            def _():
                north[...] = nhalo[...]

            for peer in range(lon):

                @pl.when((me != peer) & on_top)
                def _():
                    fold_copy(peer, me).wait_send()
                    fold_copy(peer, peer).wait_recv()

            @pl.when(on_top)
            def _():
                for f in range(fields):
                    ghost = jnp.dot(
                        gathered[lower, f],
                        reverse[0],
                        precision=lax.Precision.HIGHEST,
                        preferred_element_type=jnp.float32,
                    ) + jnp.dot(
                        gathered[upper, f],
                        reverse[1],
                        precision=lax.Precision.HIGHEST,
                        preferred_element_type=jnp.float32,
                    )
                    north[f] = ghost * (signs[f] if s == 0 else 1.0)

        return (source, wcol, ecol, ssend, nsend), (source, wcol, ecol, shalo, north), finish

    def run(stage, finish):
        stage(False)
        finish()
        stage(True)

    state_early, state_refs, finish = exchange(0, state)
    run(
        lambda rows: upwind_kernel(state_refs if rows else state_early, upwind, anti, flow, rows),
        finish,
    )
    upwind_early, upwind_refs, finish = exchange(1, upwind)
    run(
        lambda rows: ratio_kernel(
            state_refs, upwind_refs if rows else upwind_early, flow, ratio, rows
        ),
        finish,
    )
    ratio_early, ratio_refs, finish = exchange(2, ratio)
    run(
        lambda rows: advected_kernel(
            wet, upwind, anti, ratio_refs if rows else ratio_early, advected, rows
        ),
        finish,
    )
    advected_early, advected_refs, finish = exchange(3, advected)
    final = Pair(first_out, second_out)
    run(
        lambda rows: isopycnal_kernel(
            advected_refs if rows else advected_early, state_refs, final, rows
        ),
        finish,
    )


def fused(fields, seam):
    lon = lax.axis_size("lon")
    lat = lax.axis_size("lat")
    levels, height, width = fields[0].shape
    block = jax.ShapeDtypeStruct((levels, height, width), jnp.float32)
    scratch = [
        pltpu.VMEM((2, levels, height, width), jnp.float32),
        pltpu.VMEM((4, levels, height, width), jnp.float32),
        pltpu.VMEM((2, levels, height, width), jnp.float32),
        pltpu.VMEM((8, levels, height, width), jnp.float32),
        pltpu.VMEM((4, levels, height, width), jnp.float32),
        pltpu.VMEM((levels, height, width), jnp.float32),
    ]
    for count in STAGE_FIELDS:
        scratch += buffers_for(count, levels, height, width, lon)
    stages = len(STAGE_FIELDS)
    scratch += [
        pltpu.SemaphoreType.DMA((stages, lon)),
        pltpu.SemaphoreType.DMA((stages, lon)),
        pltpu.SemaphoreType.DMA((stages, 4)),
        pltpu.SemaphoreType.DMA((stages, 4)),
    ]
    return pl.pallas_call(
        functools.partial(fused_kernel, lon, lat, STATE_SIGNS),
        out_shape=(block, block),
        in_specs=[pl.BlockSpec(memory_space=pltpu.SMEM)]
        + [pl.BlockSpec(memory_space=pltpu.VMEM)] * len(fields),
        out_specs=[pl.BlockSpec(memory_space=pltpu.VMEM)] * 2,
        scratch_shapes=scratch,
        compiler_params=pltpu.CompilerParams(
            collective_id=0, has_side_effects=True, vmem_limit_bytes=60 * 1024 * 1024
        ),
    )(seam, *fields)


def local(
    heat_content_field,
    saltiness_field,
    eastward_cfl_number,
    northward_cfl_number,
    seawater_indicator,
    submerged_layer_total,
    seam_partner_index,
):
    return fused(
        (
            heat_content_field,
            saltiness_field,
            eastward_cfl_number,
            northward_cfl_number,
            seawater_indicator,
            submerged_layer_total,
        ),
        seam_partner_index,
    )


def solution(mesh):
    in_specs = (
        P(None, "lat", "lon"),
        P(None, "lat", "lon"),
        P(None, "lat", "lon"),
        P(None, "lat", "lon"),
        P("lat", "lon"),
        P("lat", "lon"),
        P(),
    )
    out_specs = (P(None, "lat", "lon"), P(None, "lat", "lon"))
    return jax.shard_map(local, mesh=mesh, in_specs=in_specs, out_specs=out_specs, check_vma=False)
```

```python
import functools

import jax
import jax.numpy as jnp
from jax import lax
from jax.experimental import pallas as pl
from jax.experimental.pallas import tpu as pltpu
from jax.sharding import PartitionSpec as P

RATIO_FLOOR = 0.05
SLOPE_FLOOR = 0.5
SLOPE_LIMIT = 2.0
DIFFUSIVITY = 0.1
THERMAL_COEF = 0.2
HALINE_COEF = 0.8
STATE_SIGNS = (1.0, 1.0, -1.0, -1.0, 1.0)


def sign_column(values):
    return jnp.array(values, jnp.float32).reshape(len(values), 1, 1, 1)


def around(x, west, east, south, north):
    height, width = x.shape
    lane = lax.broadcasted_iota(jnp.int32, x.shape, 1)
    level = lax.broadcasted_iota(jnp.int32, x.shape, 0)
    at_east = jnp.where(lane == width - 1, east, pltpu.roll(x, width - 1, 1))
    at_west = jnp.where(lane == 0, west, pltpu.roll(x, 1, 1))
    at_north = jnp.where(level == height - 1, north, pltpu.roll(x, height - 1, 0))
    at_south = jnp.where(level == 0, south, pltpu.roll(x, 1, 0))
    return (x, at_east, at_west, at_north, at_south)


def pick_rows(low, high):
    level = lax.broadcasted_iota(jnp.int32, (2, high.shape[-1]), 0)
    return jnp.where(level == 0, low, high)


def load_view(ref, index, rows):
    if not rows:
        return ref[index]
    height = ref.shape[-2]
    return pick_rows(
        ref[index + (pl.ds(0, 1), slice(None))], ref[index + (pl.ds(height - 1, 1), slice(None))]
    )


def store_view(ref, index, value, rows):
    if not rows:
        ref[index] = value
        return
    height = ref.shape[-2]
    ref[index + (pl.ds(0, 1), slice(None))] = value[0:1]
    ref[index + (pl.ds(height - 1, 1), slice(None))] = value[1:2]


def sides_of(refs, f, k, rows=False):
    block, west, east, south, north = refs
    if not rows:
        return around(
            block[f, k], west[f, k], east[f, k], south[f, pl.ds(k, 1), :], north[f, pl.ds(k, 1), :]
        )
    height = west.shape[2]
    low = block[f, k, pl.ds(0, 2), :]
    high = block[f, k, pl.ds(height - 2, 2), :]
    centre = pick_rows(low[0:1], high[1:2])
    at_north = pick_rows(low[1:2], north[f, pl.ds(k, 1), :])
    at_south = pick_rows(south[f, pl.ds(k, 1), :], high[0:1])
    west_end = pick_rows(west[f, k, pl.ds(0, 1), :], west[f, k, pl.ds(height - 1, 1), :])
    east_end = pick_rows(east[f, k, pl.ds(0, 1), :], east[f, k, pl.ds(height - 1, 1), :])
    width = centre.shape[1]
    lane = lax.broadcasted_iota(jnp.int32, centre.shape, 1)
    at_east = jnp.where(lane == width - 1, east_end, pltpu.roll(centre, width - 1, 1))
    at_west = jnp.where(lane == 0, west_end, pltpu.roll(centre, 1, 1))
    return (centre, at_east, at_west, at_north, at_south)


def low_order(tracer, zonal, meridional, wet_sides):
    value_centre, value_east, value_west, value_north, value_south = tracer
    speed_centre, speed_west = (zonal[0], zonal[2])
    flow_centre, flow_south = (meridional[0], meridional[4])
    wet_centre, wet_east, wet_west, wet_north, wet_south = wet_sides
    face_east = wet_centre * wet_east
    face_west = wet_west * wet_centre
    face_north = wet_centre * wet_north
    face_south = wet_south * wet_centre
    upwind_east = face_east * (
        jnp.maximum(speed_centre, 0.0) * value_centre + jnp.minimum(speed_centre, 0.0) * value_east
    )
    upwind_west = face_west * (
        jnp.maximum(speed_west, 0.0) * value_west + jnp.minimum(speed_west, 0.0) * value_centre
    )
    upwind_north = face_north * (
        jnp.maximum(flow_centre, 0.0) * value_centre + jnp.minimum(flow_centre, 0.0) * value_north
    )
    upwind_south = face_south * (
        jnp.maximum(flow_south, 0.0) * value_south + jnp.minimum(flow_south, 0.0) * value_centre
    )
    anti_east = face_east * speed_centre * (value_centre + value_east) * 0.5 - upwind_east
    anti_west = face_west * speed_west * (value_west + value_centre) * 0.5 - upwind_west
    anti_north = face_north * flow_centre * (value_centre + value_north) * 0.5 - upwind_north
    anti_south = face_south * flow_south * (value_south + value_centre) * 0.5 - upwind_south
    upwind = value_centre - wet_centre * (upwind_east - upwind_west + upwind_north - upwind_south)
    inflow = (
        jnp.maximum(anti_west, 0.0)
        - jnp.minimum(anti_east, 0.0)
        + jnp.maximum(anti_south, 0.0)
        - jnp.minimum(anti_north, 0.0)
    )
    outflow = (
        jnp.maximum(anti_east, 0.0)
        - jnp.minimum(anti_west, 0.0)
        + jnp.maximum(anti_north, 0.0)
        - jnp.minimum(anti_south, 0.0)
    )
    anti = (anti_east, anti_west, anti_north, anti_south)
    return (upwind, anti, inflow, outflow)


def level_low_order(state_refs, k, tracer):
    zonal = sides_of(state_refs, 2, k)
    meridional = sides_of(state_refs, 3, k)
    wet_sides = sides_of(state_refs, 4, k)
    return low_order(sides_of(state_refs, tracer, k), zonal, meridional, wet_sides), wet_sides


def ratio_pair(upwind_sides, wet_sides, inflow, outflow):
    value_centre = upwind_sides[0]
    candidates = [value_centre] + [
        jnp.where(beside_wet > 0.5, beside, value_centre)
        for beside, beside_wet in zip(upwind_sides[1:], wet_sides[1:])
    ]
    highest = functools.reduce(jnp.maximum, candidates)
    lowest = functools.reduce(jnp.minimum, candidates)
    ratio_plus = jnp.minimum(1.0, (highest - value_centre) / jnp.maximum(inflow, RATIO_FLOOR))
    ratio_minus = jnp.minimum(1.0, (value_centre - lowest) / jnp.maximum(outflow, RATIO_FLOOR))
    return ratio_plus, ratio_minus


def limited(plus, minus, upwind, anti, wet_centre):
    plus_centre, plus_east, plus_west, plus_north, plus_south = plus
    minus_centre, minus_east, minus_west, minus_north, minus_south = minus
    anti_east, anti_west, anti_north, anti_south = anti
    coef_east = jnp.where(
        anti_east >= 0.0, jnp.minimum(plus_east, minus_centre), jnp.minimum(plus_centre, minus_east)
    )
    coef_west = jnp.where(
        anti_west >= 0.0, jnp.minimum(plus_centre, minus_west), jnp.minimum(plus_west, minus_centre)
    )
    coef_north = jnp.where(
        anti_north >= 0.0,
        jnp.minimum(plus_north, minus_centre),
        jnp.minimum(plus_centre, minus_north),
    )
    coef_south = jnp.where(
        anti_south >= 0.0,
        jnp.minimum(plus_centre, minus_south),
        jnp.minimum(plus_south, minus_centre),
    )
    return upwind - wet_centre * (
        coef_east * anti_east
        - coef_west * anti_west
        + coef_north * anti_north
        - coef_south * anti_south
    )


def upwind_kernel(state_refs, out, anti_out, flow_out, rows=False):
    levels = out.shape[1]

    def body(k, carry):
        zonal = sides_of(state_refs, 2, k, rows)
        meridional = sides_of(state_refs, 3, k, rows)
        wet_sides = sides_of(state_refs, 4, k, rows)
        for tracer in range(2):
            tracer_sides = sides_of(state_refs, tracer, k, rows)
            upwind, anti, inflow, outflow = low_order(tracer_sides, zonal, meridional, wet_sides)
            store_view(out, (tracer, k), upwind, rows)
            for face in range(4):
                store_view(anti_out, (4 * tracer + face, k), anti[face], rows)
            store_view(flow_out, (tracer, k), inflow, rows)
            store_view(flow_out, (2 + tracer, k), outflow, rows)
        return carry

    lax.fori_loop(0, levels, body, 0)


def ratio_kernel(state_refs, upwind_refs, flow, out, rows=False):
    levels = out.shape[1]

    def body(k, carry):
        wet_sides = sides_of(state_refs, 4, k, rows)
        for tracer in range(2):
            plus, minus = ratio_pair(
                sides_of(upwind_refs, tracer, k, rows),
                wet_sides,
                load_view(flow, (tracer, k), rows),
                load_view(flow, (2 + tracer, k), rows),
            )
            store_view(out, (tracer, k), plus, rows)
            store_view(out, (2 + tracer, k), minus, rows)
        return carry

    lax.fori_loop(0, levels, body, 0)


def advected_kernel(wet, upwind_ref, anti_ref, ratio_refs, out, rows=False):
    levels = out.shape[1]

    def body(k, carry):
        wet_centre = load_view(wet, (k,), rows)
        for tracer in range(2):
            anti = tuple(load_view(anti_ref, (4 * tracer + face, k), rows) for face in range(4))
            plus = sides_of(ratio_refs, tracer, k, rows)
            minus = sides_of(ratio_refs, 2 + tracer, k, rows)
            upwind = load_view(upwind_ref, (tracer, k), rows)
            store_view(out, (tracer, k), limited(plus, minus, upwind, anti, wet_centre), rows)
        return carry

    lax.fori_loop(0, levels, body, 0)


def isopycnal_kernel(advected_refs, state_refs, out, rows=False):
    levels = out.shape[1]

    def body(k, carry):
        above = jnp.minimum(k + 1, levels - 1)
        values = [sides_of(advected_refs, tracer, k, rows) for tracer in range(2)]
        uppers = [sides_of(advected_refs, tracer, above, rows) for tracer in range(2)]
        wet_sides = sides_of(state_refs, 4, k, rows)
        wet_above = sides_of(state_refs, 4, above, rows)
        stacked = [w * a for w, a in zip(wet_sides, wet_above)]
        verticals = [
            [(u - v) * s for u, v, s in zip(uppers[tracer], values[tracer], stacked)]
            for tracer in range(2)
        ]
        densities = [HALINE_COEF * s - THERMAL_COEF * t for t, s in zip(values[0], values[1])]
        stratas = [HALINE_COEF * s - THERMAL_COEF * t for t, s in zip(verticals[0], verticals[1])]
        for tracer in range(2):
            value, vertical = values[tracer], verticals[tracer]

            def face_flux(first, second):
                face = wet_sides[first] * wet_sides[second]
                slope = jnp.clip(
                    (densities[second] - densities[first])
                    / jnp.maximum(0.5 * (stratas[first] + stratas[second]), SLOPE_FLOOR),
                    -SLOPE_LIMIT,
                    SLOPE_LIMIT,
                )
                return (
                    DIFFUSIVITY
                    * face
                    * (
                        value[second]
                        - value[first]
                        - slope * 0.5 * (vertical[first] + vertical[second])
                    )
                )

            east_flux = face_flux(0, 1)
            west_flux = face_flux(2, 0)
            north_flux = face_flux(0, 3)
            south_flux = face_flux(4, 0)
            result = value[0] + wet_sides[0] * (east_flux - west_flux + north_flux - south_flux)
            store_view(out, (tracer, k), result, rows)
        return carry

    lax.fori_loop(0, levels, body, 0)


class Stack:
    def __init__(self, *refs):
        self.refs = refs
        self.shape = (len(refs),) + refs[0].shape

    def __getitem__(self, index):
        return self.refs[index[0]][index[1:]]


class Pair:
    def __init__(self, first, second):
        self.refs = (first, second)
        self.shape = (2,) + first.shape

    def __setitem__(self, index, value):
        self.refs[index[0]][index[1:]] = value


def buffers_for(fields, levels, height, width, lon):
    columns = pltpu.VMEM((fields, 16, height), jnp.float32)
    rows = pltpu.VMEM((fields, levels, width), jnp.float32)
    halo = pltpu.VMEM((fields, levels, height, 1), jnp.float32)
    return [
        columns,
        columns,
        rows,
        rows,
        columns,
        columns,
        rows,
        rows,
        pltpu.VMEM((lon, fields, levels, width), jnp.float32),
        halo,
        halo,
        rows,
    ]


STAGE_FIELDS = (5, 2, 4, 2)


def fused_kernel(
    lon, lat, signs, seam, heat, salt, zonal, meridional, sea, depth, first_out, second_out, *scratch
):
    mesh = pl.DeviceIdType.MESH
    upwind, ratio, advected, anti, flow, wet = scratch[:6]
    count = len(STAGE_FIELDS)
    per_stage = [scratch[6 + 12 * s : 18 + 12 * s] for s in range(count)]
    fold_send, fold_recv, side_send, side_recv = scratch[6 + 12 * count :]
    me = lax.axis_index("lon")
    row = lax.axis_index("lat")
    west = lax.rem(me + lon - 1, lon)
    east = lax.rem(me + 1, lon)
    has_south = row > 0
    has_north = row < lat - 1
    on_top = row == lat - 1
    levels, height, width = heat.shape
    wet_column = sea[...] == 1
    for k in range(levels):
        wet[k] = jnp.where(wet_column & (k < depth[...]), 1.0, 0.0).astype(jnp.float32)
    state = Stack(heat, salt, zonal, meridional, wet)
    pivot = seam[0]
    pivot_block, pivot_offset = pivot // width, pivot % width
    lower = lax.rem(pivot_block - me - 1 + 2 * lon, lon)
    upper = lax.rem(pivot_block - me + 2 * lon, lon)
    source_lane = lax.broadcasted_iota(jnp.int32, (width, width), 0)
    target_lane = lax.broadcasted_iota(jnp.int32, (width, width), 1)
    reverse = (
        jnp.where(source_lane == width + pivot_offset - target_lane, 1.0, 0.0).astype(jnp.float32),
        jnp.where(source_lane == pivot_offset - target_lane, 1.0, 0.0).astype(jnp.float32),
    )

    barrier = pltpu.get_barrier_semaphore()
    for peer in range(lon):

        @pl.when((me != peer) & (on_top | (peer == west) | (peer == east)))
        def _():
            pl.semaphore_signal(barrier, 1, device_id={"lon": peer}, device_id_type=mesh)

    @pl.when(has_south)
    def _():
        pl.semaphore_signal(barrier, 1, device_id={"lat": row - 1}, device_id_type=mesh)

    @pl.when(has_north)
    def _():
        pl.semaphore_signal(barrier, 1, device_id={"lat": row + 1}, device_id_type=mesh)

    beside = 1 if lon == 2 else 2
    pl.semaphore_wait(
        barrier,
        jnp.where(on_top, lon - 1, beside)
        + has_south.astype(jnp.int32)
        + has_north.astype(jnp.int32),
    )

    def exchange(s, source):
        wsend, esend, ssend, nsend, whalo, ehalo, shalo, nhalo, gathered, wcol, ecol, north = (
            per_stage[s]
        )
        fields = source.shape[0]
        for f in range(fields):
            for k in range(levels):
                tile = source[f, k]
                flipped = tile.T
                wsend[f, pl.ds(k, 1), :] = flipped[0:1, :]
                esend[f, pl.ds(k, 1), :] = flipped[width - 1 : width, :]
                ssend[f, pl.ds(k, 1), :] = tile[0:1, :]
                nsend[f, pl.ds(k, 1), :] = tile[height - 1 : height, :]
            spare = wsend.shape[1] - levels
            wsend[f, pl.ds(levels, spare), :] = jnp.zeros((spare, height), jnp.float32)
            esend[f, pl.ds(levels, spare), :] = jnp.zeros((spare, height), jnp.float32)

        def fold_copy(peer, slot):
            return pltpu.make_async_remote_copy(
                src_ref=nsend,
                dst_ref=gathered.at[slot],
                send_sem=fold_send.at[s, peer],
                recv_sem=fold_recv.at[s, slot],
                device_id={"lon": peer},
                device_id_type=mesh,
            )

        def side(i, src, dst, device):
            return pltpu.make_async_remote_copy(
                src_ref=src,
                dst_ref=dst,
                send_sem=side_send.at[s, i],
                recv_sem=side_recv.at[s, i],
                device_id=device,
                device_id_type=mesh,
            )

        to_west = side(0, wsend, ehalo, {"lon": west})
        to_east = side(1, esend, whalo, {"lon": east})
        to_south = side(2, ssend, nhalo, {"lat": row - 1})
        to_north = side(3, nsend, shalo, {"lat": row + 1})
        to_west.start()
        to_east.start()

        @pl.when(has_south)
        def _():
            to_south.start()

        @pl.when(has_north)
        def _():
            to_north.start()

        for peer in range(lon):

            @pl.when((me != peer) & on_top)
            def _():
                fold_copy(peer, me).start()

        @pl.when(on_top)
        def _():
            gathered[me] = nsend[...]

        to_west.wait()
        to_east.wait()

        for f in range(fields):
            both = jnp.concatenate([whalo[f], ehalo[f]], axis=0).T
            for k in range(levels):
                wcol[f, k] = both[:, k : k + 1]
                ecol[f, k] = both[:, 16 + k : 17 + k]

        def finish():
            @pl.when(has_south)
            def _():
                to_south.wait_send()
                to_north.wait_recv()

            @pl.when(has_north)
            def _():
                to_north.wait_send()
                to_south.wait_recv()

            @pl.when(jnp.logical_not(has_south))
            def _():
                shalo[...] = jnp.zeros_like(shalo)

            @pl.when(jnp.logical_not(has_north))
            def _():
                nhalo[...] = jnp.zeros_like(nhalo)

            @pl.when(jnp.logical_not(on_top))
            def _():
                north[...] = nhalo[...]

            for peer in range(lon):

                @pl.when((me != peer) & on_top)
                def _():
                    fold_copy(peer, me).wait_send()
                    fold_copy(peer, peer).wait_recv()

            @pl.when(on_top)
            def _():
                for f in range(fields):
                    ghost = jnp.dot(
                        gathered[lower, f],
                        reverse[0],
                        precision=lax.Precision.HIGHEST,
                        preferred_element_type=jnp.float32,
                    ) + jnp.dot(
                        gathered[upper, f],
                        reverse[1],
                        precision=lax.Precision.HIGHEST,
                        preferred_element_type=jnp.float32,
                    )
                    north[f] = ghost * (signs[f] if s == 0 else 1.0)

        return (source, wcol, ecol, ssend, nsend), (source, wcol, ecol, shalo, north), finish

    def run(stage, finish):
        stage(False)
        finish()
        stage(True)

    state_early, state_refs, finish = exchange(0, state)
    run(
        lambda rows: upwind_kernel(state_refs if rows else state_early, upwind, anti, flow, rows),
        finish,
    )
    upwind_early, upwind_refs, finish = exchange(1, upwind)
    run(
        lambda rows: ratio_kernel(
            state_refs, upwind_refs if rows else upwind_early, flow, ratio, rows
        ),
        finish,
    )
    ratio_early, ratio_refs, finish = exchange(2, ratio)
    run(
        lambda rows: advected_kernel(
            wet, upwind, anti, ratio_refs if rows else ratio_early, advected, rows
        ),
        finish,
    )
    advected_early, advected_refs, finish = exchange(3, advected)
    final = Pair(first_out, second_out)
    run(
        lambda rows: isopycnal_kernel(
            advected_refs if rows else advected_early, state_refs, final, rows
        ),
        finish,
    )


def fused(fields, seam):
    lon = lax.axis_size("lon")
    lat = lax.axis_size("lat")
    levels, height, width = fields[0].shape
    block = jax.ShapeDtypeStruct((levels, height, width), jnp.float32)
    scratch = [
        pltpu.VMEM((2, levels, height, width), jnp.float32),
        pltpu.VMEM((4, levels, height, width), jnp.float32),
        pltpu.VMEM((2, levels, height, width), jnp.float32),
        pltpu.VMEM((8, levels, height, width), jnp.float32),
        pltpu.VMEM((4, levels, height, width), jnp.float32),
        pltpu.VMEM((levels, height, width), jnp.float32),
    ]
    for count in STAGE_FIELDS:
        scratch += buffers_for(count, levels, height, width, lon)
    stages = len(STAGE_FIELDS)
    scratch += [
        pltpu.SemaphoreType.DMA((stages, lon)),
        pltpu.SemaphoreType.DMA((stages, lon)),
        pltpu.SemaphoreType.DMA((stages, 4)),
        pltpu.SemaphoreType.DMA((stages, 4)),
    ]
    return pl.pallas_call(
        functools.partial(fused_kernel, lon, lat, STATE_SIGNS),
        out_shape=(block, block),
        in_specs=[pl.BlockSpec(memory_space=pltpu.SMEM)]
        + [pl.BlockSpec(memory_space=pltpu.VMEM)] * len(fields),
        out_specs=[pl.BlockSpec(memory_space=pltpu.VMEM)] * 2,
        scratch_shapes=scratch,
        compiler_params=pltpu.CompilerParams(
            collective_id=0, has_side_effects=True, vmem_limit_bytes=60 * 1024 * 1024
        ),
    )(seam, *fields)


def local(
    heat_content_field,
    saltiness_field,
    eastward_cfl_number,
    northward_cfl_number,
    seawater_indicator,
    submerged_layer_total,
    seam_partner_index,
):
    return fused(
        (
            heat_content_field,
            saltiness_field,
            eastward_cfl_number,
            northward_cfl_number,
            seawater_indicator,
            submerged_layer_total,
        ),
        seam_partner_index,
    )


def solution(mesh):
    in_specs = (
        P(None, "lat", "lon"),
        P(None, "lat", "lon"),
        P(None, "lat", "lon"),
        P(None, "lat", "lon"),
        P("lat", "lon"),
        P("lat", "lon"),
        P(),
    )
    out_specs = (P(None, "lat", "lon"), P(None, "lat", "lon"))
    return jax.shard_map(local, mesh=mesh, in_specs=in_specs, out_specs=out_specs, check_vma=False)
```

```python
import functools

import jax
import jax.numpy as jnp
from jax import lax
from jax.experimental import pallas as pl
from jax.experimental.pallas import tpu as pltpu
from jax.sharding import PartitionSpec as P

RATIO_FLOOR = 0.05
SLOPE_FLOOR = 0.5
SLOPE_LIMIT = 2.0
DIFFUSIVITY = 0.1
THERMAL_COEF = 0.2
HALINE_COEF = 0.8
STATE_SIGNS = (1.0, 1.0, -1.0, -1.0, 1.0)


def sign_column(values):
    return jnp.array(values, jnp.float32).reshape(len(values), 1, 1, 1)


def around(x, west, east, south, north):
    height, width = x.shape
    lane = lax.broadcasted_iota(jnp.int32, x.shape, 1)
    level = lax.broadcasted_iota(jnp.int32, x.shape, 0)
    at_east = jnp.where(lane == width - 1, east, pltpu.roll(x, width - 1, 1))
    at_west = jnp.where(lane == 0, west, pltpu.roll(x, 1, 1))
    at_north = jnp.where(level == height - 1, north, pltpu.roll(x, height - 1, 0))
    at_south = jnp.where(level == 0, south, pltpu.roll(x, 1, 0))
    return (x, at_east, at_west, at_north, at_south)


def pick_rows(low, high):
    level = lax.broadcasted_iota(jnp.int32, (2, high.shape[-1]), 0)
    return jnp.where(level == 0, low, high)


def load_view(ref, index, rows):
    if not rows:
        return ref[index]
    height = ref.shape[-2]
    return pick_rows(
        ref[index + (pl.ds(0, 1), slice(None))], ref[index + (pl.ds(height - 1, 1), slice(None))]
    )


def store_view(ref, index, value, rows):
    if not rows:
        ref[index] = value
        return
    height = ref.shape[-2]
    ref[index + (pl.ds(0, 1), slice(None))] = value[0:1]
    ref[index + (pl.ds(height - 1, 1), slice(None))] = value[1:2]


def sides_of(refs, f, k, rows=False):
    block, west, east, south, north = refs
    if not rows:
        return around(
            block[f, k], west[f, k], east[f, k], south[f, pl.ds(k, 1), :], north[f, pl.ds(k, 1), :]
        )
    height = west.shape[2]
    low = block[f, k, pl.ds(0, 2), :]
    high = block[f, k, pl.ds(height - 2, 2), :]
    centre = pick_rows(low[0:1], high[1:2])
    at_north = pick_rows(low[1:2], north[f, pl.ds(k, 1), :])
    at_south = pick_rows(south[f, pl.ds(k, 1), :], high[0:1])
    west_end = pick_rows(west[f, k, pl.ds(0, 1), :], west[f, k, pl.ds(height - 1, 1), :])
    east_end = pick_rows(east[f, k, pl.ds(0, 1), :], east[f, k, pl.ds(height - 1, 1), :])
    width = centre.shape[1]
    lane = lax.broadcasted_iota(jnp.int32, centre.shape, 1)
    at_east = jnp.where(lane == width - 1, east_end, pltpu.roll(centre, width - 1, 1))
    at_west = jnp.where(lane == 0, west_end, pltpu.roll(centre, 1, 1))
    return (centre, at_east, at_west, at_north, at_south)


def low_order(tracer, zonal, meridional, wet_sides):
    value_centre, value_east, value_west, value_north, value_south = tracer
    speed_centre, speed_west = (zonal[0], zonal[2])
    flow_centre, flow_south = (meridional[0], meridional[4])
    wet_centre, wet_east, wet_west, wet_north, wet_south = wet_sides
    face_east = wet_centre * wet_east
    face_west = wet_west * wet_centre
    face_north = wet_centre * wet_north
    face_south = wet_south * wet_centre
    upwind_east = face_east * (
        jnp.maximum(speed_centre, 0.0) * value_centre + jnp.minimum(speed_centre, 0.0) * value_east
    )
    upwind_west = face_west * (
        jnp.maximum(speed_west, 0.0) * value_west + jnp.minimum(speed_west, 0.0) * value_centre
    )
    upwind_north = face_north * (
        jnp.maximum(flow_centre, 0.0) * value_centre + jnp.minimum(flow_centre, 0.0) * value_north
    )
    upwind_south = face_south * (
        jnp.maximum(flow_south, 0.0) * value_south + jnp.minimum(flow_south, 0.0) * value_centre
    )
    anti_east = face_east * speed_centre * (value_centre + value_east) * 0.5 - upwind_east
    anti_west = face_west * speed_west * (value_west + value_centre) * 0.5 - upwind_west
    anti_north = face_north * flow_centre * (value_centre + value_north) * 0.5 - upwind_north
    anti_south = face_south * flow_south * (value_south + value_centre) * 0.5 - upwind_south
    upwind = value_centre - wet_centre * (upwind_east - upwind_west + upwind_north - upwind_south)
    inflow = (
        jnp.maximum(anti_west, 0.0)
        - jnp.minimum(anti_east, 0.0)
        + jnp.maximum(anti_south, 0.0)
        - jnp.minimum(anti_north, 0.0)
    )
    outflow = (
        jnp.maximum(anti_east, 0.0)
        - jnp.minimum(anti_west, 0.0)
        + jnp.maximum(anti_north, 0.0)
        - jnp.minimum(anti_south, 0.0)
    )
    anti = (anti_east, anti_west, anti_north, anti_south)
    return (upwind, anti, inflow, outflow)


def level_low_order(state_refs, k, tracer):
    zonal = sides_of(state_refs, 2, k)
    meridional = sides_of(state_refs, 3, k)
    wet_sides = sides_of(state_refs, 4, k)
    return low_order(sides_of(state_refs, tracer, k), zonal, meridional, wet_sides), wet_sides


def ratio_pair(upwind_sides, wet_sides, inflow, outflow):
    value_centre = upwind_sides[0]
    candidates = [value_centre] + [
        jnp.where(beside_wet > 0.5, beside, value_centre)
        for beside, beside_wet in zip(upwind_sides[1:], wet_sides[1:])
    ]
    highest = functools.reduce(jnp.maximum, candidates)
    lowest = functools.reduce(jnp.minimum, candidates)
    ratio_plus = jnp.minimum(1.0, (highest - value_centre) / jnp.maximum(inflow, RATIO_FLOOR))
    ratio_minus = jnp.minimum(1.0, (value_centre - lowest) / jnp.maximum(outflow, RATIO_FLOOR))
    return ratio_plus, ratio_minus


def limited(plus, minus, upwind, anti, wet_centre):
    plus_centre, plus_east, plus_west, plus_north, plus_south = plus
    minus_centre, minus_east, minus_west, minus_north, minus_south = minus
    anti_east, anti_west, anti_north, anti_south = anti
    coef_east = jnp.where(
        anti_east >= 0.0, jnp.minimum(plus_east, minus_centre), jnp.minimum(plus_centre, minus_east)
    )
    coef_west = jnp.where(
        anti_west >= 0.0, jnp.minimum(plus_centre, minus_west), jnp.minimum(plus_west, minus_centre)
    )
    coef_north = jnp.where(
        anti_north >= 0.0,
        jnp.minimum(plus_north, minus_centre),
        jnp.minimum(plus_centre, minus_north),
    )
    coef_south = jnp.where(
        anti_south >= 0.0,
        jnp.minimum(plus_centre, minus_south),
        jnp.minimum(plus_south, minus_centre),
    )
    return upwind - wet_centre * (
        coef_east * anti_east
        - coef_west * anti_west
        + coef_north * anti_north
        - coef_south * anti_south
    )


def upwind_kernel(state_refs, out, anti_out, flow_out, rows=False):
    levels = out.shape[1]

    def body(k, carry):
        zonal = sides_of(state_refs, 2, k, rows)
        meridional = sides_of(state_refs, 3, k, rows)
        wet_sides = sides_of(state_refs, 4, k, rows)
        for tracer in range(2):
            tracer_sides = sides_of(state_refs, tracer, k, rows)
            upwind, anti, inflow, outflow = low_order(tracer_sides, zonal, meridional, wet_sides)
            store_view(out, (tracer, k), upwind, rows)
            for face in range(4):
                store_view(anti_out, (4 * tracer + face, k), anti[face], rows)
            store_view(flow_out, (tracer, k), inflow, rows)
            store_view(flow_out, (2 + tracer, k), outflow, rows)
        return carry

    lax.fori_loop(0, levels, body, 0)


def ratio_kernel(state_refs, upwind_refs, flow, out, rows=False):
    levels = out.shape[1]

    def body(k, carry):
        wet_sides = sides_of(state_refs, 4, k, rows)
        for tracer in range(2):
            plus, minus = ratio_pair(
                sides_of(upwind_refs, tracer, k, rows),
                wet_sides,
                load_view(flow, (tracer, k), rows),
                load_view(flow, (2 + tracer, k), rows),
            )
            store_view(out, (tracer, k), plus, rows)
            store_view(out, (2 + tracer, k), minus, rows)
        return carry

    lax.fori_loop(0, levels, body, 0)


def advected_kernel(wet, upwind_ref, anti_ref, ratio_refs, out, rows=False):
    levels = out.shape[1]

    def body(k, carry):
        wet_centre = load_view(wet, (k,), rows)
        for tracer in range(2):
            anti = tuple(load_view(anti_ref, (4 * tracer + face, k), rows) for face in range(4))
            plus = sides_of(ratio_refs, tracer, k, rows)
            minus = sides_of(ratio_refs, 2 + tracer, k, rows)
            upwind = load_view(upwind_ref, (tracer, k), rows)
            store_view(out, (tracer, k), limited(plus, minus, upwind, anti, wet_centre), rows)
        return carry

    lax.fori_loop(0, levels, body, 0)


def isopycnal_kernel(advected_refs, state_refs, out, rows=False):
    levels = out.shape[1]

    def body(k, carry):
        above = jnp.minimum(k + 1, levels - 1)
        values = [sides_of(advected_refs, tracer, k, rows) for tracer in range(2)]
        uppers = [sides_of(advected_refs, tracer, above, rows) for tracer in range(2)]
        wet_sides = sides_of(state_refs, 4, k, rows)
        wet_above = sides_of(state_refs, 4, above, rows)
        stacked = [w * a for w, a in zip(wet_sides, wet_above)]
        verticals = [
            [(u - v) * s for u, v, s in zip(uppers[tracer], values[tracer], stacked)]
            for tracer in range(2)
        ]
        densities = [HALINE_COEF * s - THERMAL_COEF * t for t, s in zip(values[0], values[1])]
        stratas = [HALINE_COEF * s - THERMAL_COEF * t for t, s in zip(verticals[0], verticals[1])]
        for tracer in range(2):
            value, vertical = values[tracer], verticals[tracer]

            def face_flux(first, second):
                face = wet_sides[first] * wet_sides[second]
                slope = jnp.clip(
                    (densities[second] - densities[first])
                    / jnp.maximum(0.5 * (stratas[first] + stratas[second]), SLOPE_FLOOR),
                    -SLOPE_LIMIT,
                    SLOPE_LIMIT,
                )
                return (
                    DIFFUSIVITY
                    * face
                    * (
                        value[second]
                        - value[first]
                        - slope * 0.5 * (vertical[first] + vertical[second])
                    )
                )

            east_flux = face_flux(0, 1)
            west_flux = face_flux(2, 0)
            north_flux = face_flux(0, 3)
            south_flux = face_flux(4, 0)
            result = value[0] + wet_sides[0] * (east_flux - west_flux + north_flux - south_flux)
            store_view(out, (tracer, k), result, rows)
        return carry

    lax.fori_loop(0, levels, body, 0)


class Stack:
    def __init__(self, *refs):
        self.refs = refs
        self.shape = (len(refs),) + refs[0].shape

    def __getitem__(self, index):
        return self.refs[index[0]][index[1:]]


class Pair:
    def __init__(self, first, second):
        self.refs = (first, second)
        self.shape = (2,) + first.shape

    def __setitem__(self, index, value):
        self.refs[index[0]][index[1:]] = value


def buffers_for(fields, levels, height, width, lon):
    columns = pltpu.VMEM((fields, 16, height), jnp.float32)
    rows = pltpu.VMEM((fields, levels, width), jnp.float32)
    halo = pltpu.VMEM((fields, levels, height, width), jnp.float32)
    return [
        columns,
        columns,
        rows,
        rows,
        columns,
        columns,
        rows,
        rows,
        pltpu.VMEM((lon, fields, levels, width), jnp.float32),
        halo,
        halo,
        rows,
    ]


STAGE_FIELDS = (5, 2, 4, 2)


def fused_kernel(
    lon, lat, signs, seam, heat, salt, zonal, meridional, sea, depth, first_out, second_out, *scratch
):
    mesh = pl.DeviceIdType.MESH
    upwind, ratio, advected, anti, flow, wet = scratch[:6]
    count = len(STAGE_FIELDS)
    per_stage = [scratch[6 + 12 * s : 18 + 12 * s] for s in range(count)]
    fold_send, fold_recv, side_send, side_recv = scratch[6 + 12 * count :]
    me = lax.axis_index("lon")
    row = lax.axis_index("lat")
    west = lax.rem(me + lon - 1, lon)
    east = lax.rem(me + 1, lon)
    has_south = row > 0
    has_north = row < lat - 1
    on_top = row == lat - 1
    levels, height, width = heat.shape
    wet_column = sea[...] == 1
    for k in range(levels):
        wet[k] = jnp.where(wet_column & (k < depth[...]), 1.0, 0.0).astype(jnp.float32)
    state = Stack(heat, salt, zonal, meridional, wet)
    pivot = seam[0]
    pivot_block, pivot_offset = pivot // width, pivot % width
    lower = lax.rem(pivot_block - me - 1 + 2 * lon, lon)
    upper = lax.rem(pivot_block - me + 2 * lon, lon)
    source_lane = lax.broadcasted_iota(jnp.int32, (width, width), 0)
    target_lane = lax.broadcasted_iota(jnp.int32, (width, width), 1)
    reverse = (
        jnp.where(source_lane == width + pivot_offset - target_lane, 1.0, 0.0).astype(jnp.float32),
        jnp.where(source_lane == pivot_offset - target_lane, 1.0, 0.0).astype(jnp.float32),
    )

    barrier = pltpu.get_barrier_semaphore()
    for peer in range(lon):

        @pl.when((me != peer) & (on_top | (peer == west) | (peer == east)))
        def _():
            pl.semaphore_signal(barrier, 1, device_id={"lon": peer}, device_id_type=mesh)

    @pl.when(has_south)
    def _():
        pl.semaphore_signal(barrier, 1, device_id={"lat": row - 1}, device_id_type=mesh)

    @pl.when(has_north)
    def _():
        pl.semaphore_signal(barrier, 1, device_id={"lat": row + 1}, device_id_type=mesh)

    beside = 1 if lon == 2 else 2
    pl.semaphore_wait(
        barrier,
        jnp.where(on_top, lon - 1, beside)
        + has_south.astype(jnp.int32)
        + has_north.astype(jnp.int32),
    )

    def exchange(s, source):
        wsend, esend, ssend, nsend, whalo, ehalo, shalo, nhalo, gathered, wcol, ecol, north = (
            per_stage[s]
        )
        fields = source.shape[0]
        for f in range(fields):
            for k in range(levels):
                tile = source[f, k]
                flipped = tile.T
                wsend[f, pl.ds(k, 1), :] = flipped[0:1, :]
                esend[f, pl.ds(k, 1), :] = flipped[width - 1 : width, :]
                ssend[f, pl.ds(k, 1), :] = tile[0:1, :]
                nsend[f, pl.ds(k, 1), :] = tile[height - 1 : height, :]
            spare = wsend.shape[1] - levels
            wsend[f, pl.ds(levels, spare), :] = jnp.zeros((spare, height), jnp.float32)
            esend[f, pl.ds(levels, spare), :] = jnp.zeros((spare, height), jnp.float32)

        def fold_copy(peer, slot):
            return pltpu.make_async_remote_copy(
                src_ref=nsend,
                dst_ref=gathered.at[slot],
                send_sem=fold_send.at[s, peer],
                recv_sem=fold_recv.at[s, slot],
                device_id={"lon": peer},
                device_id_type=mesh,
            )

        def side(i, src, dst, device):
            return pltpu.make_async_remote_copy(
                src_ref=src,
                dst_ref=dst,
                send_sem=side_send.at[s, i],
                recv_sem=side_recv.at[s, i],
                device_id=device,
                device_id_type=mesh,
            )

        to_west = side(0, wsend, ehalo, {"lon": west})
        to_east = side(1, esend, whalo, {"lon": east})
        to_south = side(2, ssend, nhalo, {"lat": row - 1})
        to_north = side(3, nsend, shalo, {"lat": row + 1})
        to_west.start()
        to_east.start()

        @pl.when(has_south)
        def _():
            to_south.start()

        @pl.when(has_north)
        def _():
            to_north.start()

        for peer in range(lon):

            @pl.when((me != peer) & on_top)
            def _():
                fold_copy(peer, me).start()

        @pl.when(on_top)
        def _():
            gathered[me] = nsend[...]

        to_west.wait()
        to_east.wait()

        edge = lax.broadcasted_iota(jnp.int32, (height, width), 1)
        for f in range(fields):
            rows = whalo.shape[1]
            spread = jnp.concatenate(
                [whalo[f], ehalo[f], jnp.zeros((width - 2 * rows, height), jnp.float32)], axis=0
            ).T
            for k in range(levels):
                west_lane = spread if k == 0 else pltpu.roll(spread, width - k, 1)
                east_lane = pltpu.roll(spread, width - 1 - rows - k, 1)
                wcol[f, k] = jnp.where(edge == 0, west_lane, east_lane)

        def finish():
            @pl.when(has_south)
            def _():
                to_south.wait_send()
                to_north.wait_recv()

            @pl.when(has_north)
            def _():
                to_north.wait_send()
                to_south.wait_recv()

            @pl.when(jnp.logical_not(has_south))
            def _():
                shalo[...] = jnp.zeros_like(shalo)

            @pl.when(jnp.logical_not(has_north))
            def _():
                nhalo[...] = jnp.zeros_like(nhalo)

            @pl.when(jnp.logical_not(on_top))
            def _():
                north[...] = nhalo[...]

            for peer in range(lon):

                @pl.when((me != peer) & on_top)
                def _():
                    fold_copy(peer, me).wait_send()
                    fold_copy(peer, peer).wait_recv()

            @pl.when(on_top)
            def _():
                for f in range(fields):
                    ghost = jnp.dot(
                        gathered[lower, f],
                        reverse[0],
                        precision=lax.Precision.HIGHEST,
                        preferred_element_type=jnp.float32,
                    ) + jnp.dot(
                        gathered[upper, f],
                        reverse[1],
                        precision=lax.Precision.HIGHEST,
                        preferred_element_type=jnp.float32,
                    )
                    north[f] = ghost * (signs[f] if s == 0 else 1.0)

        return (source, wcol, wcol, ssend, nsend), (source, wcol, wcol, shalo, north), finish

    def run(stage, finish):
        stage(False)
        finish()
        stage(True)

    state_early, state_refs, finish = exchange(0, state)
    run(
        lambda rows: upwind_kernel(state_refs if rows else state_early, upwind, anti, flow, rows),
        finish,
    )
    upwind_early, upwind_refs, finish = exchange(1, upwind)
    run(
        lambda rows: ratio_kernel(
            state_refs, upwind_refs if rows else upwind_early, flow, ratio, rows
        ),
        finish,
    )
    ratio_early, ratio_refs, finish = exchange(2, ratio)
    run(
        lambda rows: advected_kernel(
            wet, upwind, anti, ratio_refs if rows else ratio_early, advected, rows
        ),
        finish,
    )
    advected_early, advected_refs, finish = exchange(3, advected)
    final = Pair(first_out, second_out)
    run(
        lambda rows: isopycnal_kernel(
            advected_refs if rows else advected_early, state_refs, final, rows
        ),
        finish,
    )


def fused(fields, seam):
    lon = lax.axis_size("lon")
    lat = lax.axis_size("lat")
    levels, height, width = fields[0].shape
    block = jax.ShapeDtypeStruct((levels, height, width), jnp.float32)
    scratch = [
        pltpu.VMEM((2, levels, height, width), jnp.float32),
        pltpu.VMEM((4, levels, height, width), jnp.float32),
        pltpu.VMEM((2, levels, height, width), jnp.float32),
        pltpu.VMEM((8, levels, height, width), jnp.float32),
        pltpu.VMEM((4, levels, height, width), jnp.float32),
        pltpu.VMEM((levels, height, width), jnp.float32),
    ]
    for count in STAGE_FIELDS:
        scratch += buffers_for(count, levels, height, width, lon)
    stages = len(STAGE_FIELDS)
    scratch += [
        pltpu.SemaphoreType.DMA((stages, lon)),
        pltpu.SemaphoreType.DMA((stages, lon)),
        pltpu.SemaphoreType.DMA((stages, 4)),
        pltpu.SemaphoreType.DMA((stages, 4)),
    ]
    return pl.pallas_call(
        functools.partial(fused_kernel, lon, lat, STATE_SIGNS),
        out_shape=(block, block),
        in_specs=[pl.BlockSpec(memory_space=pltpu.SMEM)]
        + [pl.BlockSpec(memory_space=pltpu.VMEM)] * len(fields),
        out_specs=[pl.BlockSpec(memory_space=pltpu.VMEM)] * 2,
        scratch_shapes=scratch,
        compiler_params=pltpu.CompilerParams(
            collective_id=0, has_side_effects=True, vmem_limit_bytes=60 * 1024 * 1024
        ),
    )(seam, *fields)


def local(
    heat_content_field,
    saltiness_field,
    eastward_cfl_number,
    northward_cfl_number,
    seawater_indicator,
    submerged_layer_total,
    seam_partner_index,
):
    return fused(
        (
            heat_content_field,
            saltiness_field,
            eastward_cfl_number,
            northward_cfl_number,
            seawater_indicator,
            submerged_layer_total,
        ),
        seam_partner_index,
    )


def solution(mesh):
    in_specs = (
        P(None, "lat", "lon"),
        P(None, "lat", "lon"),
        P(None, "lat", "lon"),
        P(None, "lat", "lon"),
        P("lat", "lon"),
        P("lat", "lon"),
        P(),
    )
    out_specs = (P(None, "lat", "lon"), P(None, "lat", "lon"))
    return jax.shard_map(local, mesh=mesh, in_specs=in_specs, out_specs=out_specs, check_vma=False)
```

```python
import functools

import jax
import jax.numpy as jnp
from jax import lax
from jax.experimental import pallas as pl
from jax.experimental.pallas import tpu as pltpu
from jax.sharding import PartitionSpec as P

RATIO_FLOOR = 0.05
SLOPE_FLOOR = 0.5
SLOPE_LIMIT = 2.0
DIFFUSIVITY = 0.1
THERMAL_COEF = 0.2
HALINE_COEF = 0.8
STATE_SIGNS = (1.0, 1.0, -1.0, -1.0, 1.0)


def sign_column(values):
    return jnp.array(values, jnp.float32).reshape(len(values), 1, 1, 1)


def around(x, west, east, south, north):
    height, width = x.shape
    lane = lax.broadcasted_iota(jnp.int32, x.shape, 1)
    level = lax.broadcasted_iota(jnp.int32, x.shape, 0)
    at_east = jnp.where(lane == width - 1, east, pltpu.roll(x, width - 1, 1))
    at_west = jnp.where(lane == 0, west, pltpu.roll(x, 1, 1))
    at_north = jnp.where(level == height - 1, north, pltpu.roll(x, height - 1, 0))
    at_south = jnp.where(level == 0, south, pltpu.roll(x, 1, 0))
    return (x, at_east, at_west, at_north, at_south)


def pick_rows(low, high):
    level = lax.broadcasted_iota(jnp.int32, (2, high.shape[-1]), 0)
    return jnp.where(level == 0, low, high)


def load_view(ref, index, rows):
    if not rows:
        return ref[index]
    height = ref.shape[-2]
    return pick_rows(
        ref[index + (pl.ds(0, 1), slice(None))], ref[index + (pl.ds(height - 1, 1), slice(None))]
    )


def store_view(ref, index, value, rows):
    if not rows:
        ref[index] = value
        return
    height = ref.shape[-2]
    ref[index + (pl.ds(0, 1), slice(None))] = value[0:1]
    ref[index + (pl.ds(height - 1, 1), slice(None))] = value[1:2]


def sides_of(refs, f, k, rows=False):
    block, west, east, south, north = refs
    line = pl.ds(f * block.shape[1] + k, 1)
    if not rows:
        return around(block[f, k], west[f, k], east[f, k], south[line, :], north[line, :])
    height = west.shape[2]
    low = block[f, k, pl.ds(0, 2), :]
    high = block[f, k, pl.ds(height - 2, 2), :]
    centre = pick_rows(low[0:1], high[1:2])
    at_north = pick_rows(low[1:2], north[line, :])
    at_south = pick_rows(south[line, :], high[0:1])
    west_end = pick_rows(west[f, k, pl.ds(0, 1), :], west[f, k, pl.ds(height - 1, 1), :])
    east_end = pick_rows(east[f, k, pl.ds(0, 1), :], east[f, k, pl.ds(height - 1, 1), :])
    width = centre.shape[1]
    lane = lax.broadcasted_iota(jnp.int32, centre.shape, 1)
    at_east = jnp.where(lane == width - 1, east_end, pltpu.roll(centre, width - 1, 1))
    at_west = jnp.where(lane == 0, west_end, pltpu.roll(centre, 1, 1))
    return (centre, at_east, at_west, at_north, at_south)


def low_order(tracer, zonal, meridional, wet_sides):
    value_centre, value_east, value_west, value_north, value_south = tracer
    speed_centre, speed_west = (zonal[0], zonal[2])
    flow_centre, flow_south = (meridional[0], meridional[4])
    wet_centre, wet_east, wet_west, wet_north, wet_south = wet_sides
    face_east = wet_centre * wet_east
    face_west = wet_west * wet_centre
    face_north = wet_centre * wet_north
    face_south = wet_south * wet_centre
    upwind_east = face_east * (
        jnp.maximum(speed_centre, 0.0) * value_centre + jnp.minimum(speed_centre, 0.0) * value_east
    )
    upwind_west = face_west * (
        jnp.maximum(speed_west, 0.0) * value_west + jnp.minimum(speed_west, 0.0) * value_centre
    )
    upwind_north = face_north * (
        jnp.maximum(flow_centre, 0.0) * value_centre + jnp.minimum(flow_centre, 0.0) * value_north
    )
    upwind_south = face_south * (
        jnp.maximum(flow_south, 0.0) * value_south + jnp.minimum(flow_south, 0.0) * value_centre
    )
    anti_east = face_east * speed_centre * (value_centre + value_east) * 0.5 - upwind_east
    anti_west = face_west * speed_west * (value_west + value_centre) * 0.5 - upwind_west
    anti_north = face_north * flow_centre * (value_centre + value_north) * 0.5 - upwind_north
    anti_south = face_south * flow_south * (value_south + value_centre) * 0.5 - upwind_south
    upwind = value_centre - wet_centre * (upwind_east - upwind_west + upwind_north - upwind_south)
    inflow = (
        jnp.maximum(anti_west, 0.0)
        - jnp.minimum(anti_east, 0.0)
        + jnp.maximum(anti_south, 0.0)
        - jnp.minimum(anti_north, 0.0)
    )
    outflow = (
        jnp.maximum(anti_east, 0.0)
        - jnp.minimum(anti_west, 0.0)
        + jnp.maximum(anti_north, 0.0)
        - jnp.minimum(anti_south, 0.0)
    )
    anti = (anti_east, anti_west, anti_north, anti_south)
    return (upwind, anti, inflow, outflow)


def level_low_order(state_refs, k, tracer):
    zonal = sides_of(state_refs, 2, k)
    meridional = sides_of(state_refs, 3, k)
    wet_sides = sides_of(state_refs, 4, k)
    return low_order(sides_of(state_refs, tracer, k), zonal, meridional, wet_sides), wet_sides


def ratio_pair(upwind_sides, wet_sides, inflow, outflow):
    value_centre = upwind_sides[0]
    candidates = [value_centre] + [
        jnp.where(beside_wet > 0.5, beside, value_centre)
        for beside, beside_wet in zip(upwind_sides[1:], wet_sides[1:])
    ]
    highest = functools.reduce(jnp.maximum, candidates)
    lowest = functools.reduce(jnp.minimum, candidates)
    ratio_plus = jnp.minimum(1.0, (highest - value_centre) / jnp.maximum(inflow, RATIO_FLOOR))
    ratio_minus = jnp.minimum(1.0, (value_centre - lowest) / jnp.maximum(outflow, RATIO_FLOOR))
    return ratio_plus, ratio_minus


def limited(plus, minus, upwind, anti, wet_centre):
    plus_centre, plus_east, plus_west, plus_north, plus_south = plus
    minus_centre, minus_east, minus_west, minus_north, minus_south = minus
    anti_east, anti_west, anti_north, anti_south = anti
    coef_east = jnp.where(
        anti_east >= 0.0, jnp.minimum(plus_east, minus_centre), jnp.minimum(plus_centre, minus_east)
    )
    coef_west = jnp.where(
        anti_west >= 0.0, jnp.minimum(plus_centre, minus_west), jnp.minimum(plus_west, minus_centre)
    )
    coef_north = jnp.where(
        anti_north >= 0.0,
        jnp.minimum(plus_north, minus_centre),
        jnp.minimum(plus_centre, minus_north),
    )
    coef_south = jnp.where(
        anti_south >= 0.0,
        jnp.minimum(plus_centre, minus_south),
        jnp.minimum(plus_south, minus_centre),
    )
    return upwind - wet_centre * (
        coef_east * anti_east
        - coef_west * anti_west
        + coef_north * anti_north
        - coef_south * anti_south
    )


def upwind_kernel(state_refs, out, anti_out, flow_out, rows=False):
    levels = out.shape[1]

    def body(k, carry):
        zonal = sides_of(state_refs, 2, k, rows)
        meridional = sides_of(state_refs, 3, k, rows)
        wet_sides = sides_of(state_refs, 4, k, rows)
        for tracer in range(2):
            tracer_sides = sides_of(state_refs, tracer, k, rows)
            upwind, anti, inflow, outflow = low_order(tracer_sides, zonal, meridional, wet_sides)
            store_view(out, (tracer, k), upwind, rows)
            for face in range(4):
                store_view(anti_out, (4 * tracer + face, k), anti[face], rows)
            store_view(flow_out, (tracer, k), inflow, rows)
            store_view(flow_out, (2 + tracer, k), outflow, rows)
        return carry

    lax.fori_loop(0, levels, body, 0)


def ratio_kernel(state_refs, upwind_refs, flow, out, rows=False):
    levels = out.shape[1]

    def body(k, carry):
        wet_sides = sides_of(state_refs, 4, k, rows)
        for tracer in range(2):
            plus, minus = ratio_pair(
                sides_of(upwind_refs, tracer, k, rows),
                wet_sides,
                load_view(flow, (tracer, k), rows),
                load_view(flow, (2 + tracer, k), rows),
            )
            store_view(out, (tracer, k), plus, rows)
            store_view(out, (2 + tracer, k), minus, rows)
        return carry

    lax.fori_loop(0, levels, body, 0)


def advected_kernel(wet, upwind_ref, anti_ref, ratio_refs, out, rows=False):
    levels = out.shape[1]

    def body(k, carry):
        wet_centre = load_view(wet, (k,), rows)
        for tracer in range(2):
            anti = tuple(load_view(anti_ref, (4 * tracer + face, k), rows) for face in range(4))
            plus = sides_of(ratio_refs, tracer, k, rows)
            minus = sides_of(ratio_refs, 2 + tracer, k, rows)
            upwind = load_view(upwind_ref, (tracer, k), rows)
            store_view(out, (tracer, k), limited(plus, minus, upwind, anti, wet_centre), rows)
        return carry

    lax.fori_loop(0, levels, body, 0)


def isopycnal_kernel(advected_refs, state_refs, out, rows=False):
    levels = out.shape[1]

    def body(k, carry):
        above = jnp.minimum(k + 1, levels - 1)
        values = [sides_of(advected_refs, tracer, k, rows) for tracer in range(2)]
        uppers = [sides_of(advected_refs, tracer, above, rows) for tracer in range(2)]
        wet_sides = sides_of(state_refs, 4, k, rows)
        wet_above = sides_of(state_refs, 4, above, rows)
        stacked = [w * a for w, a in zip(wet_sides, wet_above)]
        verticals = [
            [(u - v) * s for u, v, s in zip(uppers[tracer], values[tracer], stacked)]
            for tracer in range(2)
        ]
        densities = [HALINE_COEF * s - THERMAL_COEF * t for t, s in zip(values[0], values[1])]
        stratas = [HALINE_COEF * s - THERMAL_COEF * t for t, s in zip(verticals[0], verticals[1])]
        for tracer in range(2):
            value, vertical = values[tracer], verticals[tracer]

            def face_flux(first, second):
                face = wet_sides[first] * wet_sides[second]
                slope = jnp.clip(
                    (densities[second] - densities[first])
                    / jnp.maximum(0.5 * (stratas[first] + stratas[second]), SLOPE_FLOOR),
                    -SLOPE_LIMIT,
                    SLOPE_LIMIT,
                )
                return (
                    DIFFUSIVITY
                    * face
                    * (
                        value[second]
                        - value[first]
                        - slope * 0.5 * (vertical[first] + vertical[second])
                    )
                )

            east_flux = face_flux(0, 1)
            west_flux = face_flux(2, 0)
            north_flux = face_flux(0, 3)
            south_flux = face_flux(4, 0)
            result = value[0] + wet_sides[0] * (east_flux - west_flux + north_flux - south_flux)
            store_view(out, (tracer, k), result, rows)
        return carry

    lax.fori_loop(0, levels, body, 0)


class Stack:
    def __init__(self, *refs):
        self.refs = refs
        self.shape = (len(refs),) + refs[0].shape

    def __getitem__(self, index):
        return self.refs[index[0]][index[1:]]


class Pair:
    def __init__(self, first, second):
        self.refs = (first, second)
        self.shape = (2,) + first.shape

    def __setitem__(self, index, value):
        self.refs[index[0]][index[1:]] = value


def buffers_for(fields, levels, height, width, lon):
    columns = pltpu.VMEM((fields, 16, height), jnp.float32)
    rows = pltpu.VMEM((fields * levels, width), jnp.float32)
    halo = pltpu.VMEM((fields, levels, height, width), jnp.float32)
    return [
        columns,
        columns,
        rows,
        rows,
        columns,
        columns,
        rows,
        rows,
        pltpu.VMEM((lon, fields * levels, width), jnp.float32),
        halo,
        halo,
        rows,
    ]


STAGE_FIELDS = (5, 2, 4, 2)


def fused_kernel(
    lon, lat, signs, seam, heat, salt, zonal, meridional, sea, depth, first_out, second_out, *scratch
):
    mesh = pl.DeviceIdType.MESH
    upwind, ratio, advected, anti, flow, wet = scratch[:6]
    count = len(STAGE_FIELDS)
    per_stage = [scratch[6 + 12 * s : 18 + 12 * s] for s in range(count)]
    fold_send, fold_recv, side_send, side_recv = scratch[6 + 12 * count :]
    me = lax.axis_index("lon")
    row = lax.axis_index("lat")
    west = lax.rem(me + lon - 1, lon)
    east = lax.rem(me + 1, lon)
    has_south = row > 0
    has_north = row < lat - 1
    on_top = row == lat - 1
    levels, height, width = heat.shape
    wet_column = sea[...] == 1
    for k in range(levels):
        wet[k] = jnp.where(wet_column & (k < depth[...]), 1.0, 0.0).astype(jnp.float32)
    state = Stack(heat, salt, zonal, meridional, wet)
    pivot = seam[0]
    pivot_block, pivot_offset = pivot // width, pivot % width
    lower = lax.rem(pivot_block - me - 1 + 2 * lon, lon)
    upper = lax.rem(pivot_block - me + 2 * lon, lon)
    source_lane = lax.broadcasted_iota(jnp.int32, (width, width), 0)
    target_lane = lax.broadcasted_iota(jnp.int32, (width, width), 1)
    reverse = (
        jnp.where(source_lane == width + pivot_offset - target_lane, 1.0, 0.0).astype(jnp.float32),
        jnp.where(source_lane == pivot_offset - target_lane, 1.0, 0.0).astype(jnp.float32),
    )

    barrier = pltpu.get_barrier_semaphore()
    for peer in range(lon):

        @pl.when((me != peer) & (on_top | (peer == west) | (peer == east)))
        def _():
            pl.semaphore_signal(barrier, 1, device_id={"lon": peer}, device_id_type=mesh)

    @pl.when(has_south)
    def _():
        pl.semaphore_signal(barrier, 1, device_id={"lat": row - 1}, device_id_type=mesh)

    @pl.when(has_north)
    def _():
        pl.semaphore_signal(barrier, 1, device_id={"lat": row + 1}, device_id_type=mesh)

    beside = 1 if lon == 2 else 2
    pl.semaphore_wait(
        barrier,
        jnp.where(on_top, lon - 1, beside)
        + has_south.astype(jnp.int32)
        + has_north.astype(jnp.int32),
    )

    def exchange(s, source):
        wsend, esend, ssend, nsend, whalo, ehalo, shalo, nhalo, gathered, wcol, ecol, north = (
            per_stage[s]
        )
        fields = source.shape[0]
        for f in range(fields):
            for k in range(levels):
                tile = source[f, k]
                flipped = tile.T
                wsend[f, pl.ds(k, 1), :] = flipped[0:1, :]
                esend[f, pl.ds(k, 1), :] = flipped[width - 1 : width, :]
                ssend[pl.ds(f * levels + k, 1), :] = tile[0:1, :]
                nsend[pl.ds(f * levels + k, 1), :] = tile[height - 1 : height, :]
            spare = wsend.shape[1] - levels
            wsend[f, pl.ds(levels, spare), :] = jnp.zeros((spare, height), jnp.float32)
            esend[f, pl.ds(levels, spare), :] = jnp.zeros((spare, height), jnp.float32)

        def fold_copy(peer, slot):
            return pltpu.make_async_remote_copy(
                src_ref=nsend,
                dst_ref=gathered.at[slot],
                send_sem=fold_send.at[s, peer],
                recv_sem=fold_recv.at[s, slot],
                device_id={"lon": peer},
                device_id_type=mesh,
            )

        def side(i, src, dst, device):
            return pltpu.make_async_remote_copy(
                src_ref=src,
                dst_ref=dst,
                send_sem=side_send.at[s, i],
                recv_sem=side_recv.at[s, i],
                device_id=device,
                device_id_type=mesh,
            )

        to_west = side(0, wsend, ehalo, {"lon": west})
        to_east = side(1, esend, whalo, {"lon": east})
        to_south = side(2, ssend, nhalo, {"lat": row - 1})
        to_north = side(3, nsend, shalo, {"lat": row + 1})
        to_west.start()
        to_east.start()

        @pl.when(has_south)
        def _():
            to_south.start()

        @pl.when(has_north)
        def _():
            to_north.start()

        for peer in range(lon):

            @pl.when((me != peer) & on_top)
            def _():
                fold_copy(peer, me).start()

        @pl.when(on_top)
        def _():
            gathered[me] = nsend[...]

        to_west.wait()
        to_east.wait()

        edge = lax.broadcasted_iota(jnp.int32, (height, width), 1)
        for f in range(fields):
            rows = whalo.shape[1]
            spread = jnp.concatenate(
                [whalo[f], ehalo[f], jnp.zeros((width - 2 * rows, height), jnp.float32)], axis=0
            ).T
            for k in range(levels):
                west_lane = spread if k == 0 else pltpu.roll(spread, width - k, 1)
                east_lane = pltpu.roll(spread, width - 1 - rows - k, 1)
                wcol[f, k] = jnp.where(edge == 0, west_lane, east_lane)

        def finish():
            @pl.when(has_south)
            def _():
                to_south.wait_send()
                to_north.wait_recv()

            @pl.when(has_north)
            def _():
                to_north.wait_send()
                to_south.wait_recv()

            @pl.when(jnp.logical_not(has_south))
            def _():
                shalo[...] = jnp.zeros_like(shalo)

            @pl.when(jnp.logical_not(has_north))
            def _():
                nhalo[...] = jnp.zeros_like(nhalo)

            @pl.when(jnp.logical_not(on_top))
            def _():
                north[...] = nhalo[...]

            for peer in range(lon):

                @pl.when((me != peer) & on_top)
                def _():
                    fold_copy(peer, me).wait_send()
                    fold_copy(peer, peer).wait_recv()

            @pl.when(on_top)
            def _():
                ghost = jnp.dot(
                    gathered[lower],
                    reverse[0],
                    precision=lax.Precision.HIGHEST,
                    preferred_element_type=jnp.float32,
                ) + jnp.dot(
                    gathered[upper],
                    reverse[1],
                    precision=lax.Precision.HIGHEST,
                    preferred_element_type=jnp.float32,
                )
                if s == 0:
                    line = lax.broadcasted_iota(jnp.int32, ghost.shape, 0)
                    sign = jnp.ones(ghost.shape, jnp.float32)
                    for f in range(fields):
                        owned = (line >= f * levels) & (line < (f + 1) * levels)
                        sign = jnp.where(owned, signs[f], sign)
                    ghost = ghost * sign
                north[...] = ghost

        return (source, wcol, wcol, ssend, nsend), (source, wcol, wcol, shalo, north), finish

    def run(stage, finish):
        stage(False)
        finish()
        stage(True)

    state_early, state_refs, finish = exchange(0, state)
    run(
        lambda rows: upwind_kernel(state_refs if rows else state_early, upwind, anti, flow, rows),
        finish,
    )
    upwind_early, upwind_refs, finish = exchange(1, upwind)
    run(
        lambda rows: ratio_kernel(
            state_refs, upwind_refs if rows else upwind_early, flow, ratio, rows
        ),
        finish,
    )
    ratio_early, ratio_refs, finish = exchange(2, ratio)
    run(
        lambda rows: advected_kernel(
            wet, upwind, anti, ratio_refs if rows else ratio_early, advected, rows
        ),
        finish,
    )
    advected_early, advected_refs, finish = exchange(3, advected)
    final = Pair(first_out, second_out)
    run(
        lambda rows: isopycnal_kernel(
            advected_refs if rows else advected_early, state_refs, final, rows
        ),
        finish,
    )


def fused(fields, seam):
    lon = lax.axis_size("lon")
    lat = lax.axis_size("lat")
    levels, height, width = fields[0].shape
    block = jax.ShapeDtypeStruct((levels, height, width), jnp.float32)
    scratch = [
        pltpu.VMEM((2, levels, height, width), jnp.float32),
        pltpu.VMEM((4, levels, height, width), jnp.float32),
        pltpu.VMEM((2, levels, height, width), jnp.float32),
        pltpu.VMEM((8, levels, height, width), jnp.float32),
        pltpu.VMEM((4, levels, height, width), jnp.float32),
        pltpu.VMEM((levels, height, width), jnp.float32),
    ]
    for count in STAGE_FIELDS:
        scratch += buffers_for(count, levels, height, width, lon)
    stages = len(STAGE_FIELDS)
    scratch += [
        pltpu.SemaphoreType.DMA((stages, lon)),
        pltpu.SemaphoreType.DMA((stages, lon)),
        pltpu.SemaphoreType.DMA((stages, 4)),
        pltpu.SemaphoreType.DMA((stages, 4)),
    ]
    return pl.pallas_call(
        functools.partial(fused_kernel, lon, lat, STATE_SIGNS),
        out_shape=(block, block),
        in_specs=[pl.BlockSpec(memory_space=pltpu.SMEM)]
        + [pl.BlockSpec(memory_space=pltpu.VMEM)] * len(fields),
        out_specs=[pl.BlockSpec(memory_space=pltpu.VMEM)] * 2,
        scratch_shapes=scratch,
        compiler_params=pltpu.CompilerParams(
            collective_id=0, has_side_effects=True, vmem_limit_bytes=60 * 1024 * 1024
        ),
    )(seam, *fields)


def local(
    heat_content_field,
    saltiness_field,
    eastward_cfl_number,
    northward_cfl_number,
    seawater_indicator,
    submerged_layer_total,
    seam_partner_index,
):
    return fused(
        (
            heat_content_field,
            saltiness_field,
            eastward_cfl_number,
            northward_cfl_number,
            seawater_indicator,
            submerged_layer_total,
        ),
        seam_partner_index,
    )


def solution(mesh):
    in_specs = (
        P(None, "lat", "lon"),
        P(None, "lat", "lon"),
        P(None, "lat", "lon"),
        P(None, "lat", "lon"),
        P("lat", "lon"),
        P("lat", "lon"),
        P(),
    )
    out_specs = (P(None, "lat", "lon"), P(None, "lat", "lon"))
    return jax.shard_map(local, mesh=mesh, in_specs=in_specs, out_specs=out_specs, check_vma=False)
```

```python
import functools

import jax
import jax.numpy as jnp
from jax import lax
from jax.experimental import pallas as pl
from jax.experimental.pallas import tpu as pltpu
from jax.sharding import PartitionSpec as P

RATIO_FLOOR = 0.05
SLOPE_FLOOR = 0.5
SLOPE_LIMIT = 2.0
DIFFUSIVITY = 0.1
THERMAL_COEF = 0.2
HALINE_COEF = 0.8
STATE_SIGNS = (1.0, 1.0, -1.0, -1.0, 1.0)


def sign_column(values):
    return jnp.array(values, jnp.float32).reshape(len(values), 1, 1, 1)


def around(x, west, east, south, north):
    height, width = x.shape
    lane = lax.broadcasted_iota(jnp.int32, x.shape, 1)
    level = lax.broadcasted_iota(jnp.int32, x.shape, 0)
    at_east = jnp.where(lane == width - 1, east, pltpu.roll(x, width - 1, 1))
    at_west = jnp.where(lane == 0, west, pltpu.roll(x, 1, 1))
    at_north = jnp.where(level == height - 1, north, pltpu.roll(x, height - 1, 0))
    at_south = jnp.where(level == 0, south, pltpu.roll(x, 1, 0))
    return (x, at_east, at_west, at_north, at_south)


def pick_rows(low, high):
    level = lax.broadcasted_iota(jnp.int32, (2, high.shape[-1]), 0)
    return jnp.where(level == 0, low, high)


def load_view(ref, index, rows):
    if not rows:
        return ref[index]
    height = ref.shape[-2]
    return pick_rows(
        ref[index + (pl.ds(0, 1), slice(None))], ref[index + (pl.ds(height - 1, 1), slice(None))]
    )


def store_view(ref, index, value, rows):
    if not rows:
        ref[index] = value
        return
    height = ref.shape[-2]
    ref[index + (pl.ds(0, 1), slice(None))] = value[0:1]
    ref[index + (pl.ds(height - 1, 1), slice(None))] = value[1:2]


def sides_of(refs, f, k, rows=False):
    block, west, east, south, north = refs
    line = pl.ds(f * block.shape[1] + k, 1)
    if not rows:
        return around(block[f, k], west[f, k], east[f, k], south[line, :], north[line, :])
    height = west.shape[2]
    low = block[f, k, pl.ds(0, 2), :]
    high = block[f, k, pl.ds(height - 2, 2), :]
    centre = pick_rows(low[0:1], high[1:2])
    at_north = pick_rows(low[1:2], north[line, :])
    at_south = pick_rows(south[line, :], high[0:1])
    west_end = pick_rows(west[f, k, pl.ds(0, 1), :], west[f, k, pl.ds(height - 1, 1), :])
    east_end = pick_rows(east[f, k, pl.ds(0, 1), :], east[f, k, pl.ds(height - 1, 1), :])
    width = centre.shape[1]
    lane = lax.broadcasted_iota(jnp.int32, centre.shape, 1)
    at_east = jnp.where(lane == width - 1, east_end, pltpu.roll(centre, width - 1, 1))
    at_west = jnp.where(lane == 0, west_end, pltpu.roll(centre, 1, 1))
    return (centre, at_east, at_west, at_north, at_south)


def low_order(tracer, zonal, meridional, wet_sides):
    value_centre, value_east, value_west, value_north, value_south = tracer
    speed_centre, speed_west = (zonal[0], zonal[2])
    flow_centre, flow_south = (meridional[0], meridional[4])
    wet_centre, wet_east, wet_west, wet_north, wet_south = wet_sides
    face_east = wet_centre * wet_east
    face_west = wet_west * wet_centre
    face_north = wet_centre * wet_north
    face_south = wet_south * wet_centre
    upwind_east = face_east * (
        jnp.maximum(speed_centre, 0.0) * value_centre + jnp.minimum(speed_centre, 0.0) * value_east
    )
    upwind_west = face_west * (
        jnp.maximum(speed_west, 0.0) * value_west + jnp.minimum(speed_west, 0.0) * value_centre
    )
    upwind_north = face_north * (
        jnp.maximum(flow_centre, 0.0) * value_centre + jnp.minimum(flow_centre, 0.0) * value_north
    )
    upwind_south = face_south * (
        jnp.maximum(flow_south, 0.0) * value_south + jnp.minimum(flow_south, 0.0) * value_centre
    )
    anti_east = face_east * speed_centre * (value_centre + value_east) * 0.5 - upwind_east
    anti_west = face_west * speed_west * (value_west + value_centre) * 0.5 - upwind_west
    anti_north = face_north * flow_centre * (value_centre + value_north) * 0.5 - upwind_north
    anti_south = face_south * flow_south * (value_south + value_centre) * 0.5 - upwind_south
    upwind = value_centre - wet_centre * (upwind_east - upwind_west + upwind_north - upwind_south)
    inflow = (
        jnp.maximum(anti_west, 0.0)
        - jnp.minimum(anti_east, 0.0)
        + jnp.maximum(anti_south, 0.0)
        - jnp.minimum(anti_north, 0.0)
    )
    outflow = (
        jnp.maximum(anti_east, 0.0)
        - jnp.minimum(anti_west, 0.0)
        + jnp.maximum(anti_north, 0.0)
        - jnp.minimum(anti_south, 0.0)
    )
    anti = (anti_east, anti_west, anti_north, anti_south)
    return (upwind, anti, inflow, outflow)


def level_low_order(state_refs, k, tracer):
    zonal = sides_of(state_refs, 2, k)
    meridional = sides_of(state_refs, 3, k)
    wet_sides = sides_of(state_refs, 4, k)
    return low_order(sides_of(state_refs, tracer, k), zonal, meridional, wet_sides), wet_sides


def ratio_pair(upwind_sides, wet_sides, inflow, outflow):
    value_centre = upwind_sides[0]
    candidates = [value_centre] + [
        jnp.where(beside_wet > 0.5, beside, value_centre)
        for beside, beside_wet in zip(upwind_sides[1:], wet_sides[1:])
    ]
    highest = functools.reduce(jnp.maximum, candidates)
    lowest = functools.reduce(jnp.minimum, candidates)
    ratio_plus = jnp.minimum(1.0, (highest - value_centre) / jnp.maximum(inflow, RATIO_FLOOR))
    ratio_minus = jnp.minimum(1.0, (value_centre - lowest) / jnp.maximum(outflow, RATIO_FLOOR))
    return ratio_plus, ratio_minus


def limited(plus, minus, upwind, anti, wet_centre):
    plus_centre, plus_east, plus_west, plus_north, plus_south = plus
    minus_centre, minus_east, minus_west, minus_north, minus_south = minus
    anti_east, anti_west, anti_north, anti_south = anti
    coef_east = jnp.where(
        anti_east >= 0.0, jnp.minimum(plus_east, minus_centre), jnp.minimum(plus_centre, minus_east)
    )
    coef_west = jnp.where(
        anti_west >= 0.0, jnp.minimum(plus_centre, minus_west), jnp.minimum(plus_west, minus_centre)
    )
    coef_north = jnp.where(
        anti_north >= 0.0,
        jnp.minimum(plus_north, minus_centre),
        jnp.minimum(plus_centre, minus_north),
    )
    coef_south = jnp.where(
        anti_south >= 0.0,
        jnp.minimum(plus_centre, minus_south),
        jnp.minimum(plus_south, minus_centre),
    )
    return upwind - wet_centre * (
        coef_east * anti_east
        - coef_west * anti_west
        + coef_north * anti_north
        - coef_south * anti_south
    )


def upwind_kernel(state_refs, out, anti_out, flow_out, rows=False):
    levels = out.shape[1]

    def body(k, carry):
        zonal = sides_of(state_refs, 2, k, rows)
        meridional = sides_of(state_refs, 3, k, rows)
        wet_sides = sides_of(state_refs, 4, k, rows)
        for tracer in range(2):
            tracer_sides = sides_of(state_refs, tracer, k, rows)
            upwind, anti, inflow, outflow = low_order(tracer_sides, zonal, meridional, wet_sides)
            store_view(out, (tracer, k), upwind, rows)
            for face in range(4):
                store_view(anti_out, (4 * tracer + face, k), anti[face], rows)
            store_view(flow_out, (tracer, k), inflow, rows)
            store_view(flow_out, (2 + tracer, k), outflow, rows)
        return carry

    lax.fori_loop(0, levels, body, 0)


def ratio_kernel(state_refs, upwind_refs, flow, out, rows=False):
    levels = out.shape[1]

    def body(k, carry):
        wet_sides = sides_of(state_refs, 4, k, rows)
        for tracer in range(2):
            plus, minus = ratio_pair(
                sides_of(upwind_refs, tracer, k, rows),
                wet_sides,
                load_view(flow, (tracer, k), rows),
                load_view(flow, (2 + tracer, k), rows),
            )
            store_view(out, (tracer, k), plus, rows)
            store_view(out, (2 + tracer, k), minus, rows)
        return carry

    lax.fori_loop(0, levels, body, 0)


def advected_kernel(wet, upwind_ref, anti_ref, ratio_refs, out, rows=False):
    levels = out.shape[1]

    def body(k, carry):
        wet_centre = load_view(wet, (k,), rows)
        for tracer in range(2):
            anti = tuple(load_view(anti_ref, (4 * tracer + face, k), rows) for face in range(4))
            plus = sides_of(ratio_refs, tracer, k, rows)
            minus = sides_of(ratio_refs, 2 + tracer, k, rows)
            upwind = load_view(upwind_ref, (tracer, k), rows)
            store_view(out, (tracer, k), limited(plus, minus, upwind, anti, wet_centre), rows)
        return carry

    lax.fori_loop(0, levels, body, 0)


def isopycnal_kernel(advected_refs, state_refs, out, rows=False):
    levels = out.shape[1]

    def body(k, carry):
        above = jnp.minimum(k + 1, levels - 1)
        values = [sides_of(advected_refs, tracer, k, rows) for tracer in range(2)]
        uppers = [sides_of(advected_refs, tracer, above, rows) for tracer in range(2)]
        wet_sides = sides_of(state_refs, 4, k, rows)
        wet_above = sides_of(state_refs, 4, above, rows)
        stacked = [w * a for w, a in zip(wet_sides, wet_above)]
        verticals = [
            [(u - v) * s for u, v, s in zip(uppers[tracer], values[tracer], stacked)]
            for tracer in range(2)
        ]
        densities = [HALINE_COEF * s - THERMAL_COEF * t for t, s in zip(values[0], values[1])]
        stratas = [HALINE_COEF * s - THERMAL_COEF * t for t, s in zip(verticals[0], verticals[1])]
        for tracer in range(2):
            value, vertical = values[tracer], verticals[tracer]

            def face_flux(first, second):
                face = wet_sides[first] * wet_sides[second]
                slope = jnp.clip(
                    (densities[second] - densities[first])
                    / jnp.maximum(0.5 * (stratas[first] + stratas[second]), SLOPE_FLOOR),
                    -SLOPE_LIMIT,
                    SLOPE_LIMIT,
                )
                return (
                    DIFFUSIVITY
                    * face
                    * (
                        value[second]
                        - value[first]
                        - slope * 0.5 * (vertical[first] + vertical[second])
                    )
                )

            east_flux = face_flux(0, 1)
            west_flux = face_flux(2, 0)
            north_flux = face_flux(0, 3)
            south_flux = face_flux(4, 0)
            result = value[0] + wet_sides[0] * (east_flux - west_flux + north_flux - south_flux)
            store_view(out, (tracer, k), result, rows)
        return carry

    lax.fori_loop(0, levels, body, 0)


class Stack:
    def __init__(self, *refs):
        self.refs = refs
        self.shape = (len(refs),) + refs[0].shape

    def __getitem__(self, index):
        return self.refs[index[0]][index[1:]]


class Pair:
    def __init__(self, first, second):
        self.refs = (first, second)
        self.shape = (2,) + first.shape

    def __setitem__(self, index, value):
        self.refs[index[0]][index[1:]] = value


def buffers_for(fields, levels, height, width, lon):
    columns = pltpu.VMEM((fields, 16, height), jnp.float32)
    rows = pltpu.VMEM((fields * levels, width), jnp.float32)
    halo = pltpu.VMEM((fields, levels, height, width), jnp.float32)
    return [
        columns,
        columns,
        rows,
        rows,
        columns,
        columns,
        rows,
        rows,
        pltpu.VMEM((lon, fields * levels, width), jnp.float32),
        halo,
        halo,
        rows,
    ]


STAGE_FIELDS = (5, 2, 4, 2)


def fused_kernel(
    lon, lat, signs, seam, heat, salt, zonal, meridional, sea, depth, first_out, second_out, *scratch
):
    mesh = pl.DeviceIdType.MESH
    upwind, ratio, advected, anti, flow, wet = scratch[:6]
    count = len(STAGE_FIELDS)
    per_stage = [scratch[6 + 12 * s : 18 + 12 * s] for s in range(count)]
    fold_send, fold_recv, side_send, side_recv = scratch[6 + 12 * count :]
    me = lax.axis_index("lon")
    row = lax.axis_index("lat")
    west = lax.rem(me + lon - 1, lon)
    east = lax.rem(me + 1, lon)
    has_south = row > 0
    has_north = row < lat - 1
    on_top = row == lat - 1
    levels, height, width = heat.shape
    wet_column = sea[...] == 1
    for k in range(levels):
        wet[k] = jnp.where(wet_column & (k < depth[...]), 1.0, 0.0).astype(jnp.float32)
    state = Stack(heat, salt, zonal, meridional, wet)
    pivot = seam[0]
    pivot_block, pivot_offset = pivot // width, pivot % width
    lower = lax.rem(pivot_block - me - 1 + 2 * lon, lon)
    upper = lax.rem(pivot_block - me + 2 * lon, lon)
    source_lane = lax.broadcasted_iota(jnp.int32, (width, width), 0)
    target_lane = lax.broadcasted_iota(jnp.int32, (width, width), 1)
    reverse = (
        jnp.where(source_lane == width + pivot_offset - target_lane, 1.0, 0.0).astype(jnp.float32),
        jnp.where(source_lane == pivot_offset - target_lane, 1.0, 0.0).astype(jnp.float32),
    )

    barrier = pltpu.get_barrier_semaphore()
    for peer in range(lon):

        @pl.when((me != peer) & (on_top | (peer == west) | (peer == east)))
        def _():
            pl.semaphore_signal(barrier, 1, device_id={"lon": peer}, device_id_type=mesh)

    @pl.when(has_south)
    def _():
        pl.semaphore_signal(barrier, 1, device_id={"lat": row - 1}, device_id_type=mesh)

    @pl.when(has_north)
    def _():
        pl.semaphore_signal(barrier, 1, device_id={"lat": row + 1}, device_id_type=mesh)

    beside = 1 if lon == 2 else 2
    pl.semaphore_wait(
        barrier,
        jnp.where(on_top, lon - 1, beside)
        + has_south.astype(jnp.int32)
        + has_north.astype(jnp.int32),
    )

    def exchange(s, source):
        wsend, esend, ssend, nsend, whalo, ehalo, shalo, nhalo, gathered, wcol, ecol, north = (
            per_stage[s]
        )
        fields = source.shape[0]
        for f in range(fields):
            for k in range(levels):
                tile = source[f, k]
                if s == 0 and f == 3:
                    wsend[f, pl.ds(k, 1), :] = jnp.zeros((1, height), jnp.float32)
                    esend[f, pl.ds(k, 1), :] = jnp.zeros((1, height), jnp.float32)
                else:
                    flipped = tile.T
                    wsend[f, pl.ds(k, 1), :] = flipped[0:1, :]
                    esend[f, pl.ds(k, 1), :] = flipped[width - 1 : width, :]
                ssend[pl.ds(f * levels + k, 1), :] = tile[0:1, :]
                nsend[pl.ds(f * levels + k, 1), :] = tile[height - 1 : height, :]
            spare = wsend.shape[1] - levels
            wsend[f, pl.ds(levels, spare), :] = jnp.zeros((spare, height), jnp.float32)
            esend[f, pl.ds(levels, spare), :] = jnp.zeros((spare, height), jnp.float32)

        def fold_copy(peer, slot):
            return pltpu.make_async_remote_copy(
                src_ref=nsend,
                dst_ref=gathered.at[slot],
                send_sem=fold_send.at[s, peer],
                recv_sem=fold_recv.at[s, slot],
                device_id={"lon": peer},
                device_id_type=mesh,
            )

        def side(i, src, dst, device):
            return pltpu.make_async_remote_copy(
                src_ref=src,
                dst_ref=dst,
                send_sem=side_send.at[s, i],
                recv_sem=side_recv.at[s, i],
                device_id=device,
                device_id_type=mesh,
            )

        to_west = side(0, wsend, ehalo, {"lon": west})
        to_east = side(1, esend, whalo, {"lon": east})
        to_south = side(2, ssend, nhalo, {"lat": row - 1})
        to_north = side(3, nsend, shalo, {"lat": row + 1})
        to_west.start()
        to_east.start()

        @pl.when(has_south)
        def _():
            to_south.start()

        @pl.when(has_north)
        def _():
            to_north.start()

        for peer in range(lon):

            @pl.when((me != peer) & on_top)
            def _():
                fold_copy(peer, me).start()

        @pl.when(on_top)
        def _():
            gathered[me] = nsend[...]

        to_west.wait()
        to_east.wait()

        edge = lax.broadcasted_iota(jnp.int32, (height, width), 1)
        for f in range(fields):
            if s == 0 and f == 3:
                wcol[f] = jnp.zeros(wcol.shape[1:], jnp.float32)
                continue
            rows = whalo.shape[1]
            spread = jnp.concatenate(
                [whalo[f], ehalo[f], jnp.zeros((width - 2 * rows, height), jnp.float32)], axis=0
            ).T
            for k in range(levels):
                west_lane = spread if k == 0 else pltpu.roll(spread, width - k, 1)
                east_lane = pltpu.roll(spread, width - 1 - rows - k, 1)
                wcol[f, k] = jnp.where(edge == 0, west_lane, east_lane)

        def finish():
            @pl.when(has_south)
            def _():
                to_south.wait_send()
                to_north.wait_recv()

            @pl.when(has_north)
            def _():
                to_north.wait_send()
                to_south.wait_recv()

            @pl.when(jnp.logical_not(has_south))
            def _():
                shalo[...] = jnp.zeros_like(shalo)

            @pl.when(jnp.logical_not(has_north))
            def _():
                nhalo[...] = jnp.zeros_like(nhalo)

            @pl.when(jnp.logical_not(on_top))
            def _():
                north[...] = nhalo[...]

            for peer in range(lon):

                @pl.when((me != peer) & on_top)
                def _():
                    fold_copy(peer, me).wait_send()
                    fold_copy(peer, peer).wait_recv()

            @pl.when(on_top)
            def _():
                ghost = jnp.dot(
                    gathered[lower],
                    reverse[0],
                    precision=lax.Precision.HIGHEST,
                    preferred_element_type=jnp.float32,
                ) + jnp.dot(
                    gathered[upper],
                    reverse[1],
                    precision=lax.Precision.HIGHEST,
                    preferred_element_type=jnp.float32,
                )
                if s == 0:
                    line = lax.broadcasted_iota(jnp.int32, ghost.shape, 0)
                    sign = jnp.ones(ghost.shape, jnp.float32)
                    for f in range(fields):
                        owned = (line >= f * levels) & (line < (f + 1) * levels)
                        sign = jnp.where(owned, signs[f], sign)
                    ghost = ghost * sign
                north[...] = ghost

        return (source, wcol, wcol, ssend, nsend), (source, wcol, wcol, shalo, north), finish

    def run(stage, finish):
        stage(False)
        finish()
        stage(True)

    state_early, state_refs, finish = exchange(0, state)
    run(
        lambda rows: upwind_kernel(state_refs if rows else state_early, upwind, anti, flow, rows),
        finish,
    )
    upwind_early, upwind_refs, finish = exchange(1, upwind)
    run(
        lambda rows: ratio_kernel(
            state_refs, upwind_refs if rows else upwind_early, flow, ratio, rows
        ),
        finish,
    )
    ratio_early, ratio_refs, finish = exchange(2, ratio)
    run(
        lambda rows: advected_kernel(
            wet, upwind, anti, ratio_refs if rows else ratio_early, advected, rows
        ),
        finish,
    )
    advected_early, advected_refs, finish = exchange(3, advected)
    final = Pair(first_out, second_out)
    run(
        lambda rows: isopycnal_kernel(
            advected_refs if rows else advected_early, state_refs, final, rows
        ),
        finish,
    )


def fused(fields, seam):
    lon = lax.axis_size("lon")
    lat = lax.axis_size("lat")
    levels, height, width = fields[0].shape
    block = jax.ShapeDtypeStruct((levels, height, width), jnp.float32)
    scratch = [
        pltpu.VMEM((2, levels, height, width), jnp.float32),
        pltpu.VMEM((4, levels, height, width), jnp.float32),
        pltpu.VMEM((2, levels, height, width), jnp.float32),
        pltpu.VMEM((8, levels, height, width), jnp.float32),
        pltpu.VMEM((4, levels, height, width), jnp.float32),
        pltpu.VMEM((levels, height, width), jnp.float32),
    ]
    for count in STAGE_FIELDS:
        scratch += buffers_for(count, levels, height, width, lon)
    stages = len(STAGE_FIELDS)
    scratch += [
        pltpu.SemaphoreType.DMA((stages, lon)),
        pltpu.SemaphoreType.DMA((stages, lon)),
        pltpu.SemaphoreType.DMA((stages, 4)),
        pltpu.SemaphoreType.DMA((stages, 4)),
    ]
    return pl.pallas_call(
        functools.partial(fused_kernel, lon, lat, STATE_SIGNS),
        out_shape=(block, block),
        in_specs=[pl.BlockSpec(memory_space=pltpu.SMEM)]
        + [pl.BlockSpec(memory_space=pltpu.VMEM)] * len(fields),
        out_specs=[pl.BlockSpec(memory_space=pltpu.VMEM)] * 2,
        scratch_shapes=scratch,
        compiler_params=pltpu.CompilerParams(
            collective_id=0, has_side_effects=True, vmem_limit_bytes=60 * 1024 * 1024
        ),
    )(seam, *fields)


def local(
    heat_content_field,
    saltiness_field,
    eastward_cfl_number,
    northward_cfl_number,
    seawater_indicator,
    submerged_layer_total,
    seam_partner_index,
):
    return fused(
        (
            heat_content_field,
            saltiness_field,
            eastward_cfl_number,
            northward_cfl_number,
            seawater_indicator,
            submerged_layer_total,
        ),
        seam_partner_index,
    )


def solution(mesh):
    in_specs = (
        P(None, "lat", "lon"),
        P(None, "lat", "lon"),
        P(None, "lat", "lon"),
        P(None, "lat", "lon"),
        P("lat", "lon"),
        P("lat", "lon"),
        P(),
    )
    out_specs = (P(None, "lat", "lon"), P(None, "lat", "lon"))
    return jax.shard_map(local, mesh=mesh, in_specs=in_specs, out_specs=out_specs, check_vma=False)
```

```python
import functools

import jax
import jax.numpy as jnp
from jax import lax
from jax.experimental import pallas as pl
from jax.experimental.pallas import tpu as pltpu
from jax.sharding import PartitionSpec as P

RATIO_FLOOR = 0.05
SLOPE_FLOOR = 0.5
SLOPE_LIMIT = 2.0
DIFFUSIVITY = 0.1
THERMAL_COEF = 0.2
HALINE_COEF = 0.8
STATE_SIGNS = (1.0, 1.0, -1.0, -1.0, 1.0)


def sign_column(values):
    return jnp.array(values, jnp.float32).reshape(len(values), 1, 1, 1)


def around(x, west, east, south, north):
    height, width = x.shape
    lane = lax.broadcasted_iota(jnp.int32, x.shape, 1)
    level = lax.broadcasted_iota(jnp.int32, x.shape, 0)
    at_east = jnp.where(lane == width - 1, east, pltpu.roll(x, width - 1, 1))
    at_west = jnp.where(lane == 0, west, pltpu.roll(x, 1, 1))
    at_north = jnp.where(level == height - 1, north, pltpu.roll(x, height - 1, 0))
    at_south = jnp.where(level == 0, south, pltpu.roll(x, 1, 0))
    return (x, at_east, at_west, at_north, at_south)


def pick_rows(low, high):
    level = lax.broadcasted_iota(jnp.int32, (2, high.shape[-1]), 0)
    return jnp.where(level == 0, low, high)


def load_view(ref, index, rows):
    if not rows:
        return ref[index]
    height = ref.shape[-2]
    return pick_rows(
        ref[index + (pl.ds(0, 1), slice(None))], ref[index + (pl.ds(height - 1, 1), slice(None))]
    )


def store_view(ref, index, value, rows):
    if not rows:
        ref[index] = value
        return
    height = ref.shape[-2]
    ref[index + (pl.ds(0, 1), slice(None))] = value[0:1]
    ref[index + (pl.ds(height - 1, 1), slice(None))] = value[1:2]


def sides_of(refs, f, k, rows=False):
    block, west, east, south, north = refs
    line = pl.ds(f * block.shape[1] + k, 1)
    if not rows:
        return around(block[f, k], west[f, k], east[f, k], south[line, :], north[line, :])
    height = west.shape[2]
    low = block[f, k, pl.ds(0, 2), :]
    high = block[f, k, pl.ds(height - 2, 2), :]
    centre = pick_rows(low[0:1], high[1:2])
    at_north = pick_rows(low[1:2], north[line, :])
    at_south = pick_rows(south[line, :], high[0:1])
    west_end = pick_rows(west[f, k, pl.ds(0, 1), :], west[f, k, pl.ds(height - 1, 1), :])
    east_end = pick_rows(east[f, k, pl.ds(0, 1), :], east[f, k, pl.ds(height - 1, 1), :])
    width = centre.shape[1]
    lane = lax.broadcasted_iota(jnp.int32, centre.shape, 1)
    at_east = jnp.where(lane == width - 1, east_end, pltpu.roll(centre, width - 1, 1))
    at_west = jnp.where(lane == 0, west_end, pltpu.roll(centre, 1, 1))
    return (centre, at_east, at_west, at_north, at_south)


def low_order(tracer, zonal, meridional, wet_sides):
    value_centre, value_east, value_west, value_north, value_south = tracer
    speed_centre, speed_west = (zonal[0], zonal[2])
    flow_centre, flow_south = (meridional[0], meridional[4])
    wet_centre, wet_east, wet_west, wet_north, wet_south = wet_sides
    face_east = wet_centre * wet_east
    face_west = wet_west * wet_centre
    face_north = wet_centre * wet_north
    face_south = wet_south * wet_centre
    upwind_east = face_east * (
        jnp.maximum(speed_centre, 0.0) * value_centre + jnp.minimum(speed_centre, 0.0) * value_east
    )
    upwind_west = face_west * (
        jnp.maximum(speed_west, 0.0) * value_west + jnp.minimum(speed_west, 0.0) * value_centre
    )
    upwind_north = face_north * (
        jnp.maximum(flow_centre, 0.0) * value_centre + jnp.minimum(flow_centre, 0.0) * value_north
    )
    upwind_south = face_south * (
        jnp.maximum(flow_south, 0.0) * value_south + jnp.minimum(flow_south, 0.0) * value_centre
    )
    anti_east = face_east * speed_centre * (value_centre + value_east) * 0.5 - upwind_east
    anti_west = face_west * speed_west * (value_west + value_centre) * 0.5 - upwind_west
    anti_north = face_north * flow_centre * (value_centre + value_north) * 0.5 - upwind_north
    anti_south = face_south * flow_south * (value_south + value_centre) * 0.5 - upwind_south
    upwind = value_centre - wet_centre * (upwind_east - upwind_west + upwind_north - upwind_south)
    inflow = (
        jnp.maximum(anti_west, 0.0)
        - jnp.minimum(anti_east, 0.0)
        + jnp.maximum(anti_south, 0.0)
        - jnp.minimum(anti_north, 0.0)
    )
    outflow = (
        jnp.maximum(anti_east, 0.0)
        - jnp.minimum(anti_west, 0.0)
        + jnp.maximum(anti_north, 0.0)
        - jnp.minimum(anti_south, 0.0)
    )
    anti = (anti_east, anti_west, anti_north, anti_south)
    return (upwind, anti, inflow, outflow)


def level_low_order(state_refs, k, tracer):
    zonal = sides_of(state_refs, 2, k)
    meridional = sides_of(state_refs, 3, k)
    wet_sides = sides_of(state_refs, 4, k)
    return low_order(sides_of(state_refs, tracer, k), zonal, meridional, wet_sides), wet_sides


def ratio_pair(upwind_sides, wet_sides, inflow, outflow):
    value_centre = upwind_sides[0]
    candidates = [value_centre] + [
        jnp.where(beside_wet > 0.5, beside, value_centre)
        for beside, beside_wet in zip(upwind_sides[1:], wet_sides[1:])
    ]
    highest = functools.reduce(jnp.maximum, candidates)
    lowest = functools.reduce(jnp.minimum, candidates)
    ratio_plus = jnp.minimum(1.0, (highest - value_centre) / jnp.maximum(inflow, RATIO_FLOOR))
    ratio_minus = jnp.minimum(1.0, (value_centre - lowest) / jnp.maximum(outflow, RATIO_FLOOR))
    return ratio_plus, ratio_minus


def limited(plus, minus, upwind, anti, wet_centre):
    plus_centre, plus_east, plus_west, plus_north, plus_south = plus
    minus_centre, minus_east, minus_west, minus_north, minus_south = minus
    anti_east, anti_west, anti_north, anti_south = anti
    coef_east = jnp.where(
        anti_east >= 0.0, jnp.minimum(plus_east, minus_centre), jnp.minimum(plus_centre, minus_east)
    )
    coef_west = jnp.where(
        anti_west >= 0.0, jnp.minimum(plus_centre, minus_west), jnp.minimum(plus_west, minus_centre)
    )
    coef_north = jnp.where(
        anti_north >= 0.0,
        jnp.minimum(plus_north, minus_centre),
        jnp.minimum(plus_centre, minus_north),
    )
    coef_south = jnp.where(
        anti_south >= 0.0,
        jnp.minimum(plus_centre, minus_south),
        jnp.minimum(plus_south, minus_centre),
    )
    return upwind - wet_centre * (
        coef_east * anti_east
        - coef_west * anti_west
        + coef_north * anti_north
        - coef_south * anti_south
    )


def upwind_kernel(state_refs, out, anti_out, flow_out, rows=False):
    levels = out.shape[1]

    def body(k, carry):
        zonal = sides_of(state_refs, 2, k, rows)
        meridional = sides_of(state_refs, 3, k, rows)
        wet_sides = sides_of(state_refs, 4, k, rows)
        for tracer in range(2):
            tracer_sides = sides_of(state_refs, tracer, k, rows)
            upwind, anti, inflow, outflow = low_order(tracer_sides, zonal, meridional, wet_sides)
            store_view(out, (tracer, k), upwind, rows)
            for face in range(4):
                store_view(anti_out, (4 * tracer + face, k), anti[face], rows)
            store_view(flow_out, (tracer, k), inflow, rows)
            store_view(flow_out, (2 + tracer, k), outflow, rows)
        return carry

    lax.fori_loop(0, levels, body, 0)


def ratio_kernel(state_refs, upwind_refs, flow, out, rows=False):
    levels = out.shape[1]

    def body(k, carry):
        wet_sides = sides_of(state_refs, 4, k, rows)
        for tracer in range(2):
            plus, minus = ratio_pair(
                sides_of(upwind_refs, tracer, k, rows),
                wet_sides,
                load_view(flow, (tracer, k), rows),
                load_view(flow, (2 + tracer, k), rows),
            )
            store_view(out, (tracer, k), plus, rows)
            store_view(out, (2 + tracer, k), minus, rows)
        return carry

    lax.fori_loop(0, levels, body, 0)


def advected_kernel(wet, upwind_ref, anti_ref, ratio_refs, out, rows=False):
    levels = out.shape[1]

    def body(k, carry):
        wet_centre = load_view(wet, (k,), rows)
        for tracer in range(2):
            anti = tuple(load_view(anti_ref, (4 * tracer + face, k), rows) for face in range(4))
            plus = sides_of(ratio_refs, tracer, k, rows)
            minus = sides_of(ratio_refs, 2 + tracer, k, rows)
            upwind = load_view(upwind_ref, (tracer, k), rows)
            store_view(out, (tracer, k), limited(plus, minus, upwind, anti, wet_centre), rows)
        return carry

    lax.fori_loop(0, levels, body, 0)


def isopycnal_kernel(advected_refs, state_refs, out, rows=False):
    levels = out.shape[1]

    def level(k):
        values = [sides_of(advected_refs, tracer, k, rows) for tracer in range(2)]
        return values, sides_of(state_refs, 4, k, rows)

    def body(pair, carry):
        k = 2 * pair
        lower, middle = level(k), level(k + 1)
        upper = level(jnp.minimum(k + 2, levels - 1))
        emit(k, lower, middle)
        emit(k + 1, middle, upper)
        return carry

    def emit(k, here, there):
        values, wet_sides = here
        uppers, wet_above = there
        stacked = [w * a for w, a in zip(wet_sides, wet_above)]
        verticals = [
            [(u - v) * s for u, v, s in zip(uppers[tracer], values[tracer], stacked)]
            for tracer in range(2)
        ]
        densities = [HALINE_COEF * s - THERMAL_COEF * t for t, s in zip(values[0], values[1])]
        stratas = [HALINE_COEF * s - THERMAL_COEF * t for t, s in zip(verticals[0], verticals[1])]
        for tracer in range(2):
            value, vertical = values[tracer], verticals[tracer]

            def face_flux(first, second):
                face = wet_sides[first] * wet_sides[second]
                slope = jnp.clip(
                    (densities[second] - densities[first])
                    / jnp.maximum(0.5 * (stratas[first] + stratas[second]), SLOPE_FLOOR),
                    -SLOPE_LIMIT,
                    SLOPE_LIMIT,
                )
                return (
                    DIFFUSIVITY
                    * face
                    * (
                        value[second]
                        - value[first]
                        - slope * 0.5 * (vertical[first] + vertical[second])
                    )
                )

            east_flux = face_flux(0, 1)
            west_flux = face_flux(2, 0)
            north_flux = face_flux(0, 3)
            south_flux = face_flux(4, 0)
            result = value[0] + wet_sides[0] * (east_flux - west_flux + north_flux - south_flux)
            store_view(out, (tracer, k), result, rows)

    lax.fori_loop(0, levels // 2, body, 0)


class Stack:
    def __init__(self, *refs):
        self.refs = refs
        self.shape = (len(refs),) + refs[0].shape

    def __getitem__(self, index):
        return self.refs[index[0]][index[1:]]


class Pair:
    def __init__(self, first, second):
        self.refs = (first, second)
        self.shape = (2,) + first.shape

    def __setitem__(self, index, value):
        self.refs[index[0]][index[1:]] = value


def buffers_for(fields, levels, height, width, lon):
    columns = pltpu.VMEM((fields, 16, height), jnp.float32)
    rows = pltpu.VMEM((fields * levels, width), jnp.float32)
    halo = pltpu.VMEM((fields, levels, height, width), jnp.float32)
    return [
        columns,
        columns,
        rows,
        rows,
        columns,
        columns,
        rows,
        rows,
        pltpu.VMEM((lon, fields * levels, width), jnp.float32),
        halo,
        halo,
        rows,
    ]


STAGE_FIELDS = (5, 2, 4, 2)


def fused_kernel(
    lon, lat, signs, seam, heat, salt, zonal, meridional, sea, depth, first_out, second_out, *scratch
):
    mesh = pl.DeviceIdType.MESH
    upwind, ratio, advected, anti, flow, wet = scratch[:6]
    count = len(STAGE_FIELDS)
    per_stage = [scratch[6 + 12 * s : 18 + 12 * s] for s in range(count)]
    fold_send, fold_recv, side_send, side_recv = scratch[6 + 12 * count :]
    me = lax.axis_index("lon")
    row = lax.axis_index("lat")
    west = lax.rem(me + lon - 1, lon)
    east = lax.rem(me + 1, lon)
    has_south = row > 0
    has_north = row < lat - 1
    on_top = row == lat - 1
    levels, height, width = heat.shape
    wet_column = sea[...] == 1
    for k in range(levels):
        wet[k] = jnp.where(wet_column & (k < depth[...]), 1.0, 0.0).astype(jnp.float32)
    state = Stack(heat, salt, zonal, meridional, wet)
    pivot = seam[0]
    pivot_block, pivot_offset = pivot // width, pivot % width
    lower = lax.rem(pivot_block - me - 1 + 2 * lon, lon)
    upper = lax.rem(pivot_block - me + 2 * lon, lon)
    source_lane = lax.broadcasted_iota(jnp.int32, (width, width), 0)
    target_lane = lax.broadcasted_iota(jnp.int32, (width, width), 1)
    reverse = (
        jnp.where(source_lane == width + pivot_offset - target_lane, 1.0, 0.0).astype(jnp.float32),
        jnp.where(source_lane == pivot_offset - target_lane, 1.0, 0.0).astype(jnp.float32),
    )

    barrier = pltpu.get_barrier_semaphore()
    for peer in range(lon):

        @pl.when((me != peer) & (on_top | (peer == west) | (peer == east)))
        def _():
            pl.semaphore_signal(barrier, 1, device_id={"lon": peer}, device_id_type=mesh)

    @pl.when(has_south)
    def _():
        pl.semaphore_signal(barrier, 1, device_id={"lat": row - 1}, device_id_type=mesh)

    @pl.when(has_north)
    def _():
        pl.semaphore_signal(barrier, 1, device_id={"lat": row + 1}, device_id_type=mesh)

    beside = 1 if lon == 2 else 2
    pl.semaphore_wait(
        barrier,
        jnp.where(on_top, lon - 1, beside)
        + has_south.astype(jnp.int32)
        + has_north.astype(jnp.int32),
    )

    def exchange(s, source):
        wsend, esend, ssend, nsend, whalo, ehalo, shalo, nhalo, gathered, wcol, ecol, north = (
            per_stage[s]
        )
        fields = source.shape[0]
        for f in range(fields):
            for k in range(levels):
                tile = source[f, k]
                if s == 0 and f == 3:
                    wsend[f, pl.ds(k, 1), :] = jnp.zeros((1, height), jnp.float32)
                    esend[f, pl.ds(k, 1), :] = jnp.zeros((1, height), jnp.float32)
                else:
                    flipped = tile.T
                    wsend[f, pl.ds(k, 1), :] = flipped[0:1, :]
                    esend[f, pl.ds(k, 1), :] = flipped[width - 1 : width, :]
                ssend[pl.ds(f * levels + k, 1), :] = tile[0:1, :]
                nsend[pl.ds(f * levels + k, 1), :] = tile[height - 1 : height, :]
            spare = wsend.shape[1] - levels
            wsend[f, pl.ds(levels, spare), :] = jnp.zeros((spare, height), jnp.float32)
            esend[f, pl.ds(levels, spare), :] = jnp.zeros((spare, height), jnp.float32)

        def fold_copy(peer, slot):
            return pltpu.make_async_remote_copy(
                src_ref=nsend,
                dst_ref=gathered.at[slot],
                send_sem=fold_send.at[s, peer],
                recv_sem=fold_recv.at[s, slot],
                device_id={"lon": peer},
                device_id_type=mesh,
            )

        def side(i, src, dst, device):
            return pltpu.make_async_remote_copy(
                src_ref=src,
                dst_ref=dst,
                send_sem=side_send.at[s, i],
                recv_sem=side_recv.at[s, i],
                device_id=device,
                device_id_type=mesh,
            )

        to_west = side(0, wsend, ehalo, {"lon": west})
        to_east = side(1, esend, whalo, {"lon": east})
        to_south = side(2, ssend, nhalo, {"lat": row - 1})
        to_north = side(3, nsend, shalo, {"lat": row + 1})
        to_west.start()
        to_east.start()

        @pl.when(has_south)
        def _():
            to_south.start()

        @pl.when(has_north)
        def _():
            to_north.start()

        for peer in range(lon):

            @pl.when((me != peer) & on_top)
            def _():
                fold_copy(peer, me).start()

        @pl.when(on_top)
        def _():
            gathered[me] = nsend[...]

        to_west.wait()
        to_east.wait()

        edge = lax.broadcasted_iota(jnp.int32, (height, width), 1)
        for f in range(fields):
            if s == 0 and f == 3:
                wcol[f] = jnp.zeros(wcol.shape[1:], jnp.float32)
                continue
            rows = whalo.shape[1]
            spread = jnp.concatenate(
                [whalo[f], ehalo[f], jnp.zeros((width - 2 * rows, height), jnp.float32)], axis=0
            ).T
            for k in range(levels):
                west_lane = spread if k == 0 else pltpu.roll(spread, width - k, 1)
                east_lane = pltpu.roll(spread, width - 1 - rows - k, 1)
                wcol[f, k] = jnp.where(edge == 0, west_lane, east_lane)

        def finish():
            @pl.when(has_south)
            def _():
                to_south.wait_send()
                to_north.wait_recv()

            @pl.when(has_north)
            def _():
                to_north.wait_send()
                to_south.wait_recv()

            @pl.when(jnp.logical_not(has_south))
            def _():
                shalo[...] = jnp.zeros_like(shalo)

            @pl.when(jnp.logical_not(has_north))
            def _():
                nhalo[...] = jnp.zeros_like(nhalo)

            @pl.when(jnp.logical_not(on_top))
            def _():
                north[...] = nhalo[...]

            for peer in range(lon):

                @pl.when((me != peer) & on_top)
                def _():
                    fold_copy(peer, me).wait_send()
                    fold_copy(peer, peer).wait_recv()

            @pl.when(on_top)
            def _():
                ghost = jnp.dot(
                    gathered[lower],
                    reverse[0],
                    precision=lax.Precision.HIGHEST,
                    preferred_element_type=jnp.float32,
                ) + jnp.dot(
                    gathered[upper],
                    reverse[1],
                    precision=lax.Precision.HIGHEST,
                    preferred_element_type=jnp.float32,
                )
                if s == 0:
                    line = lax.broadcasted_iota(jnp.int32, ghost.shape, 0)
                    sign = jnp.ones(ghost.shape, jnp.float32)
                    for f in range(fields):
                        owned = (line >= f * levels) & (line < (f + 1) * levels)
                        sign = jnp.where(owned, signs[f], sign)
                    ghost = ghost * sign
                north[...] = ghost

        return (source, wcol, wcol, ssend, nsend), (source, wcol, wcol, shalo, north), finish

    def run(stage, finish):
        stage(False)
        finish()
        stage(True)

    state_early, state_refs, finish = exchange(0, state)
    run(
        lambda rows: upwind_kernel(state_refs if rows else state_early, upwind, anti, flow, rows),
        finish,
    )
    upwind_early, upwind_refs, finish = exchange(1, upwind)
    run(
        lambda rows: ratio_kernel(
            state_refs, upwind_refs if rows else upwind_early, flow, ratio, rows
        ),
        finish,
    )
    ratio_early, ratio_refs, finish = exchange(2, ratio)
    run(
        lambda rows: advected_kernel(
            wet, upwind, anti, ratio_refs if rows else ratio_early, advected, rows
        ),
        finish,
    )
    advected_early, advected_refs, finish = exchange(3, advected)
    final = Pair(first_out, second_out)
    run(
        lambda rows: isopycnal_kernel(
            advected_refs if rows else advected_early, state_refs, final, rows
        ),
        finish,
    )


def fused(fields, seam):
    lon = lax.axis_size("lon")
    lat = lax.axis_size("lat")
    levels, height, width = fields[0].shape
    block = jax.ShapeDtypeStruct((levels, height, width), jnp.float32)
    scratch = [
        pltpu.VMEM((2, levels, height, width), jnp.float32),
        pltpu.VMEM((4, levels, height, width), jnp.float32),
        pltpu.VMEM((2, levels, height, width), jnp.float32),
        pltpu.VMEM((8, levels, height, width), jnp.float32),
        pltpu.VMEM((4, levels, height, width), jnp.float32),
        pltpu.VMEM((levels, height, width), jnp.float32),
    ]
    for count in STAGE_FIELDS:
        scratch += buffers_for(count, levels, height, width, lon)
    stages = len(STAGE_FIELDS)
    scratch += [
        pltpu.SemaphoreType.DMA((stages, lon)),
        pltpu.SemaphoreType.DMA((stages, lon)),
        pltpu.SemaphoreType.DMA((stages, 4)),
        pltpu.SemaphoreType.DMA((stages, 4)),
    ]
    return pl.pallas_call(
        functools.partial(fused_kernel, lon, lat, STATE_SIGNS),
        out_shape=(block, block),
        in_specs=[pl.BlockSpec(memory_space=pltpu.SMEM)]
        + [pl.BlockSpec(memory_space=pltpu.VMEM)] * len(fields),
        out_specs=[pl.BlockSpec(memory_space=pltpu.VMEM)] * 2,
        scratch_shapes=scratch,
        compiler_params=pltpu.CompilerParams(
            collective_id=0, has_side_effects=True, vmem_limit_bytes=60 * 1024 * 1024
        ),
    )(seam, *fields)


def local(
    heat_content_field,
    saltiness_field,
    eastward_cfl_number,
    northward_cfl_number,
    seawater_indicator,
    submerged_layer_total,
    seam_partner_index,
):
    return fused(
        (
            heat_content_field,
            saltiness_field,
            eastward_cfl_number,
            northward_cfl_number,
            seawater_indicator,
            submerged_layer_total,
        ),
        seam_partner_index,
    )


def solution(mesh):
    in_specs = (
        P(None, "lat", "lon"),
        P(None, "lat", "lon"),
        P(None, "lat", "lon"),
        P(None, "lat", "lon"),
        P("lat", "lon"),
        P("lat", "lon"),
        P(),
    )
    out_specs = (P(None, "lat", "lon"), P(None, "lat", "lon"))
    return jax.shard_map(local, mesh=mesh, in_specs=in_specs, out_specs=out_specs, check_vma=False)
```

```python
import functools

import jax
import jax.numpy as jnp
from jax import lax
from jax.experimental import pallas as pl
from jax.experimental.pallas import tpu as pltpu
from jax.sharding import PartitionSpec as P

RATIO_FLOOR = 0.05
SLOPE_FLOOR = 0.5
SLOPE_LIMIT = 2.0
DIFFUSIVITY = 0.1
THERMAL_COEF = 0.2
HALINE_COEF = 0.8
STATE_SIGNS = (1.0, 1.0, -1.0, -1.0, 1.0)


def sign_column(values):
    return jnp.array(values, jnp.float32).reshape(len(values), 1, 1, 1)


def around(x, west, east, south, north):
    height, width = x.shape
    lane = lax.broadcasted_iota(jnp.int32, x.shape, 1)
    level = lax.broadcasted_iota(jnp.int32, x.shape, 0)
    at_east = jnp.where(lane == width - 1, east, pltpu.roll(x, width - 1, 1))
    at_west = jnp.where(lane == 0, west, pltpu.roll(x, 1, 1))
    at_north = jnp.where(level == height - 1, north, pltpu.roll(x, height - 1, 0))
    at_south = jnp.where(level == 0, south, pltpu.roll(x, 1, 0))
    return (x, at_east, at_west, at_north, at_south)


def pick_rows(low, high):
    level = lax.broadcasted_iota(jnp.int32, (2, high.shape[-1]), 0)
    return jnp.where(level == 0, low, high)


def load_view(ref, index, rows):
    if not rows:
        return ref[index]
    height = ref.shape[-2]
    return pick_rows(
        ref[index + (pl.ds(0, 1), slice(None))], ref[index + (pl.ds(height - 1, 1), slice(None))]
    )


def store_view(ref, index, value, rows):
    if not rows:
        ref[index] = value
        return
    height = ref.shape[-2]
    ref[index + (pl.ds(0, 1), slice(None))] = value[0:1]
    ref[index + (pl.ds(height - 1, 1), slice(None))] = value[1:2]


def sides_of(refs, f, k, rows=False):
    block, west, east, south, north = refs
    line = pl.ds(f * block.shape[1] + k, 1)
    if not rows:
        return around(block[f, k], west[f, k], east[f, k], south[line, :], north[line, :])
    height = west.shape[2]
    low = block[f, k, pl.ds(0, 2), :]
    high = block[f, k, pl.ds(height - 2, 2), :]
    centre = pick_rows(low[0:1], high[1:2])
    at_north = pick_rows(low[1:2], north[line, :])
    at_south = pick_rows(south[line, :], high[0:1])
    west_end = pick_rows(west[f, k, pl.ds(0, 1), :], west[f, k, pl.ds(height - 1, 1), :])
    east_end = pick_rows(east[f, k, pl.ds(0, 1), :], east[f, k, pl.ds(height - 1, 1), :])
    width = centre.shape[1]
    lane = lax.broadcasted_iota(jnp.int32, centre.shape, 1)
    at_east = jnp.where(lane == width - 1, east_end, pltpu.roll(centre, width - 1, 1))
    at_west = jnp.where(lane == 0, west_end, pltpu.roll(centre, 1, 1))
    return (centre, at_east, at_west, at_north, at_south)


def low_order(tracer, zonal, meridional, wet_sides):
    value_centre, value_east, value_west, value_north, value_south = tracer
    speed_centre, speed_west = (zonal[0], zonal[2])
    flow_centre, flow_south = (meridional[0], meridional[4])
    wet_centre, wet_east, wet_west, wet_north, wet_south = wet_sides
    face_east = wet_centre * wet_east
    face_west = wet_west * wet_centre
    face_north = wet_centre * wet_north
    face_south = wet_south * wet_centre
    upwind_east = face_east * (
        jnp.maximum(speed_centre, 0.0) * value_centre + jnp.minimum(speed_centre, 0.0) * value_east
    )
    upwind_west = face_west * (
        jnp.maximum(speed_west, 0.0) * value_west + jnp.minimum(speed_west, 0.0) * value_centre
    )
    upwind_north = face_north * (
        jnp.maximum(flow_centre, 0.0) * value_centre + jnp.minimum(flow_centre, 0.0) * value_north
    )
    upwind_south = face_south * (
        jnp.maximum(flow_south, 0.0) * value_south + jnp.minimum(flow_south, 0.0) * value_centre
    )
    anti_east = face_east * speed_centre * (value_centre + value_east) * 0.5 - upwind_east
    anti_west = face_west * speed_west * (value_west + value_centre) * 0.5 - upwind_west
    anti_north = face_north * flow_centre * (value_centre + value_north) * 0.5 - upwind_north
    anti_south = face_south * flow_south * (value_south + value_centre) * 0.5 - upwind_south
    upwind = value_centre - wet_centre * (upwind_east - upwind_west + upwind_north - upwind_south)
    inflow = (
        jnp.maximum(anti_west, 0.0)
        - jnp.minimum(anti_east, 0.0)
        + jnp.maximum(anti_south, 0.0)
        - jnp.minimum(anti_north, 0.0)
    )
    outflow = (
        jnp.maximum(anti_east, 0.0)
        - jnp.minimum(anti_west, 0.0)
        + jnp.maximum(anti_north, 0.0)
        - jnp.minimum(anti_south, 0.0)
    )
    anti = (anti_east, anti_west, anti_north, anti_south)
    return (upwind, anti, inflow, outflow)


def level_low_order(state_refs, k, tracer):
    zonal = sides_of(state_refs, 2, k)
    meridional = sides_of(state_refs, 3, k)
    wet_sides = sides_of(state_refs, 4, k)
    return low_order(sides_of(state_refs, tracer, k), zonal, meridional, wet_sides), wet_sides


def ratio_pair(upwind_sides, wet_sides, inflow, outflow):
    value_centre = upwind_sides[0]
    candidates = [value_centre] + [
        jnp.where(beside_wet > 0.5, beside, value_centre)
        for beside, beside_wet in zip(upwind_sides[1:], wet_sides[1:])
    ]
    highest = functools.reduce(jnp.maximum, candidates)
    lowest = functools.reduce(jnp.minimum, candidates)
    ratio_plus = jnp.minimum(1.0, (highest - value_centre) / jnp.maximum(inflow, RATIO_FLOOR))
    ratio_minus = jnp.minimum(1.0, (value_centre - lowest) / jnp.maximum(outflow, RATIO_FLOOR))
    return ratio_plus, ratio_minus


def limited(plus, minus, upwind, anti, wet_centre):
    plus_centre, plus_east, plus_west, plus_north, plus_south = plus
    minus_centre, minus_east, minus_west, minus_north, minus_south = minus
    anti_east, anti_west, anti_north, anti_south = anti
    coef_east = jnp.where(
        anti_east >= 0.0, jnp.minimum(plus_east, minus_centre), jnp.minimum(plus_centre, minus_east)
    )
    coef_west = jnp.where(
        anti_west >= 0.0, jnp.minimum(plus_centre, minus_west), jnp.minimum(plus_west, minus_centre)
    )
    coef_north = jnp.where(
        anti_north >= 0.0,
        jnp.minimum(plus_north, minus_centre),
        jnp.minimum(plus_centre, minus_north),
    )
    coef_south = jnp.where(
        anti_south >= 0.0,
        jnp.minimum(plus_centre, minus_south),
        jnp.minimum(plus_south, minus_centre),
    )
    return upwind - wet_centre * (
        coef_east * anti_east
        - coef_west * anti_west
        + coef_north * anti_north
        - coef_south * anti_south
    )


def upwind_kernel(state_refs, out, anti_out, flow_out, rows=False):
    levels = out.shape[1]

    def body(k, carry):
        zonal = sides_of(state_refs, 2, k, rows)
        meridional = sides_of(state_refs, 3, k, rows)
        wet_sides = sides_of(state_refs, 4, k, rows)
        for tracer in range(2):
            tracer_sides = sides_of(state_refs, tracer, k, rows)
            upwind, anti, inflow, outflow = low_order(tracer_sides, zonal, meridional, wet_sides)
            store_view(out, (tracer, k), upwind, rows)
            for face in range(4):
                store_view(anti_out, (4 * tracer + face, k), anti[face], rows)
            store_view(flow_out, (tracer, k), inflow, rows)
            store_view(flow_out, (2 + tracer, k), outflow, rows)
        return carry

    lax.fori_loop(0, levels, body, 0, unroll=2)


def ratio_kernel(state_refs, upwind_refs, flow, out, rows=False):
    levels = out.shape[1]

    def body(k, carry):
        wet_sides = sides_of(state_refs, 4, k, rows)
        for tracer in range(2):
            plus, minus = ratio_pair(
                sides_of(upwind_refs, tracer, k, rows),
                wet_sides,
                load_view(flow, (tracer, k), rows),
                load_view(flow, (2 + tracer, k), rows),
            )
            store_view(out, (tracer, k), plus, rows)
            store_view(out, (2 + tracer, k), minus, rows)
        return carry

    lax.fori_loop(0, levels, body, 0, unroll=2)


def advected_kernel(wet, upwind_ref, anti_ref, ratio_refs, out, rows=False):
    levels = out.shape[1]

    def body(k, carry):
        wet_centre = load_view(wet, (k,), rows)
        for tracer in range(2):
            anti = tuple(load_view(anti_ref, (4 * tracer + face, k), rows) for face in range(4))
            plus = sides_of(ratio_refs, tracer, k, rows)
            minus = sides_of(ratio_refs, 2 + tracer, k, rows)
            upwind = load_view(upwind_ref, (tracer, k), rows)
            store_view(out, (tracer, k), limited(plus, minus, upwind, anti, wet_centre), rows)
        return carry

    lax.fori_loop(0, levels, body, 0, unroll=2)


def isopycnal_kernel(advected_refs, state_refs, out, rows=False):
    levels = out.shape[1]

    def level(k):
        values = [sides_of(advected_refs, tracer, k, rows) for tracer in range(2)]
        return values, sides_of(state_refs, 4, k, rows)

    def body(pair, carry):
        k = 2 * pair
        lower, middle = level(k), level(k + 1)
        upper = level(jnp.minimum(k + 2, levels - 1))
        emit(k, lower, middle)
        emit(k + 1, middle, upper)
        return carry

    def emit(k, here, there):
        values, wet_sides = here
        uppers, wet_above = there
        stacked = [w * a for w, a in zip(wet_sides, wet_above)]
        verticals = [
            [(u - v) * s for u, v, s in zip(uppers[tracer], values[tracer], stacked)]
            for tracer in range(2)
        ]
        densities = [HALINE_COEF * s - THERMAL_COEF * t for t, s in zip(values[0], values[1])]
        stratas = [HALINE_COEF * s - THERMAL_COEF * t for t, s in zip(verticals[0], verticals[1])]
        for tracer in range(2):
            value, vertical = values[tracer], verticals[tracer]

            def face_flux(first, second):
                face = wet_sides[first] * wet_sides[second]
                slope = jnp.clip(
                    (densities[second] - densities[first])
                    / jnp.maximum(0.5 * (stratas[first] + stratas[second]), SLOPE_FLOOR),
                    -SLOPE_LIMIT,
                    SLOPE_LIMIT,
                )
                return (
                    DIFFUSIVITY
                    * face
                    * (
                        value[second]
                        - value[first]
                        - slope * 0.5 * (vertical[first] + vertical[second])
                    )
                )

            east_flux = face_flux(0, 1)
            west_flux = face_flux(2, 0)
            north_flux = face_flux(0, 3)
            south_flux = face_flux(4, 0)
            result = value[0] + wet_sides[0] * (east_flux - west_flux + north_flux - south_flux)
            store_view(out, (tracer, k), result, rows)

    lax.fori_loop(0, levels // 2, body, 0)


class Stack:
    def __init__(self, *refs):
        self.refs = refs
        self.shape = (len(refs),) + refs[0].shape

    def __getitem__(self, index):
        return self.refs[index[0]][index[1:]]


class Pair:
    def __init__(self, first, second):
        self.refs = (first, second)
        self.shape = (2,) + first.shape

    def __setitem__(self, index, value):
        self.refs[index[0]][index[1:]] = value


def buffers_for(fields, levels, height, width, lon):
    columns = pltpu.VMEM((fields, 16, height), jnp.float32)
    rows = pltpu.VMEM((fields * levels, width), jnp.float32)
    halo = pltpu.VMEM((fields, levels, height, width), jnp.float32)
    return [
        columns,
        columns,
        rows,
        rows,
        columns,
        columns,
        rows,
        rows,
        pltpu.VMEM((lon, fields * levels, width), jnp.float32),
        halo,
        halo,
        rows,
    ]


STAGE_FIELDS = (5, 2, 4, 2)


def fused_kernel(
    lon, lat, signs, seam, heat, salt, zonal, meridional, sea, depth, first_out, second_out, *scratch
):
    mesh = pl.DeviceIdType.MESH
    upwind, ratio, advected, anti, flow, wet = scratch[:6]
    count = len(STAGE_FIELDS)
    per_stage = [scratch[6 + 12 * s : 18 + 12 * s] for s in range(count)]
    fold_send, fold_recv, side_send, side_recv = scratch[6 + 12 * count :]
    me = lax.axis_index("lon")
    row = lax.axis_index("lat")
    west = lax.rem(me + lon - 1, lon)
    east = lax.rem(me + 1, lon)
    has_south = row > 0
    has_north = row < lat - 1
    on_top = row == lat - 1
    levels, height, width = heat.shape
    wet_column = sea[...] == 1
    for k in range(levels):
        wet[k] = jnp.where(wet_column & (k < depth[...]), 1.0, 0.0).astype(jnp.float32)
    state = Stack(heat, salt, zonal, meridional, wet)
    pivot = seam[0]
    pivot_block, pivot_offset = pivot // width, pivot % width
    lower = lax.rem(pivot_block - me - 1 + 2 * lon, lon)
    upper = lax.rem(pivot_block - me + 2 * lon, lon)
    source_lane = lax.broadcasted_iota(jnp.int32, (width, width), 0)
    target_lane = lax.broadcasted_iota(jnp.int32, (width, width), 1)
    reverse = (
        jnp.where(source_lane == width + pivot_offset - target_lane, 1.0, 0.0).astype(jnp.float32),
        jnp.where(source_lane == pivot_offset - target_lane, 1.0, 0.0).astype(jnp.float32),
    )

    barrier = pltpu.get_barrier_semaphore()
    for peer in range(lon):

        @pl.when((me != peer) & (on_top | (peer == west) | (peer == east)))
        def _():
            pl.semaphore_signal(barrier, 1, device_id={"lon": peer}, device_id_type=mesh)

    @pl.when(has_south)
    def _():
        pl.semaphore_signal(barrier, 1, device_id={"lat": row - 1}, device_id_type=mesh)

    @pl.when(has_north)
    def _():
        pl.semaphore_signal(barrier, 1, device_id={"lat": row + 1}, device_id_type=mesh)

    beside = 1 if lon == 2 else 2
    pl.semaphore_wait(
        barrier,
        jnp.where(on_top, lon - 1, beside)
        + has_south.astype(jnp.int32)
        + has_north.astype(jnp.int32),
    )

    def exchange(s, source):
        wsend, esend, ssend, nsend, whalo, ehalo, shalo, nhalo, gathered, wcol, ecol, north = (
            per_stage[s]
        )
        fields = source.shape[0]
        for f in range(fields):
            for k in range(levels):
                tile = source[f, k]
                if s == 0 and f == 3:
                    wsend[f, pl.ds(k, 1), :] = jnp.zeros((1, height), jnp.float32)
                    esend[f, pl.ds(k, 1), :] = jnp.zeros((1, height), jnp.float32)
                else:
                    flipped = tile.T
                    wsend[f, pl.ds(k, 1), :] = flipped[0:1, :]
                    esend[f, pl.ds(k, 1), :] = flipped[width - 1 : width, :]
                ssend[pl.ds(f * levels + k, 1), :] = tile[0:1, :]
                nsend[pl.ds(f * levels + k, 1), :] = tile[height - 1 : height, :]
            spare = wsend.shape[1] - levels
            wsend[f, pl.ds(levels, spare), :] = jnp.zeros((spare, height), jnp.float32)
            esend[f, pl.ds(levels, spare), :] = jnp.zeros((spare, height), jnp.float32)

        def fold_copy(peer, slot):
            return pltpu.make_async_remote_copy(
                src_ref=nsend,
                dst_ref=gathered.at[slot],
                send_sem=fold_send.at[s, peer],
                recv_sem=fold_recv.at[s, slot],
                device_id={"lon": peer},
                device_id_type=mesh,
            )

        def side(i, src, dst, device):
            return pltpu.make_async_remote_copy(
                src_ref=src,
                dst_ref=dst,
                send_sem=side_send.at[s, i],
                recv_sem=side_recv.at[s, i],
                device_id=device,
                device_id_type=mesh,
            )

        to_west = side(0, wsend, ehalo, {"lon": west})
        to_east = side(1, esend, whalo, {"lon": east})
        to_south = side(2, ssend, nhalo, {"lat": row - 1})
        to_north = side(3, nsend, shalo, {"lat": row + 1})
        to_west.start()
        to_east.start()

        @pl.when(has_south)
        def _():
            to_south.start()

        @pl.when(has_north)
        def _():
            to_north.start()

        for peer in range(lon):

            @pl.when((me != peer) & on_top)
            def _():
                fold_copy(peer, me).start()

        @pl.when(on_top)
        def _():
            gathered[me] = nsend[...]

        to_west.wait()
        to_east.wait()

        edge = lax.broadcasted_iota(jnp.int32, (height, width), 1)
        for f in range(fields):
            if s == 0 and f == 3:
                wcol[f] = jnp.zeros(wcol.shape[1:], jnp.float32)
                continue
            rows = whalo.shape[1]
            spread = jnp.concatenate(
                [whalo[f], ehalo[f], jnp.zeros((width - 2 * rows, height), jnp.float32)], axis=0
            ).T
            for k in range(levels):
                west_lane = spread if k == 0 else pltpu.roll(spread, width - k, 1)
                east_lane = pltpu.roll(spread, width - 1 - rows - k, 1)
                wcol[f, k] = jnp.where(edge == 0, west_lane, east_lane)

        def finish():
            @pl.when(has_south)
            def _():
                to_south.wait_send()
                to_north.wait_recv()

            @pl.when(has_north)
            def _():
                to_north.wait_send()
                to_south.wait_recv()

            @pl.when(jnp.logical_not(has_south))
            def _():
                shalo[...] = jnp.zeros_like(shalo)

            @pl.when(jnp.logical_not(has_north))
            def _():
                nhalo[...] = jnp.zeros_like(nhalo)

            @pl.when(jnp.logical_not(on_top))
            def _():
                north[...] = nhalo[...]

            for peer in range(lon):

                @pl.when((me != peer) & on_top)
                def _():
                    fold_copy(peer, me).wait_send()
                    fold_copy(peer, peer).wait_recv()

            @pl.when(on_top)
            def _():
                ghost = jnp.dot(
                    gathered[lower],
                    reverse[0],
                    precision=lax.Precision.HIGHEST,
                    preferred_element_type=jnp.float32,
                ) + jnp.dot(
                    gathered[upper],
                    reverse[1],
                    precision=lax.Precision.HIGHEST,
                    preferred_element_type=jnp.float32,
                )
                if s == 0:
                    line = lax.broadcasted_iota(jnp.int32, ghost.shape, 0)
                    sign = jnp.ones(ghost.shape, jnp.float32)
                    for f in range(fields):
                        owned = (line >= f * levels) & (line < (f + 1) * levels)
                        sign = jnp.where(owned, signs[f], sign)
                    ghost = ghost * sign
                north[...] = ghost

        return (source, wcol, wcol, ssend, nsend), (source, wcol, wcol, shalo, north), finish

    def run(stage, finish):
        stage(False)
        finish()
        stage(True)

    state_early, state_refs, finish = exchange(0, state)
    run(
        lambda rows: upwind_kernel(state_refs if rows else state_early, upwind, anti, flow, rows),
        finish,
    )
    upwind_early, upwind_refs, finish = exchange(1, upwind)
    run(
        lambda rows: ratio_kernel(
            state_refs, upwind_refs if rows else upwind_early, flow, ratio, rows
        ),
        finish,
    )
    ratio_early, ratio_refs, finish = exchange(2, ratio)
    run(
        lambda rows: advected_kernel(
            wet, upwind, anti, ratio_refs if rows else ratio_early, advected, rows
        ),
        finish,
    )
    advected_early, advected_refs, finish = exchange(3, advected)
    final = Pair(first_out, second_out)
    run(
        lambda rows: isopycnal_kernel(
            advected_refs if rows else advected_early, state_refs, final, rows
        ),
        finish,
    )


def fused(fields, seam):
    lon = lax.axis_size("lon")
    lat = lax.axis_size("lat")
    levels, height, width = fields[0].shape
    block = jax.ShapeDtypeStruct((levels, height, width), jnp.float32)
    scratch = [
        pltpu.VMEM((2, levels, height, width), jnp.float32),
        pltpu.VMEM((4, levels, height, width), jnp.float32),
        pltpu.VMEM((2, levels, height, width), jnp.float32),
        pltpu.VMEM((8, levels, height, width), jnp.float32),
        pltpu.VMEM((4, levels, height, width), jnp.float32),
        pltpu.VMEM((levels, height, width), jnp.float32),
    ]
    for count in STAGE_FIELDS:
        scratch += buffers_for(count, levels, height, width, lon)
    stages = len(STAGE_FIELDS)
    scratch += [
        pltpu.SemaphoreType.DMA((stages, lon)),
        pltpu.SemaphoreType.DMA((stages, lon)),
        pltpu.SemaphoreType.DMA((stages, 4)),
        pltpu.SemaphoreType.DMA((stages, 4)),
    ]
    return pl.pallas_call(
        functools.partial(fused_kernel, lon, lat, STATE_SIGNS),
        out_shape=(block, block),
        in_specs=[pl.BlockSpec(memory_space=pltpu.SMEM)]
        + [pl.BlockSpec(memory_space=pltpu.VMEM)] * len(fields),
        out_specs=[pl.BlockSpec(memory_space=pltpu.VMEM)] * 2,
        scratch_shapes=scratch,
        compiler_params=pltpu.CompilerParams(
            collective_id=0, has_side_effects=True, vmem_limit_bytes=60 * 1024 * 1024
        ),
    )(seam, *fields)


def local(
    heat_content_field,
    saltiness_field,
    eastward_cfl_number,
    northward_cfl_number,
    seawater_indicator,
    submerged_layer_total,
    seam_partner_index,
):
    return fused(
        (
            heat_content_field,
            saltiness_field,
            eastward_cfl_number,
            northward_cfl_number,
            seawater_indicator,
            submerged_layer_total,
        ),
        seam_partner_index,
    )


def solution(mesh):
    in_specs = (
        P(None, "lat", "lon"),
        P(None, "lat", "lon"),
        P(None, "lat", "lon"),
        P(None, "lat", "lon"),
        P("lat", "lon"),
        P("lat", "lon"),
        P(),
    )
    out_specs = (P(None, "lat", "lon"), P(None, "lat", "lon"))
    return jax.shard_map(local, mesh=mesh, in_specs=in_specs, out_specs=out_specs, check_vma=False)
```

```python
import functools

import jax
import jax.numpy as jnp
from jax import lax
from jax.experimental import pallas as pl
from jax.experimental.pallas import tpu as pltpu
from jax.sharding import PartitionSpec as P

RATIO_FLOOR = 0.05
SLOPE_FLOOR = 0.5
SLOPE_LIMIT = 2.0
DIFFUSIVITY = 0.1
THERMAL_COEF = 0.2
HALINE_COEF = 0.8
STATE_SIGNS = (1.0, 1.0, -1.0, -1.0, 1.0)


def sign_column(values):
    return jnp.array(values, jnp.float32).reshape(len(values), 1, 1, 1)


def around(x, west, east, south, north):
    height, width = x.shape
    lane = lax.broadcasted_iota(jnp.int32, x.shape, 1)
    level = lax.broadcasted_iota(jnp.int32, x.shape, 0)
    at_east = jnp.where(lane == width - 1, east, pltpu.roll(x, width - 1, 1))
    at_west = jnp.where(lane == 0, west, pltpu.roll(x, 1, 1))
    at_north = jnp.where(level == height - 1, north, pltpu.roll(x, height - 1, 0))
    at_south = jnp.where(level == 0, south, pltpu.roll(x, 1, 0))
    return (x, at_east, at_west, at_north, at_south)


def pick_rows(low, high):
    level = lax.broadcasted_iota(jnp.int32, (2, high.shape[-1]), 0)
    return jnp.where(level == 0, low, high)


def load_view(ref, index, rows):
    if not rows:
        return ref[index]
    height = ref.shape[-2]
    return pick_rows(
        ref[index + (pl.ds(0, 1), slice(None))], ref[index + (pl.ds(height - 1, 1), slice(None))]
    )


def store_view(ref, index, value, rows):
    if not rows:
        ref[index] = value
        return
    height = ref.shape[-2]
    ref[index + (pl.ds(0, 1), slice(None))] = value[0:1]
    ref[index + (pl.ds(height - 1, 1), slice(None))] = value[1:2]


def sides_of(refs, f, k, rows=False):
    block, west, east, south, north = refs
    line = pl.ds(f * block.shape[1] + k, 1)
    if not rows:
        return around(block[f, k], west[f, k], east[f, k], south[line, :], north[line, :])
    height = west.shape[2]
    low = block[f, k, pl.ds(0, 2), :]
    high = block[f, k, pl.ds(height - 2, 2), :]
    centre = pick_rows(low[0:1], high[1:2])
    at_north = pick_rows(low[1:2], north[line, :])
    at_south = pick_rows(south[line, :], high[0:1])
    west_end = pick_rows(west[f, k, pl.ds(0, 1), :], west[f, k, pl.ds(height - 1, 1), :])
    east_end = pick_rows(east[f, k, pl.ds(0, 1), :], east[f, k, pl.ds(height - 1, 1), :])
    width = centre.shape[1]
    lane = lax.broadcasted_iota(jnp.int32, centre.shape, 1)
    at_east = jnp.where(lane == width - 1, east_end, pltpu.roll(centre, width - 1, 1))
    at_west = jnp.where(lane == 0, west_end, pltpu.roll(centre, 1, 1))
    return (centre, at_east, at_west, at_north, at_south)


def low_order(tracer, zonal, meridional, wet_sides):
    value_centre, value_east, value_west, value_north, value_south = tracer
    speed_centre, speed_west = (zonal[0], zonal[2])
    flow_centre, flow_south = (meridional[0], meridional[4])
    wet_centre, wet_east, wet_west, wet_north, wet_south = wet_sides
    face_east = wet_centre * wet_east
    face_west = wet_west * wet_centre
    face_north = wet_centre * wet_north
    face_south = wet_south * wet_centre
    upwind_east = face_east * (
        jnp.maximum(speed_centre, 0.0) * value_centre + jnp.minimum(speed_centre, 0.0) * value_east
    )
    upwind_west = face_west * (
        jnp.maximum(speed_west, 0.0) * value_west + jnp.minimum(speed_west, 0.0) * value_centre
    )
    upwind_north = face_north * (
        jnp.maximum(flow_centre, 0.0) * value_centre + jnp.minimum(flow_centre, 0.0) * value_north
    )
    upwind_south = face_south * (
        jnp.maximum(flow_south, 0.0) * value_south + jnp.minimum(flow_south, 0.0) * value_centre
    )
    anti_east = face_east * speed_centre * (value_centre + value_east) * 0.5 - upwind_east
    anti_west = face_west * speed_west * (value_west + value_centre) * 0.5 - upwind_west
    anti_north = face_north * flow_centre * (value_centre + value_north) * 0.5 - upwind_north
    anti_south = face_south * flow_south * (value_south + value_centre) * 0.5 - upwind_south
    upwind = value_centre - wet_centre * (upwind_east - upwind_west + upwind_north - upwind_south)
    inflow = (
        jnp.maximum(anti_west, 0.0)
        - jnp.minimum(anti_east, 0.0)
        + jnp.maximum(anti_south, 0.0)
        - jnp.minimum(anti_north, 0.0)
    )
    outflow = (
        jnp.maximum(anti_east, 0.0)
        - jnp.minimum(anti_west, 0.0)
        + jnp.maximum(anti_north, 0.0)
        - jnp.minimum(anti_south, 0.0)
    )
    anti = (anti_east, anti_west, anti_north, anti_south)
    return (upwind, anti, inflow, outflow)


def level_low_order(state_refs, k, tracer):
    zonal = sides_of(state_refs, 2, k)
    meridional = sides_of(state_refs, 3, k)
    wet_sides = sides_of(state_refs, 4, k)
    return low_order(sides_of(state_refs, tracer, k), zonal, meridional, wet_sides), wet_sides


def ratio_pair(upwind_sides, wet_sides, inflow, outflow):
    value_centre = upwind_sides[0]
    candidates = [value_centre] + [
        jnp.where(beside_wet > 0.5, beside, value_centre)
        for beside, beside_wet in zip(upwind_sides[1:], wet_sides[1:])
    ]
    highest = functools.reduce(jnp.maximum, candidates)
    lowest = functools.reduce(jnp.minimum, candidates)
    ratio_plus = jnp.minimum(1.0, (highest - value_centre) / jnp.maximum(inflow, RATIO_FLOOR))
    ratio_minus = jnp.minimum(1.0, (value_centre - lowest) / jnp.maximum(outflow, RATIO_FLOOR))
    return ratio_plus, ratio_minus


def limited(plus, minus, upwind, anti, wet_centre):
    plus_centre, plus_east, plus_west, plus_north, plus_south = plus
    minus_centre, minus_east, minus_west, minus_north, minus_south = minus
    anti_east, anti_west, anti_north, anti_south = anti
    coef_east = jnp.where(
        anti_east >= 0.0, jnp.minimum(plus_east, minus_centre), jnp.minimum(plus_centre, minus_east)
    )
    coef_west = jnp.where(
        anti_west >= 0.0, jnp.minimum(plus_centre, minus_west), jnp.minimum(plus_west, minus_centre)
    )
    coef_north = jnp.where(
        anti_north >= 0.0,
        jnp.minimum(plus_north, minus_centre),
        jnp.minimum(plus_centre, minus_north),
    )
    coef_south = jnp.where(
        anti_south >= 0.0,
        jnp.minimum(plus_centre, minus_south),
        jnp.minimum(plus_south, minus_centre),
    )
    return upwind - wet_centre * (
        coef_east * anti_east
        - coef_west * anti_west
        + coef_north * anti_north
        - coef_south * anti_south
    )


def upwind_kernel(state_refs, out, anti_out, flow_out, rows=False):
    levels = out.shape[1]

    def body(k, carry):
        zonal = sides_of(state_refs, 2, k, rows)
        meridional = sides_of(state_refs, 3, k, rows)
        wet_sides = sides_of(state_refs, 4, k, rows)
        for tracer in range(2):
            tracer_sides = sides_of(state_refs, tracer, k, rows)
            upwind, anti, inflow, outflow = low_order(tracer_sides, zonal, meridional, wet_sides)
            store_view(out, (tracer, k), upwind, rows)
            for face in range(4):
                store_view(anti_out, (4 * tracer + face, k), anti[face], rows)
            store_view(flow_out, (tracer, k), inflow, rows)
            store_view(flow_out, (2 + tracer, k), outflow, rows)
        return carry

    lax.fori_loop(0, levels, body, 0, unroll=3)


def ratio_kernel(state_refs, upwind_refs, flow, out, rows=False):
    levels = out.shape[1]

    def body(k, carry):
        wet_sides = sides_of(state_refs, 4, k, rows)
        for tracer in range(2):
            plus, minus = ratio_pair(
                sides_of(upwind_refs, tracer, k, rows),
                wet_sides,
                load_view(flow, (tracer, k), rows),
                load_view(flow, (2 + tracer, k), rows),
            )
            store_view(out, (tracer, k), plus, rows)
            store_view(out, (2 + tracer, k), minus, rows)
        return carry

    lax.fori_loop(0, levels, body, 0, unroll=3)


def advected_kernel(wet, upwind_ref, anti_ref, ratio_refs, out, rows=False):
    levels = out.shape[1]

    def body(k, carry):
        wet_centre = load_view(wet, (k,), rows)
        for tracer in range(2):
            anti = tuple(load_view(anti_ref, (4 * tracer + face, k), rows) for face in range(4))
            plus = sides_of(ratio_refs, tracer, k, rows)
            minus = sides_of(ratio_refs, 2 + tracer, k, rows)
            upwind = load_view(upwind_ref, (tracer, k), rows)
            store_view(out, (tracer, k), limited(plus, minus, upwind, anti, wet_centre), rows)
        return carry

    lax.fori_loop(0, levels, body, 0, unroll=3)


def isopycnal_kernel(advected_refs, state_refs, out, rows=False):
    levels = out.shape[1]

    def level(k):
        values = [sides_of(advected_refs, tracer, k, rows) for tracer in range(2)]
        return values, sides_of(state_refs, 4, k, rows)

    def body(pair, carry):
        k = 2 * pair
        lower, middle = level(k), level(k + 1)
        upper = level(jnp.minimum(k + 2, levels - 1))
        emit(k, lower, middle)
        emit(k + 1, middle, upper)
        return carry

    def emit(k, here, there):
        values, wet_sides = here
        uppers, wet_above = there
        stacked = [w * a for w, a in zip(wet_sides, wet_above)]
        verticals = [
            [(u - v) * s for u, v, s in zip(uppers[tracer], values[tracer], stacked)]
            for tracer in range(2)
        ]
        densities = [HALINE_COEF * s - THERMAL_COEF * t for t, s in zip(values[0], values[1])]
        stratas = [HALINE_COEF * s - THERMAL_COEF * t for t, s in zip(verticals[0], verticals[1])]
        for tracer in range(2):
            value, vertical = values[tracer], verticals[tracer]

            def face_flux(first, second):
                face = wet_sides[first] * wet_sides[second]
                slope = jnp.clip(
                    (densities[second] - densities[first])
                    / jnp.maximum(0.5 * (stratas[first] + stratas[second]), SLOPE_FLOOR),
                    -SLOPE_LIMIT,
                    SLOPE_LIMIT,
                )
                return (
                    DIFFUSIVITY
                    * face
                    * (
                        value[second]
                        - value[first]
                        - slope * 0.5 * (vertical[first] + vertical[second])
                    )
                )

            east_flux = face_flux(0, 1)
            west_flux = face_flux(2, 0)
            north_flux = face_flux(0, 3)
            south_flux = face_flux(4, 0)
            result = value[0] + wet_sides[0] * (east_flux - west_flux + north_flux - south_flux)
            store_view(out, (tracer, k), result, rows)

    lax.fori_loop(0, levels // 2, body, 0)


class Stack:
    def __init__(self, *refs):
        self.refs = refs
        self.shape = (len(refs),) + refs[0].shape

    def __getitem__(self, index):
        return self.refs[index[0]][index[1:]]


class Pair:
    def __init__(self, first, second):
        self.refs = (first, second)
        self.shape = (2,) + first.shape

    def __setitem__(self, index, value):
        self.refs[index[0]][index[1:]] = value


def buffers_for(fields, levels, height, width, lon):
    columns = pltpu.VMEM((fields, 16, height), jnp.float32)
    rows = pltpu.VMEM((fields * levels, width), jnp.float32)
    halo = pltpu.VMEM((fields, levels, height, width), jnp.float32)
    return [
        columns,
        columns,
        rows,
        rows,
        columns,
        columns,
        rows,
        rows,
        pltpu.VMEM((lon, fields * levels, width), jnp.float32),
        halo,
        halo,
        rows,
    ]


STAGE_FIELDS = (5, 2, 4, 2)


def fused_kernel(
    lon, lat, signs, seam, heat, salt, zonal, meridional, sea, depth, first_out, second_out, *scratch
):
    mesh = pl.DeviceIdType.MESH
    upwind, ratio, advected, anti, flow, wet = scratch[:6]
    count = len(STAGE_FIELDS)
    per_stage = [scratch[6 + 12 * s : 18 + 12 * s] for s in range(count)]
    fold_send, fold_recv, side_send, side_recv = scratch[6 + 12 * count :]
    me = lax.axis_index("lon")
    row = lax.axis_index("lat")
    west = lax.rem(me + lon - 1, lon)
    east = lax.rem(me + 1, lon)
    has_south = row > 0
    has_north = row < lat - 1
    on_top = row == lat - 1
    levels, height, width = heat.shape
    wet_column = sea[...] == 1
    for k in range(levels):
        wet[k] = jnp.where(wet_column & (k < depth[...]), 1.0, 0.0).astype(jnp.float32)
    state = Stack(heat, salt, zonal, meridional, wet)
    pivot = seam[0]
    pivot_block, pivot_offset = pivot // width, pivot % width
    lower = lax.rem(pivot_block - me - 1 + 2 * lon, lon)
    upper = lax.rem(pivot_block - me + 2 * lon, lon)
    source_lane = lax.broadcasted_iota(jnp.int32, (width, width), 0)
    target_lane = lax.broadcasted_iota(jnp.int32, (width, width), 1)
    reverse = (
        jnp.where(source_lane == width + pivot_offset - target_lane, 1.0, 0.0).astype(jnp.float32),
        jnp.where(source_lane == pivot_offset - target_lane, 1.0, 0.0).astype(jnp.float32),
    )

    barrier = pltpu.get_barrier_semaphore()
    for peer in range(lon):

        @pl.when((me != peer) & (on_top | (peer == west) | (peer == east)))
        def _():
            pl.semaphore_signal(barrier, 1, device_id={"lon": peer}, device_id_type=mesh)

    @pl.when(has_south)
    def _():
        pl.semaphore_signal(barrier, 1, device_id={"lat": row - 1}, device_id_type=mesh)

    @pl.when(has_north)
    def _():
        pl.semaphore_signal(barrier, 1, device_id={"lat": row + 1}, device_id_type=mesh)

    beside = 1 if lon == 2 else 2
    pl.semaphore_wait(
        barrier,
        jnp.where(on_top, lon - 1, beside)
        + has_south.astype(jnp.int32)
        + has_north.astype(jnp.int32),
    )

    def exchange(s, source):
        wsend, esend, ssend, nsend, whalo, ehalo, shalo, nhalo, gathered, wcol, ecol, north = (
            per_stage[s]
        )
        fields = source.shape[0]
        for f in range(fields):
            for k in range(levels):
                tile = source[f, k]
                if s == 0 and f == 3:
                    wsend[f, pl.ds(k, 1), :] = jnp.zeros((1, height), jnp.float32)
                    esend[f, pl.ds(k, 1), :] = jnp.zeros((1, height), jnp.float32)
                else:
                    flipped = tile.T
                    wsend[f, pl.ds(k, 1), :] = flipped[0:1, :]
                    esend[f, pl.ds(k, 1), :] = flipped[width - 1 : width, :]
                ssend[pl.ds(f * levels + k, 1), :] = tile[0:1, :]
                nsend[pl.ds(f * levels + k, 1), :] = tile[height - 1 : height, :]
            spare = wsend.shape[1] - levels
            wsend[f, pl.ds(levels, spare), :] = jnp.zeros((spare, height), jnp.float32)
            esend[f, pl.ds(levels, spare), :] = jnp.zeros((spare, height), jnp.float32)

        def fold_copy(peer, slot):
            return pltpu.make_async_remote_copy(
                src_ref=nsend,
                dst_ref=gathered.at[slot],
                send_sem=fold_send.at[s, peer],
                recv_sem=fold_recv.at[s, slot],
                device_id={"lon": peer},
                device_id_type=mesh,
            )

        def side(i, src, dst, device):
            return pltpu.make_async_remote_copy(
                src_ref=src,
                dst_ref=dst,
                send_sem=side_send.at[s, i],
                recv_sem=side_recv.at[s, i],
                device_id=device,
                device_id_type=mesh,
            )

        to_west = side(0, wsend, ehalo, {"lon": west})
        to_east = side(1, esend, whalo, {"lon": east})
        to_south = side(2, ssend, nhalo, {"lat": row - 1})
        to_north = side(3, nsend, shalo, {"lat": row + 1})
        to_west.start()
        to_east.start()

        @pl.when(has_south)
        def _():
            to_south.start()

        @pl.when(has_north)
        def _():
            to_north.start()

        for peer in range(lon):

            @pl.when((me != peer) & on_top)
            def _():
                fold_copy(peer, me).start()

        @pl.when(on_top)
        def _():
            gathered[me] = nsend[...]

        to_west.wait()
        to_east.wait()

        edge = lax.broadcasted_iota(jnp.int32, (height, width), 1)
        for f in range(fields):
            if s == 0 and f == 3:
                wcol[f] = jnp.zeros(wcol.shape[1:], jnp.float32)
                continue
            rows = whalo.shape[1]
            spread = jnp.concatenate(
                [whalo[f], ehalo[f], jnp.zeros((width - 2 * rows, height), jnp.float32)], axis=0
            ).T
            for k in range(levels):
                west_lane = spread if k == 0 else pltpu.roll(spread, width - k, 1)
                east_lane = pltpu.roll(spread, width - 1 - rows - k, 1)
                wcol[f, k] = jnp.where(edge == 0, west_lane, east_lane)

        def finish():
            @pl.when(has_south)
            def _():
                to_south.wait_send()
                to_north.wait_recv()

            @pl.when(has_north)
            def _():
                to_north.wait_send()
                to_south.wait_recv()

            @pl.when(jnp.logical_not(has_south))
            def _():
                shalo[...] = jnp.zeros_like(shalo)

            @pl.when(jnp.logical_not(has_north))
            def _():
                nhalo[...] = jnp.zeros_like(nhalo)

            @pl.when(jnp.logical_not(on_top))
            def _():
                north[...] = nhalo[...]

            for peer in range(lon):

                @pl.when((me != peer) & on_top)
                def _():
                    fold_copy(peer, me).wait_send()
                    fold_copy(peer, peer).wait_recv()

            @pl.when(on_top)
            def _():
                ghost = jnp.dot(
                    gathered[lower],
                    reverse[0],
                    precision=lax.Precision.HIGHEST,
                    preferred_element_type=jnp.float32,
                ) + jnp.dot(
                    gathered[upper],
                    reverse[1],
                    precision=lax.Precision.HIGHEST,
                    preferred_element_type=jnp.float32,
                )
                if s == 0:
                    line = lax.broadcasted_iota(jnp.int32, ghost.shape, 0)
                    sign = jnp.ones(ghost.shape, jnp.float32)
                    for f in range(fields):
                        owned = (line >= f * levels) & (line < (f + 1) * levels)
                        sign = jnp.where(owned, signs[f], sign)
                    ghost = ghost * sign
                north[...] = ghost

        return (source, wcol, wcol, ssend, nsend), (source, wcol, wcol, shalo, north), finish

    def run(stage, finish):
        stage(False)
        finish()
        stage(True)

    state_early, state_refs, finish = exchange(0, state)
    run(
        lambda rows: upwind_kernel(state_refs if rows else state_early, upwind, anti, flow, rows),
        finish,
    )
    upwind_early, upwind_refs, finish = exchange(1, upwind)
    run(
        lambda rows: ratio_kernel(
            state_refs, upwind_refs if rows else upwind_early, flow, ratio, rows
        ),
        finish,
    )
    ratio_early, ratio_refs, finish = exchange(2, ratio)
    run(
        lambda rows: advected_kernel(
            wet, upwind, anti, ratio_refs if rows else ratio_early, advected, rows
        ),
        finish,
    )
    advected_early, advected_refs, finish = exchange(3, advected)
    final = Pair(first_out, second_out)
    run(
        lambda rows: isopycnal_kernel(
            advected_refs if rows else advected_early, state_refs, final, rows
        ),
        finish,
    )


def fused(fields, seam):
    lon = lax.axis_size("lon")
    lat = lax.axis_size("lat")
    levels, height, width = fields[0].shape
    block = jax.ShapeDtypeStruct((levels, height, width), jnp.float32)
    scratch = [
        pltpu.VMEM((2, levels, height, width), jnp.float32),
        pltpu.VMEM((4, levels, height, width), jnp.float32),
        pltpu.VMEM((2, levels, height, width), jnp.float32),
        pltpu.VMEM((8, levels, height, width), jnp.float32),
        pltpu.VMEM((4, levels, height, width), jnp.float32),
        pltpu.VMEM((levels, height, width), jnp.float32),
    ]
    for count in STAGE_FIELDS:
        scratch += buffers_for(count, levels, height, width, lon)
    stages = len(STAGE_FIELDS)
    scratch += [
        pltpu.SemaphoreType.DMA((stages, lon)),
        pltpu.SemaphoreType.DMA((stages, lon)),
        pltpu.SemaphoreType.DMA((stages, 4)),
        pltpu.SemaphoreType.DMA((stages, 4)),
    ]
    return pl.pallas_call(
        functools.partial(fused_kernel, lon, lat, STATE_SIGNS),
        out_shape=(block, block),
        in_specs=[pl.BlockSpec(memory_space=pltpu.SMEM)]
        + [pl.BlockSpec(memory_space=pltpu.VMEM)] * len(fields),
        out_specs=[pl.BlockSpec(memory_space=pltpu.VMEM)] * 2,
        scratch_shapes=scratch,
        compiler_params=pltpu.CompilerParams(
            collective_id=0, has_side_effects=True, vmem_limit_bytes=60 * 1024 * 1024
        ),
    )(seam, *fields)


def local(
    heat_content_field,
    saltiness_field,
    eastward_cfl_number,
    northward_cfl_number,
    seawater_indicator,
    submerged_layer_total,
    seam_partner_index,
):
    return fused(
        (
            heat_content_field,
            saltiness_field,
            eastward_cfl_number,
            northward_cfl_number,
            seawater_indicator,
            submerged_layer_total,
        ),
        seam_partner_index,
    )


def solution(mesh):
    in_specs = (
        P(None, "lat", "lon"),
        P(None, "lat", "lon"),
        P(None, "lat", "lon"),
        P(None, "lat", "lon"),
        P("lat", "lon"),
        P("lat", "lon"),
        P(),
    )
    out_specs = (P(None, "lat", "lon"), P(None, "lat", "lon"))
    return jax.shard_map(local, mesh=mesh, in_specs=in_specs, out_specs=out_specs, check_vma=False)
```

```python
import functools

import jax
import jax.numpy as jnp
from jax import lax
from jax.experimental import pallas as pl
from jax.experimental.pallas import tpu as pltpu
from jax.sharding import PartitionSpec as P

RATIO_FLOOR = 0.05
SLOPE_FLOOR = 0.5
SLOPE_LIMIT = 2.0
DIFFUSIVITY = 0.1
THERMAL_COEF = 0.2
HALINE_COEF = 0.8
STATE_SIGNS = (1.0, 1.0, -1.0, -1.0, 1.0)


def sign_column(values):
    return jnp.array(values, jnp.float32).reshape(len(values), 1, 1, 1)


def around(x, west, east, south, north):
    height, width = x.shape
    lane = lax.broadcasted_iota(jnp.int32, x.shape, 1)
    level = lax.broadcasted_iota(jnp.int32, x.shape, 0)
    at_east = jnp.where(lane == width - 1, east, pltpu.roll(x, width - 1, 1))
    at_west = jnp.where(lane == 0, west, pltpu.roll(x, 1, 1))
    at_north = jnp.where(level == height - 1, north, pltpu.roll(x, height - 1, 0))
    at_south = jnp.where(level == 0, south, pltpu.roll(x, 1, 0))
    return (x, at_east, at_west, at_north, at_south)


def pick_rows(low, high):
    level = lax.broadcasted_iota(jnp.int32, (2, high.shape[-1]), 0)
    return jnp.where(level == 0, low, high)


def load_view(ref, index, rows):
    if not rows:
        return ref[index]
    height = ref.shape[-2]
    return pick_rows(
        ref[index + (pl.ds(0, 1), slice(None))], ref[index + (pl.ds(height - 1, 1), slice(None))]
    )


def store_view(ref, index, value, rows):
    if not rows:
        ref[index] = value
        return
    height = ref.shape[-2]
    ref[index + (pl.ds(0, 1), slice(None))] = value[0:1]
    ref[index + (pl.ds(height - 1, 1), slice(None))] = value[1:2]


def sides_of(refs, f, k, rows=False):
    block, west, east, south, north = refs
    line = pl.ds(f * block.shape[1] + k, 1)
    if not rows:
        return around(block[f, k], west[f, k], east[f, k], south[line, :], north[line, :])
    height = west.shape[2]
    low = block[f, k, pl.ds(0, 2), :]
    high = block[f, k, pl.ds(height - 2, 2), :]
    centre = pick_rows(low[0:1], high[1:2])
    at_north = pick_rows(low[1:2], north[line, :])
    at_south = pick_rows(south[line, :], high[0:1])
    west_end = pick_rows(west[f, k, pl.ds(0, 1), :], west[f, k, pl.ds(height - 1, 1), :])
    east_end = pick_rows(east[f, k, pl.ds(0, 1), :], east[f, k, pl.ds(height - 1, 1), :])
    width = centre.shape[1]
    lane = lax.broadcasted_iota(jnp.int32, centre.shape, 1)
    at_east = jnp.where(lane == width - 1, east_end, pltpu.roll(centre, width - 1, 1))
    at_west = jnp.where(lane == 0, west_end, pltpu.roll(centre, 1, 1))
    return (centre, at_east, at_west, at_north, at_south)


def low_order(tracer, zonal, meridional, wet_sides):
    value_centre, value_east, value_west, value_north, value_south = tracer
    speed_centre, speed_west = (zonal[0], zonal[2])
    flow_centre, flow_south = (meridional[0], meridional[4])
    wet_centre, wet_east, wet_west, wet_north, wet_south = wet_sides
    face_east = wet_centre * wet_east
    face_west = wet_west * wet_centre
    face_north = wet_centre * wet_north
    face_south = wet_south * wet_centre
    upwind_east = face_east * (
        jnp.maximum(speed_centre, 0.0) * value_centre + jnp.minimum(speed_centre, 0.0) * value_east
    )
    upwind_west = face_west * (
        jnp.maximum(speed_west, 0.0) * value_west + jnp.minimum(speed_west, 0.0) * value_centre
    )
    upwind_north = face_north * (
        jnp.maximum(flow_centre, 0.0) * value_centre + jnp.minimum(flow_centre, 0.0) * value_north
    )
    upwind_south = face_south * (
        jnp.maximum(flow_south, 0.0) * value_south + jnp.minimum(flow_south, 0.0) * value_centre
    )
    anti_east = face_east * speed_centre * (value_centre + value_east) * 0.5 - upwind_east
    anti_west = face_west * speed_west * (value_west + value_centre) * 0.5 - upwind_west
    anti_north = face_north * flow_centre * (value_centre + value_north) * 0.5 - upwind_north
    anti_south = face_south * flow_south * (value_south + value_centre) * 0.5 - upwind_south
    upwind = value_centre - wet_centre * (upwind_east - upwind_west + upwind_north - upwind_south)
    inflow = (
        jnp.maximum(anti_west, 0.0)
        - jnp.minimum(anti_east, 0.0)
        + jnp.maximum(anti_south, 0.0)
        - jnp.minimum(anti_north, 0.0)
    )
    outflow = (
        jnp.maximum(anti_east, 0.0)
        - jnp.minimum(anti_west, 0.0)
        + jnp.maximum(anti_north, 0.0)
        - jnp.minimum(anti_south, 0.0)
    )
    anti = (anti_east, anti_west, anti_north, anti_south)
    return (upwind, anti, inflow, outflow)


def level_low_order(state_refs, k, tracer):
    zonal = sides_of(state_refs, 2, k)
    meridional = sides_of(state_refs, 3, k)
    wet_sides = sides_of(state_refs, 4, k)
    return low_order(sides_of(state_refs, tracer, k), zonal, meridional, wet_sides), wet_sides


def ratio_pair(upwind_sides, wet_sides, inflow, outflow):
    value_centre = upwind_sides[0]
    candidates = [value_centre] + [
        jnp.where(beside_wet > 0.5, beside, value_centre)
        for beside, beside_wet in zip(upwind_sides[1:], wet_sides[1:])
    ]
    highest = functools.reduce(jnp.maximum, candidates)
    lowest = functools.reduce(jnp.minimum, candidates)
    ratio_plus = jnp.minimum(1.0, (highest - value_centre) / jnp.maximum(inflow, RATIO_FLOOR))
    ratio_minus = jnp.minimum(1.0, (value_centre - lowest) / jnp.maximum(outflow, RATIO_FLOOR))
    return ratio_plus, ratio_minus


def limited(plus, minus, upwind, anti, wet_centre):
    plus_centre, plus_east, plus_west, plus_north, plus_south = plus
    minus_centre, minus_east, minus_west, minus_north, minus_south = minus
    anti_east, anti_west, anti_north, anti_south = anti
    coef_east = jnp.where(
        anti_east >= 0.0, jnp.minimum(plus_east, minus_centre), jnp.minimum(plus_centre, minus_east)
    )
    coef_west = jnp.where(
        anti_west >= 0.0, jnp.minimum(plus_centre, minus_west), jnp.minimum(plus_west, minus_centre)
    )
    coef_north = jnp.where(
        anti_north >= 0.0,
        jnp.minimum(plus_north, minus_centre),
        jnp.minimum(plus_centre, minus_north),
    )
    coef_south = jnp.where(
        anti_south >= 0.0,
        jnp.minimum(plus_centre, minus_south),
        jnp.minimum(plus_south, minus_centre),
    )
    return upwind - wet_centre * (
        coef_east * anti_east
        - coef_west * anti_west
        + coef_north * anti_north
        - coef_south * anti_south
    )


def upwind_kernel(state_refs, out, anti_out, flow_out, rows=False):
    levels = out.shape[1]

    def body(k, carry):
        zonal = sides_of(state_refs, 2, k, rows)
        meridional = sides_of(state_refs, 3, k, rows)
        wet_sides = sides_of(state_refs, 4, k, rows)
        for tracer in range(2):
            tracer_sides = sides_of(state_refs, tracer, k, rows)
            upwind, anti, inflow, outflow = low_order(tracer_sides, zonal, meridional, wet_sides)
            store_view(out, (tracer, k), upwind, rows)
            for face in range(4):
                store_view(anti_out, (4 * tracer + face, k), anti[face], rows)
            store_view(flow_out, (tracer, k), inflow, rows)
            store_view(flow_out, (2 + tracer, k), outflow, rows)
        return carry

    lax.fori_loop(0, levels, body, 0, unroll=4)


def ratio_kernel(state_refs, upwind_refs, flow, out, rows=False):
    levels = out.shape[1]

    def body(k, carry):
        wet_sides = sides_of(state_refs, 4, k, rows)
        for tracer in range(2):
            plus, minus = ratio_pair(
                sides_of(upwind_refs, tracer, k, rows),
                wet_sides,
                load_view(flow, (tracer, k), rows),
                load_view(flow, (2 + tracer, k), rows),
            )
            store_view(out, (tracer, k), plus, rows)
            store_view(out, (2 + tracer, k), minus, rows)
        return carry

    lax.fori_loop(0, levels, body, 0, unroll=4)


def advected_kernel(wet, upwind_ref, anti_ref, ratio_refs, out, rows=False):
    levels = out.shape[1]

    def body(k, carry):
        wet_centre = load_view(wet, (k,), rows)
        for tracer in range(2):
            anti = tuple(load_view(anti_ref, (4 * tracer + face, k), rows) for face in range(4))
            plus = sides_of(ratio_refs, tracer, k, rows)
            minus = sides_of(ratio_refs, 2 + tracer, k, rows)
            upwind = load_view(upwind_ref, (tracer, k), rows)
            store_view(out, (tracer, k), limited(plus, minus, upwind, anti, wet_centre), rows)
        return carry

    lax.fori_loop(0, levels, body, 0, unroll=4)


def isopycnal_kernel(advected_refs, state_refs, out, rows=False):
    levels = out.shape[1]

    def level(k):
        values = [sides_of(advected_refs, tracer, k, rows) for tracer in range(2)]
        return values, sides_of(state_refs, 4, k, rows)

    def body(pair, carry):
        k = 2 * pair
        lower, middle = level(k), level(k + 1)
        upper = level(jnp.minimum(k + 2, levels - 1))
        emit(k, lower, middle)
        emit(k + 1, middle, upper)
        return carry

    def emit(k, here, there):
        values, wet_sides = here
        uppers, wet_above = there
        stacked = [w * a for w, a in zip(wet_sides, wet_above)]
        verticals = [
            [(u - v) * s for u, v, s in zip(uppers[tracer], values[tracer], stacked)]
            for tracer in range(2)
        ]
        densities = [HALINE_COEF * s - THERMAL_COEF * t for t, s in zip(values[0], values[1])]
        stratas = [HALINE_COEF * s - THERMAL_COEF * t for t, s in zip(verticals[0], verticals[1])]
        for tracer in range(2):
            value, vertical = values[tracer], verticals[tracer]

            def face_flux(first, second):
                face = wet_sides[first] * wet_sides[second]
                slope = jnp.clip(
                    (densities[second] - densities[first])
                    / jnp.maximum(0.5 * (stratas[first] + stratas[second]), SLOPE_FLOOR),
                    -SLOPE_LIMIT,
                    SLOPE_LIMIT,
                )
                return (
                    DIFFUSIVITY
                    * face
                    * (
                        value[second]
                        - value[first]
                        - slope * 0.5 * (vertical[first] + vertical[second])
                    )
                )

            east_flux = face_flux(0, 1)
            west_flux = face_flux(2, 0)
            north_flux = face_flux(0, 3)
            south_flux = face_flux(4, 0)
            result = value[0] + wet_sides[0] * (east_flux - west_flux + north_flux - south_flux)
            store_view(out, (tracer, k), result, rows)

    lax.fori_loop(0, levels // 2, body, 0)


class Stack:
    def __init__(self, *refs):
        self.refs = refs
        self.shape = (len(refs),) + refs[0].shape

    def __getitem__(self, index):
        return self.refs[index[0]][index[1:]]


class Pair:
    def __init__(self, first, second):
        self.refs = (first, second)
        self.shape = (2,) + first.shape

    def __setitem__(self, index, value):
        self.refs[index[0]][index[1:]] = value


def buffers_for(fields, levels, height, width, lon):
    columns = pltpu.VMEM((fields, 16, height), jnp.float32)
    rows = pltpu.VMEM((fields * levels, width), jnp.float32)
    halo = pltpu.VMEM((fields, levels, height, width), jnp.float32)
    return [
        columns,
        columns,
        rows,
        rows,
        columns,
        columns,
        rows,
        rows,
        pltpu.VMEM((lon, fields * levels, width), jnp.float32),
        halo,
        halo,
        rows,
    ]


STAGE_FIELDS = (5, 2, 4, 2)


def fused_kernel(
    lon, lat, signs, seam, heat, salt, zonal, meridional, sea, depth, first_out, second_out, *scratch
):
    mesh = pl.DeviceIdType.MESH
    upwind, ratio, advected, anti, flow, wet = scratch[:6]
    count = len(STAGE_FIELDS)
    per_stage = [scratch[6 + 12 * s : 18 + 12 * s] for s in range(count)]
    fold_send, fold_recv, side_send, side_recv = scratch[6 + 12 * count :]
    me = lax.axis_index("lon")
    row = lax.axis_index("lat")
    west = lax.rem(me + lon - 1, lon)
    east = lax.rem(me + 1, lon)
    has_south = row > 0
    has_north = row < lat - 1
    on_top = row == lat - 1
    levels, height, width = heat.shape
    wet_column = sea[...] == 1
    for k in range(levels):
        wet[k] = jnp.where(wet_column & (k < depth[...]), 1.0, 0.0).astype(jnp.float32)
    state = Stack(heat, salt, zonal, meridional, wet)
    pivot = seam[0]
    pivot_block, pivot_offset = pivot // width, pivot % width
    lower = lax.rem(pivot_block - me - 1 + 2 * lon, lon)
    upper = lax.rem(pivot_block - me + 2 * lon, lon)
    source_lane = lax.broadcasted_iota(jnp.int32, (width, width), 0)
    target_lane = lax.broadcasted_iota(jnp.int32, (width, width), 1)
    reverse = (
        jnp.where(source_lane == width + pivot_offset - target_lane, 1.0, 0.0).astype(jnp.float32),
        jnp.where(source_lane == pivot_offset - target_lane, 1.0, 0.0).astype(jnp.float32),
    )

    barrier = pltpu.get_barrier_semaphore()
    for peer in range(lon):

        @pl.when((me != peer) & (on_top | (peer == west) | (peer == east)))
        def _():
            pl.semaphore_signal(barrier, 1, device_id={"lon": peer}, device_id_type=mesh)

    @pl.when(has_south)
    def _():
        pl.semaphore_signal(barrier, 1, device_id={"lat": row - 1}, device_id_type=mesh)

    @pl.when(has_north)
    def _():
        pl.semaphore_signal(barrier, 1, device_id={"lat": row + 1}, device_id_type=mesh)

    beside = 1 if lon == 2 else 2
    pl.semaphore_wait(
        barrier,
        jnp.where(on_top, lon - 1, beside)
        + has_south.astype(jnp.int32)
        + has_north.astype(jnp.int32),
    )

    def exchange(s, source):
        wsend, esend, ssend, nsend, whalo, ehalo, shalo, nhalo, gathered, wcol, ecol, north = (
            per_stage[s]
        )
        fields = source.shape[0]
        for f in range(fields):
            for k in range(levels):
                tile = source[f, k]
                if s == 0 and f == 3:
                    wsend[f, pl.ds(k, 1), :] = jnp.zeros((1, height), jnp.float32)
                    esend[f, pl.ds(k, 1), :] = jnp.zeros((1, height), jnp.float32)
                else:
                    flipped = tile.T
                    wsend[f, pl.ds(k, 1), :] = flipped[0:1, :]
                    esend[f, pl.ds(k, 1), :] = flipped[width - 1 : width, :]
                ssend[pl.ds(f * levels + k, 1), :] = tile[0:1, :]
                nsend[pl.ds(f * levels + k, 1), :] = tile[height - 1 : height, :]
            spare = wsend.shape[1] - levels
            wsend[f, pl.ds(levels, spare), :] = jnp.zeros((spare, height), jnp.float32)
            esend[f, pl.ds(levels, spare), :] = jnp.zeros((spare, height), jnp.float32)

        def fold_copy(peer, slot):
            return pltpu.make_async_remote_copy(
                src_ref=nsend,
                dst_ref=gathered.at[slot],
                send_sem=fold_send.at[s, peer],
                recv_sem=fold_recv.at[s, slot],
                device_id={"lon": peer},
                device_id_type=mesh,
            )

        def side(i, src, dst, device):
            return pltpu.make_async_remote_copy(
                src_ref=src,
                dst_ref=dst,
                send_sem=side_send.at[s, i],
                recv_sem=side_recv.at[s, i],
                device_id=device,
                device_id_type=mesh,
            )

        to_west = side(0, wsend, ehalo, {"lon": west})
        to_east = side(1, esend, whalo, {"lon": east})
        to_south = side(2, ssend, nhalo, {"lat": row - 1})
        to_north = side(3, nsend, shalo, {"lat": row + 1})
        to_west.start()
        to_east.start()

        @pl.when(has_south)
        def _():
            to_south.start()

        @pl.when(has_north)
        def _():
            to_north.start()

        for peer in range(lon):

            @pl.when((me != peer) & on_top)
            def _():
                fold_copy(peer, me).start()

        @pl.when(on_top)
        def _():
            gathered[me] = nsend[...]

        to_west.wait()
        to_east.wait()

        edge = lax.broadcasted_iota(jnp.int32, (height, width), 1)
        for f in range(fields):
            if s == 0 and f == 3:
                wcol[f] = jnp.zeros(wcol.shape[1:], jnp.float32)
                continue
            rows = whalo.shape[1]
            spread = jnp.concatenate(
                [whalo[f], ehalo[f], jnp.zeros((width - 2 * rows, height), jnp.float32)], axis=0
            ).T
            for k in range(levels):
                west_lane = spread if k == 0 else pltpu.roll(spread, width - k, 1)
                east_lane = pltpu.roll(spread, width - 1 - rows - k, 1)
                wcol[f, k] = jnp.where(edge == 0, west_lane, east_lane)

        def finish():
            @pl.when(has_south)
            def _():
                to_south.wait_send()
                to_north.wait_recv()

            @pl.when(has_north)
            def _():
                to_north.wait_send()
                to_south.wait_recv()

            @pl.when(jnp.logical_not(has_south))
            def _():
                shalo[...] = jnp.zeros_like(shalo)

            @pl.when(jnp.logical_not(has_north))
            def _():
                nhalo[...] = jnp.zeros_like(nhalo)

            @pl.when(jnp.logical_not(on_top))
            def _():
                north[...] = nhalo[...]

            for peer in range(lon):

                @pl.when((me != peer) & on_top)
                def _():
                    fold_copy(peer, me).wait_send()
                    fold_copy(peer, peer).wait_recv()

            @pl.when(on_top)
            def _():
                ghost = jnp.dot(
                    gathered[lower],
                    reverse[0],
                    precision=lax.Precision.HIGHEST,
                    preferred_element_type=jnp.float32,
                ) + jnp.dot(
                    gathered[upper],
                    reverse[1],
                    precision=lax.Precision.HIGHEST,
                    preferred_element_type=jnp.float32,
                )
                if s == 0:
                    line = lax.broadcasted_iota(jnp.int32, ghost.shape, 0)
                    sign = jnp.ones(ghost.shape, jnp.float32)
                    for f in range(fields):
                        owned = (line >= f * levels) & (line < (f + 1) * levels)
                        sign = jnp.where(owned, signs[f], sign)
                    ghost = ghost * sign
                north[...] = ghost

        return (source, wcol, wcol, ssend, nsend), (source, wcol, wcol, shalo, north), finish

    def run(stage, finish):
        stage(False)
        finish()
        stage(True)

    state_early, state_refs, finish = exchange(0, state)
    run(
        lambda rows: upwind_kernel(state_refs if rows else state_early, upwind, anti, flow, rows),
        finish,
    )
    upwind_early, upwind_refs, finish = exchange(1, upwind)
    run(
        lambda rows: ratio_kernel(
            state_refs, upwind_refs if rows else upwind_early, flow, ratio, rows
        ),
        finish,
    )
    ratio_early, ratio_refs, finish = exchange(2, ratio)
    run(
        lambda rows: advected_kernel(
            wet, upwind, anti, ratio_refs if rows else ratio_early, advected, rows
        ),
        finish,
    )
    advected_early, advected_refs, finish = exchange(3, advected)
    final = Pair(first_out, second_out)
    run(
        lambda rows: isopycnal_kernel(
            advected_refs if rows else advected_early, state_refs, final, rows
        ),
        finish,
    )


def fused(fields, seam):
    lon = lax.axis_size("lon")
    lat = lax.axis_size("lat")
    levels, height, width = fields[0].shape
    block = jax.ShapeDtypeStruct((levels, height, width), jnp.float32)
    scratch = [
        pltpu.VMEM((2, levels, height, width), jnp.float32),
        pltpu.VMEM((4, levels, height, width), jnp.float32),
        pltpu.VMEM((2, levels, height, width), jnp.float32),
        pltpu.VMEM((8, levels, height, width), jnp.float32),
        pltpu.VMEM((4, levels, height, width), jnp.float32),
        pltpu.VMEM((levels, height, width), jnp.float32),
    ]
    for count in STAGE_FIELDS:
        scratch += buffers_for(count, levels, height, width, lon)
    stages = len(STAGE_FIELDS)
    scratch += [
        pltpu.SemaphoreType.DMA((stages, lon)),
        pltpu.SemaphoreType.DMA((stages, lon)),
        pltpu.SemaphoreType.DMA((stages, 4)),
        pltpu.SemaphoreType.DMA((stages, 4)),
    ]
    return pl.pallas_call(
        functools.partial(fused_kernel, lon, lat, STATE_SIGNS),
        out_shape=(block, block),
        in_specs=[pl.BlockSpec(memory_space=pltpu.SMEM)]
        + [pl.BlockSpec(memory_space=pltpu.VMEM)] * len(fields),
        out_specs=[pl.BlockSpec(memory_space=pltpu.VMEM)] * 2,
        scratch_shapes=scratch,
        compiler_params=pltpu.CompilerParams(
            collective_id=0, has_side_effects=True, vmem_limit_bytes=60 * 1024 * 1024
        ),
    )(seam, *fields)


def local(
    heat_content_field,
    saltiness_field,
    eastward_cfl_number,
    northward_cfl_number,
    seawater_indicator,
    submerged_layer_total,
    seam_partner_index,
):
    return fused(
        (
            heat_content_field,
            saltiness_field,
            eastward_cfl_number,
            northward_cfl_number,
            seawater_indicator,
            submerged_layer_total,
        ),
        seam_partner_index,
    )


def solution(mesh):
    in_specs = (
        P(None, "lat", "lon"),
        P(None, "lat", "lon"),
        P(None, "lat", "lon"),
        P(None, "lat", "lon"),
        P("lat", "lon"),
        P("lat", "lon"),
        P(),
    )
    out_specs = (P(None, "lat", "lon"), P(None, "lat", "lon"))
    return jax.shard_map(local, mesh=mesh, in_specs=in_specs, out_specs=out_specs, check_vma=False)
```
